32 devices in a mesh: section: 4 (over y, core), tp: 8 (over z, x).
Axes of the slice: x: 2, y: 2, z: 4, core: 2. Of those that a mesh axis runs over, the one named last changes fastest.
Arguments:
- section_inputs: bfloat16 [4, 2, 64, 8192], P('section', None, 'tp'), may hold values from -6 to 6
- norm_gain: bfloat16 [4, 8192], P('section'), may hold values from 0.5 to 1.5
- w_query: bfloat16 [4, 8192, 4096], P('section', None, 'tp'), may hold values from -0.0625 to 0.0625
- key_projection: bfloat16 [4, 8192, 512], P('section', 'tp'), may hold values from -0.0625 to 0.0625
- value_projection: bfloat16 [4, 8192, 512], P('section', 'tp'), may hold values from -0.0625 to 0.0625
- w_out: bfloat16 [4, 4096, 8192], P('section', 'tp'), may hold values from -0.09375 to 0.09375
- token_dir: bfloat16 [2, 64, 8192], P(None, 'tp'), may hold values from -6 to 6
- tok_logratio: float32 [2, 64], P(None, 'tp'), may hold values from -4 to 4
- segment_ids: int32 [2, 64], replicated, may hold values from 0 to 7, as said below
- pair_of_slot: int32 [2, 4], replicated, may hold values from 0 to 7, as said below
- pair_counts: int32 [8, 2], replicated, may hold values from 1 to 24, as said below
Outputs:
- input_grads: bfloat16 [4, 2, 64, 8192], P('section', None, 'tp')
- grad_w_query: bfloat16 [4, 8192, 4096], P('section', None, 'tp')
- grad_w_key: bfloat16 [4, 8192, 512], P('section', 'tp')
- grad_w_value: bfloat16 [4, 8192, 512], P('section', 'tp')
- grad_w_out: bfloat16 [4, 4096, 8192], P('section', 'tp')
- grad_norm_gain: float32 [4, 8192], P('section')
The draws below stay inside these ranges and needn't reach their ends.
Inputs may be any that keep to these rules, and one draw needn't show every extreme that they name: `segment_ids`: in each micro-batch the segment ids do not fall along the tokens and take every value of 0 to 7; segment 2 j is the chosen and 2 j + 1 the rejected sequence of slot j; each sequence has 1 to 24 tokens and one of each micro-batch has exactly 24. `pair_of_slot`: every pair stands in exactly one slot. pair_counts[p] holds the token counts of the chosen and the rejected sequence of pair p as they stand in segment_ids.
All inputs are finite; a program needn't handle non-finite values.
Results may differ from the reference program's by a relative error of at most 0.038.
Values may be sent and summed in bfloat16 or wider, within the bound.
A program may use at most 192 MiB of HBM per device.

```python
import math
import jax
import jax.numpy as jnp
from jax import lax

MODEL_WIDTH = 8192
HEAD_WIDTH = 128
QUERY_HEAD_COUNT = 32
KEY_VALUE_HEADS = 4
MICRO = 2
SLOTS = 4
TOK_MB = 64
RELAY_SECTIONS = 4
PAIRS = 8
LONGEST = 24
N_TP = 8


def pack_layout(key):
    length_rows = []
    for batch in range(MICRO):
        branch_key = jax.random.fold_in(key, 101 + batch)
        unit_key, place_key = jax.random.split(branch_key)
        others = 2 * SLOTS - 1
        spare = LONGEST - 1
        handed = TOK_MB - LONGEST - others
        chosen_units = jax.random.permutation(unit_key, others * spare)[:handed]
        owners = chosen_units // spare
        counts = jnp.sum((owners[:, None] == jnp.arange(others, dtype=jnp.int32)[None, :]).astype(jnp.int32), 0)
        shorter = 1 + counts
        slot_place = jax.random.randint(place_key, (), 0, 2 * SLOTS)
        position = jnp.arange(2 * SLOTS, dtype=jnp.int32)
        before = jnp.take(shorter, jnp.clip(position, 0, others - 1))
        after = jnp.take(shorter, jnp.clip(position - 1, 0, others - 1))
        length_rows.append(jnp.where(position < slot_place, before, jnp.where(position == slot_place, LONGEST, after)))
    lengths = jnp.stack(length_rows).astype(jnp.int32)
    ordering = jax.random.permutation(jax.random.fold_in(key, 7), PAIRS).astype(jnp.int32)
    return (lengths, ordering)


def draw_segment_ids(key, part):
    lengths, ordering = pack_layout(key)
    ends = jnp.cumsum(lengths, 1)
    position = jnp.arange(TOK_MB, dtype=jnp.int32)
    return jnp.sum((position[None, :, None] >= ends[:, None, :-1]).astype(jnp.int32), -1).astype(jnp.int32)


def draw_pair_of_slot(key, part):
    lengths, ordering = pack_layout(key)
    return ordering.reshape(MICRO, SLOTS)


def draw_pair_counts(key, part):
    lengths, ordering = pack_layout(key)
    return jnp.zeros((PAIRS, 2), jnp.int32).at[ordering].set(lengths.reshape(PAIRS, 2))


def level_of(own_key, dims, cuts, low, largest):
    level, own = 1.0, jax.random.fold_in(own_key, 6)
    for axis_at, blocks in cuts:
        heights = jnp.exp(jax.random.uniform(jax.random.fold_in(own, axis_at), (blocks,), jnp.float32, low / len(cuts), largest / len(cuts)))
        level = level * jnp.repeat(heights, dims[axis_at] // blocks).reshape([-1 if axis == axis_at else 1 for axis in range(len(dims))])
    return level


def normal_values(rng, shape, deviation, reach, pieces=(), kind=jnp.bfloat16):
    drawn = deviation * jax.random.normal(rng, shape, jnp.float32)
    if pieces:
        drawn = drawn * level_of(rng, shape, pieces, -0.22, 0.18)
    return jnp.clip(drawn, -reach, reach).astype(kind)


def setup_inputs(seed: int = 0) -> dict:
    key_list = jax.random.split(jax.random.key(seed), 12)
    section_inputs = normal_values(key_list[0], (RELAY_SECTIONS, MICRO, TOK_MB, MODEL_WIDTH), 1.0, 6.0, ((0, 4), (2, 8)))
    norm_gain = jnp.clip(1.0 + 0.1 * jax.random.normal(key_list[1], (RELAY_SECTIONS, MODEL_WIDTH), jnp.float32), 0.5, 1.5).astype(jnp.bfloat16)
    w_query = normal_values(key_list[2], (RELAY_SECTIONS, MODEL_WIDTH, QUERY_HEAD_COUNT * HEAD_WIDTH), MODEL_WIDTH ** -0.5, 0.0625, ((0, 4), (2, 8)))
    key_projection = normal_values(key_list[3], (RELAY_SECTIONS, MODEL_WIDTH, KEY_VALUE_HEADS * HEAD_WIDTH), MODEL_WIDTH ** -0.5, 0.0625, ((0, 4), (1, 8)))
    value_projection = normal_values(key_list[4], (RELAY_SECTIONS, MODEL_WIDTH, KEY_VALUE_HEADS * HEAD_WIDTH), MODEL_WIDTH ** -0.5, 0.0625, ((0, 4), (1, 8)))
    w_out = normal_values(key_list[5], (RELAY_SECTIONS, QUERY_HEAD_COUNT * HEAD_WIDTH, MODEL_WIDTH), (QUERY_HEAD_COUNT * HEAD_WIDTH) ** -0.5, 0.09375, ((0, 4), (1, 8)))
    token_dir = normal_values(key_list[6], (MICRO, TOK_MB, MODEL_WIDTH), 1.0, 6.0, ((1, 8),))
    tok_logratio = normal_values(key_list[7], (MICRO, TOK_MB), 0.5, 4.0, ((1, 8),), jnp.float32)
    segment_ids = draw_segment_ids(jax.random.fold_in(key_list[11], 71), 0)
    pair_of_slot = draw_pair_of_slot(jax.random.fold_in(key_list[11], 71), 0)
    pair_counts = draw_pair_counts(jax.random.fold_in(key_list[11], 71), 0)
    return dict(section_inputs=section_inputs, norm_gain=norm_gain, w_query=w_query, key_projection=key_projection, value_projection=value_projection, w_out=w_out, token_dir=token_dir, tok_logratio=tok_logratio, segment_ids=segment_ids, pair_of_slot=pair_of_slot, pair_counts=pair_counts)


norm_epsilon = 1e-05
pair_beta = 4.0
masked_score = -1e+30

def rounded_down(array):
    return lax.optimization_barrier(array.astype(jnp.bfloat16)).astype(jnp.float32)

def pair_weights(seq_sums, pair_of_slot, pair_counts):
    table = (pair_of_slot[:, :, None] == jnp.arange(pair_counts.shape[0], dtype=jnp.int32)[None, None, :]).astype(jnp.float32)
    counts = jnp.einsum('msp,pc->msc', table, pair_counts.astype(jnp.float32))
    margin = pair_beta * (seq_sums[:, 0::2] / counts[:, :, 0] - seq_sums[:, 1::2] / counts[:, :, 1])
    weight = pair_beta * jax.nn.sigmoid(-margin)
    stacked = jnp.stack([-weight / counts[:, :, 0], weight / counts[:, :, 1]], -1)
    return stacked.reshape(seq_sums.shape)

def layer_backward(saved, gain_row, query_weight, key_weight, value_weight, out_weight, upstream, allowed):
    query_group = QUERY_HEAD_COUNT // KEY_VALUE_HEADS
    scale = 1.0 / math.sqrt(HEAD_WIDTH)
    batch_groups = saved.shape[0]
    token_total = saved.shape[1]
    inputs = saved.astype(jnp.float32)
    inverse_rms = lax.rsqrt(lax.optimization_barrier(jnp.mean(inputs * inputs, -1, keepdims=True)) + norm_epsilon)
    unit_rows = inputs * inverse_rms
    gain_values = gain_row.astype(jnp.float32)
    normed_wide = rounded_down(unit_rows * gain_values)
    queries = rounded_down(jnp.einsum('mtd,dc->mtc', normed_wide, query_weight.astype(jnp.float32)))
    key_tensor = rounded_down(jnp.einsum('mtd,dc->mtc', normed_wide, key_weight.astype(jnp.float32)))
    value_tensor = rounded_down(jnp.einsum('mtd,dc->mtc', normed_wide, value_weight.astype(jnp.float32)))
    query_heads = queries.reshape(batch_groups, token_total, QUERY_HEAD_COUNT, HEAD_WIDTH)
    heads_of_key = jnp.repeat(key_tensor.reshape(batch_groups, token_total, KEY_VALUE_HEADS, HEAD_WIDTH), query_group, axis=2)
    heads_of_value = jnp.repeat(value_tensor.reshape(batch_groups, token_total, KEY_VALUE_HEADS, HEAD_WIDTH), query_group, axis=2)
    scores = jnp.einsum('mthc,muhc->mhtu', query_heads, heads_of_key) * scale
    scores = jnp.where(allowed[:, None], scores, masked_score)
    softmax_rows = jnp.exp(scores)
    softmax_rows = softmax_rows / lax.optimization_barrier(jnp.sum(softmax_rows, -1, keepdims=True))
    soft_low = rounded_down(softmax_rows)
    attended = rounded_down(jnp.einsum('mhtu,muhc->mthc', soft_low, heads_of_value)).reshape(batch_groups, token_total, QUERY_HEAD_COUNT * HEAD_WIDTH)
    upstream_wide = upstream.astype(jnp.float32)
    grad_attended = rounded_down(jnp.einsum('mtd,cd->mtc', upstream_wide, out_weight.astype(jnp.float32)))
    grad_heads = grad_attended.reshape(batch_groups, token_total, QUERY_HEAD_COUNT, HEAD_WIDTH)
    grad_probs = jnp.einsum('mthc,muhc->mhtu', grad_heads, heads_of_value)
    grad_scores = softmax_rows * (grad_probs - lax.optimization_barrier(jnp.sum(softmax_rows * grad_probs, -1, keepdims=True)))
    scores_low = rounded_down(grad_scores * scale)
    grad_queries = rounded_down(jnp.einsum('mhtu,muhc->mthc', scores_low, heads_of_key)).reshape(batch_groups, token_total, QUERY_HEAD_COUNT * HEAD_WIDTH)
    key_summands = jnp.einsum('mhtu,mthc->muhc', scores_low, query_heads)
    key_gradient = rounded_down(key_summands.reshape(batch_groups, token_total, KEY_VALUE_HEADS, query_group, HEAD_WIDTH).sum(3).reshape(batch_groups, token_total, KEY_VALUE_HEADS * HEAD_WIDTH))
    value_summands = jnp.einsum('mhtu,mthc->muhc', soft_low, grad_heads)
    value_gradient = rounded_down(value_summands.reshape(batch_groups, token_total, KEY_VALUE_HEADS, query_group, HEAD_WIDTH).sum(3).reshape(batch_groups, token_total, KEY_VALUE_HEADS * HEAD_WIDTH))
    per_device = QUERY_HEAD_COUNT * HEAD_WIDTH // N_TP
    query_parts = grad_queries.reshape(batch_groups, token_total, N_TP, per_device).transpose(2, 0, 1, 3)
    weight_parts = query_weight.astype(jnp.float32).reshape(MODEL_WIDTH, N_TP, per_device).transpose(1, 0, 2)

    def add_part(total, members):
        part, weight_part = members
        return (total + rounded_down(jnp.einsum('mtc,dc->mtd', part, weight_part)), None)
    grad_normed, unused = lax.scan(add_part, jnp.zeros((batch_groups, token_total, MODEL_WIDTH), jnp.float32), (query_parts, weight_parts))
    key_path = jnp.einsum('mtk,dk->mtd', key_gradient, key_weight.astype(jnp.float32)) + jnp.einsum('mtk,dk->mtd', value_gradient, value_weight.astype(jnp.float32))
    grad_normed = grad_normed + rounded_down(key_path)
    grad_unit = grad_normed * gain_values
    grad_input = (upstream_wide + inverse_rms * (grad_unit - unit_rows * lax.optimization_barrier(jnp.mean(grad_unit * unit_rows, -1, keepdims=True)))).astype(jnp.bfloat16)
    grad_query_w = jnp.einsum('mtd,mtc->dc', normed_wide, grad_queries).astype(jnp.bfloat16)
    grad_key_w = jnp.einsum('mtd,mtc->dc', normed_wide, key_gradient).astype(jnp.bfloat16)
    grad_value_w = jnp.einsum('mtd,mtc->dc', normed_wide, value_gradient).astype(jnp.bfloat16)
    grad_out_w = jnp.einsum('mtc,mtd->cd', attended, upstream_wide).astype(jnp.bfloat16)
    grad_gain = lax.optimization_barrier(jnp.sum(grad_normed * unit_rows, (0, 1)))
    return (grad_input, grad_query_w, grad_key_w, grad_value_w, grad_out_w, grad_gain)

def reference(section_inputs, norm_gain, w_query, key_projection, value_projection, w_out, token_dir, tok_logratio, segment_ids, pair_of_slot, pair_counts):
    seq_count = 2 * SLOTS
    member = (segment_ids[:, :, None] == jnp.arange(seq_count, dtype=jnp.int32)[None, None, :]).astype(jnp.float32)
    seq_sums = jnp.einsum('mt,mts->ms', tok_logratio.astype(jnp.float32), member)
    weights = pair_weights(seq_sums, pair_of_slot, pair_counts)
    token_weight = jnp.einsum('mts,ms->mt', member, weights)
    upstream = (token_weight[:, :, None] * token_dir.astype(jnp.float32)).astype(jnp.bfloat16)
    position = jnp.arange(TOK_MB, dtype=jnp.int32)
    allowed = (segment_ids[:, :, None] == segment_ids[:, None, :]) & (position[:, None] >= position[None, :])[None]
    results = [None] * RELAY_SECTIONS
    for section in reversed(range(RELAY_SECTIONS)):
        results[section] = layer_backward(section_inputs[section], norm_gain[section], w_query[section], key_projection[section], value_projection[section], w_out[section], upstream, allowed)
        upstream = results[section][0]
    gathered = [jnp.stack([entry[number] for entry in results]) for number in range(6)]
    return (gathered[0], gathered[1], gathered[2], gathered[3], gathered[4], gathered[5])
```

```python
import functools
import math

import jax
import jax.numpy as jnp
from jax import lax
from jax.experimental import pallas as pl
from jax.experimental.pallas import tpu as pltpu
from jax.sharding import PartitionSpec as P

HEAD_WIDTH = 128
SLOTS = 4
LANES = 128

norm_epsilon = 1e-05
pair_beta = 4.0
masked_score = -1e30

MESH = pl.DeviceIdType.MESH
VMEM_LIMIT = 56 * 1024 * 1024
low, wide = jnp.bfloat16, jnp.float32


def contract(left, right, left_dim, right_dim):
    return lax.dot_general(
        left, right, (((left_dim,), (right_dim,)), ((), ())), preferred_element_type=wide
    )


def inner_size(tp_count):
    inner = 1
    while 2 * (2 * inner) ** 2 <= tp_count:
        inner *= 2
    return inner


def relay_kernel(
    section_count,
    tp_count,
    saved_ref,
    gain_ref,
    wq_hbm,
    kw_hbm,
    vw_hbm,
    wo_hbm,
    dir_ref,
    sums_ref,
    counts_ref,
    member_ref,
    allowed_ref,
    gin_ref,
    up_ref,
    normed_ref,
    att_ref,
    gq_ref,
    dkv_ref,
    gain_out_ref,
    wq,
    kw,
    vw,
    wo,
    nall,
    gall,
    part,
    near_recv,
    far_send,
    far_recv,
    unit,
    inverse,
    grad_unit,
    queries,
    kv,
    kv_part,
    kv_far,
    kv_near,
    probs,
    grad_heads,
    key_add,
    dkv_near,
    dkv_far,
    sums_all,
    gain_all,
    w_sem,
    s_send,
    s_recv,
    nf_send,
    nf_recv,
    nn_send,
    nn_recv,
    gf_send,
    gf_recv,
    gn_send,
    gn_recv,
    hop_send,
    kf_send,
    kf_recv,
    kn_send,
    kn_recv,
    dn_send,
    dn_recv,
    df_send,
    df_recv,
    pn_send,
    pn_recv,
    pf_send,
    pf_recv,
    t_send,
    t_recv,
):
    sec = lax.axis_index("section")
    me = lax.axis_index("tp")
    inner = inner_size(tp_count)
    outer = tp_count // inner
    z, x = me // inner, lax.rem(me, inner)
    batch_groups, rows, width = saved_ref.shape
    tokens = rows * tp_count
    every = batch_groups * tokens
    head_cols = wq.shape[1]
    local_heads = head_cols // HEAD_WIDTH
    slice_width, key_width = kw.shape
    key_count = key_width // HEAD_WIDTH
    sharers = tp_count // key_count
    group_width = inner * slice_width
    step_width = min(1024, group_width)
    scale = 1.0 / math.sqrt(HEAD_WIDTH)
    is_last = sec == section_count - 1
    feeds = sec > 0

    def zpeer(zd):
        return lax.rem(z + zd, outer)

    def xpeer(xd):
        return lax.rem(x + xd, inner)

    def remote(source, target, send, receive, section, index):
        return pltpu.make_async_remote_copy(
            src_ref=source,
            dst_ref=target,
            send_sem=send,
            recv_sem=receive,
            device_id=(section, index),
            device_id_type=MESH,
        )

    def far(source, target, send, receive, zd):
        return remote(source, target, send, receive, sec, zpeer(zd) * inner + x)

    def near(source, target, send, receive, xd):
        return remote(source, target, send, receive, sec, z * inner + xpeer(xd))

    def columns(start, size):
        return pl.ds(pl.multiple_of(start, HEAD_WIDTH), size)

    loads = [
        pltpu.make_async_copy(source, target, w_sem.at[i])
        for i, (source, target) in enumerate(
            ((kw_hbm, kw), (vw_hbm, vw), (wq_hbm, wq), (wo_hbm, wo))
        )
    ]
    for load in loads:
        load.start()

    barrier = pltpu.get_barrier_semaphore()
    for d in range(1, tp_count):
        pl.semaphore_signal(
            barrier, inc=1, device_id=(sec, lax.rem(me + d, tp_count)), device_id_type=MESH
        )

    @pl.when(sec < section_count - 1)
    def _():
        for zd in range(outer):
            pl.semaphore_signal(
                barrier, inc=1, device_id=(sec + 1, zpeer(zd) * inner + x), device_id_type=MESH
            )

    gain_row = gain_ref[...].astype(wide)
    for m in range(batch_groups):
        rows_in = saved_ref[m].astype(wide)
        inv = lax.rsqrt(jnp.mean(rows_in * rows_in, -1, keepdims=True) + norm_epsilon)
        inverse[m] = jnp.broadcast_to(inv, (rows, LANES))
        unit_rows = rows_in * inv
        unit[m] = unit_rows
        nall[me, m] = (unit_rows * gain_row).astype(low)

    @pl.when(feeds)
    def _():
        pl.semaphore_wait(barrier, tp_count - 1 + outer)

    @pl.when(jnp.logical_not(feeds))
    def _():
        pl.semaphore_wait(barrier, tp_count - 1)

    def sums_copy(d):
        return remote(
            sums_ref, sums_all.at[me], s_send.at[d], s_recv.at[d], sec, lax.rem(me + d, tp_count)
        )

    def block_from(zd):
        return lax.rem(z - zd + outer, outer) * inner + x

    def normed_far(zd):
        return far(nall.at[me], nall.at[me], nf_send.at[zd], nf_recv.at[zd], zd)

    def normed_near(zd, xd):
        block = nall.at[block_from(zd)]
        slot = zd * inner + xd
        return near(block, block, nn_send.at[slot], nn_recv.at[slot], xd)

    def top_far(m, zd):
        return far(gall.at[m, me], gall.at[m, me], gf_send.at[m, zd], gf_recv.at[m, zd], zd)

    def hop(m, zd, section):
        return remote(
            gin_ref.at[m],
            gall.at[m, me],
            hop_send.at[m, zd],
            gf_recv.at[m, zd],
            section,
            zpeer(zd) * inner + x,
        )

    def grad_near(m, zd, xd):
        block = gall.at[m, block_from(zd)]
        slot = zd * inner + xd
        return near(block, block, gn_send.at[m, slot], gn_recv.at[m, slot], xd)

    def top_forward(m):
        for zd in range(1, outer):
            top_far(m, zd).wait()
            for xd in range(1, inner):
                grad_near(m, zd, xd).start()

    @pl.when(is_last)
    def _():
        for d in range(1, tp_count):
            sums_copy(d).start()
        sums_all[me] = sums_ref[...]

    for zd in range(1, outer):
        normed_far(zd).start()
    for xd in range(1, inner):
        normed_near(0, xd).start()

    @pl.when(is_last)
    def _():
        for d in range(1, tp_count):
            sums_copy(d).wait()
        total = sums_all[0]
        for d in range(1, tp_count):
            total = total + sums_all[d]
        chosen, rejected = counts_ref[0:1], counts_ref[1:2]
        margin = pair_beta * (total[0:1] / chosen - total[1:2] / rejected)
        weight = pair_beta * jax.nn.sigmoid(-margin)
        for m in range(batch_groups):
            token_weight = jnp.sum(
                member_ref[0, m] * (-weight / chosen) + member_ref[1, m] * (weight / rejected),
                -1,
                keepdims=True,
            )
            gall[m, me] = (token_weight * dir_ref[m].astype(wide)).astype(low)
            for zd in range(1, outer):
                top_far(m, zd).start()
            for xd in range(1, inner):
                grad_near(m, 0, xd).start()

    for zd in range(1, outer):
        normed_far(zd).wait()
        for xd in range(1, inner):
            normed_near(zd, xd).start()
    for zd in range(outer):
        for xd in range(1, inner):
            normed_near(zd, xd).wait()

    pl.when(is_last)(functools.partial(top_forward, 0))

    def merge(k, carry):
        cols = columns(k * step_width, step_width)
        for m in range(batch_groups):
            normed_ref[m * tokens : (m + 1) * tokens, cols] = jnp.concatenate(
                [nall[j, m, :, cols].astype(wide) for j in range(tp_count)], 0
            ).astype(low)
        return carry

    lax.fori_loop(0, width // step_width, merge, 0)

    own_slice = columns(me * slice_width, slice_width)
    loads[0].wait()
    loads[1].wait()
    for kind, weight_ref in enumerate((kw, vw)):
        product = jnp.dot(normed_ref[:, own_slice], weight_ref[...], preferred_element_type=wide)
        for k in range(key_count):
            kv_part[k, kind] = product[:, k * HEAD_WIDTH : (k + 1) * HEAD_WIDTH].astype(low)

    def kv_far_copy(zd):
        head = zpeer(zd) * inner // sharers
        return far(kv_part.at[head], kv_far.at[zd], kf_send.at[zd], kf_recv.at[zd], zd)

    def kv_near_copy(xd):
        return near(kv_near.at[0], kv_near.at[xd], kn_send.at[xd], kn_recv.at[xd], xd)

    for zd in range(1, outer):
        kv_far_copy(zd).start()

    loads[2].wait()

    def project(k, total):
        cols = columns(k * step_width, step_width)
        return total + jnp.dot(normed_ref[:, cols], wq[cols, :], preferred_element_type=wide)

    product = lax.fori_loop(
        0, width // step_width, project, jnp.zeros((every, head_cols), wide)
    ).astype(low)
    for m in range(batch_groups):
        queries[m] = product[m * tokens : (m + 1) * tokens]

    pl.when(is_last)(functools.partial(top_forward, 1))

    for zd in range(1, outer):
        kv_far_copy(zd).wait()
    for kind in range(2):
        total = kv_part[z * inner // sharers, kind].astype(wide)
        for zd in range(1, outer):
            total = total + kv_far[zd, kind].astype(wide)
        kv_near[0, kind] = total.astype(low)
    for xd in range(1, inner):
        kv_near_copy(xd).start()
    for xd in range(1, inner):
        kv_near_copy(xd).wait()
    for kind in range(2):
        total = kv_near[0, kind].astype(wide)
        for xd in range(1, inner):
            total = total + kv_near[xd, kind].astype(wide)
        total = total.astype(low)
        for m in range(batch_groups):
            kv[m, kind] = total[m * tokens : (m + 1) * tokens]

    for m in range(batch_groups):
        mask = allowed_ref[m] > 0.5
        for h in range(local_heads):
            head = slice(h * HEAD_WIDTH, (h + 1) * HEAD_WIDTH)
            scores = contract(queries[m, :, head], kv[m, 0], 1, 1) * scale
            value = jnp.exp(jnp.where(mask, scores, masked_score))
            value = value / jnp.sum(value, -1, keepdims=True)
            probs[m, h] = value
            att_ref[m * tokens : (m + 1) * tokens, head] = jnp.dot(
                value.astype(low), kv[m, 1], preferred_element_type=wide
            ).astype(low)
    loads[3].wait()
    gain_out_ref[...] = jnp.zeros_like(gain_out_ref)
    key_add[...] = jnp.zeros_like(key_add)

    def dkv_near_copy(m, xd):
        return near(
            dkv_near.at[m, 0], dkv_near.at[m, xd], dn_send.at[m, xd], dn_recv.at[m, xd], xd
        )

    def dkv_far_copy(m, zd):
        block = dkv_far.at[m, z]
        return far(block, block, df_send.at[m, zd], df_recv.at[m, zd], zd)

    def group(i):
        return columns(lax.rem(z + i, outer) * group_width, group_width)

    def part_near(m, i, xd):
        return near(
            part.at[m, xpeer(xd), :, :, group(i)],
            near_recv.at[m, xd - 1, :, :, group(i)],
            pn_send.at[m, xd, i - 1],
            pn_recv.at[m, xd, i - 1],
            xd,
        )

    def part_far(m, i, c, zd):
        cols = columns(c * group_width, group_width)
        return far(
            far_send.at[m, zd, :, cols],
            far_recv.at[m, zd, :, cols],
            pf_send.at[m, zd, i - 1],
            pf_recv.at[m, zd, i - 1],
            zd,
        )

    def part_group(m, i, with_keys):
        base = lax.rem(z + i, outer) * group_width

        def piece(k, carry):
            start = base + k * step_width
            cols = columns(start, step_width)
            product = contract(gq_ref[m], wq[cols, :], 1, 1)
            if with_keys:
                product = product + key_add[:, columns(k * step_width, step_width)]
            for block in range(tp_count):
                part[m, block % inner, block // inner, :, cols] = product[
                    block * rows : (block + 1) * rows
                ].astype(low)
            return carry

        lax.fori_loop(0, group_width // step_width, piece, 0)
        for xd in range(1, inner):
            part_near(m, i, xd).start()

    def sum_group(m, i):
        cols = group(i)
        for xd in range(1, inner):
            part_near(m, i, xd).wait()
        for zd in range(outer):
            total = part[m, x, zpeer(zd), :, cols].astype(wide)
            for xd in range(1, inner):
                total = total + near_recv[m, xd - 1, zpeer(zd), :, cols].astype(wide)
            if zd:
                far_send[m, zd, :, cols] = total.astype(low)
                part_far(m, i, lax.rem(z + i, outer), zd).start()
            else:
                far_recv[m, 0, :, cols] = total.astype(low)

    def step(m, carry):
        @pl.when(jnp.logical_not(is_last))
        def _():
            for zd in range(outer):
                hop(m, zd, sec).wait_recv()
                for xd in range(1, inner):
                    grad_near(m, zd, xd).start()

        for zd in range(outer):
            for xd in range(1, inner):
                grad_near(m, zd, xd).wait()

        def upstream(k, total):
            cols = columns(k * step_width, step_width)
            piece = jnp.concatenate(
                [gall[m, j, :, cols].astype(wide) for j in range(tp_count)], 0
            ).astype(low)
            up_ref[m, :, cols] = piece
            return total + contract(piece, wo[:, cols], 1, 1)

        grad_heads[...] = lax.fori_loop(
            0, width // step_width, upstream, jnp.zeros((tokens, head_cols), wide)
        ).astype(low)
        grad_keys = jnp.zeros((tokens, HEAD_WIDTH), wide)
        grad_values = jnp.zeros((tokens, HEAD_WIDTH), wide)
        for h in range(local_heads):
            head = slice(h * HEAD_WIDTH, (h + 1) * HEAD_WIDTH)
            grad_head = grad_heads[:, head]
            prob = probs[m, h]
            grad_probs = contract(grad_head, kv[m, 1], 1, 1)
            grad_scores = prob * (grad_probs - jnp.sum(prob * grad_probs, -1, keepdims=True))
            scores_low = (grad_scores * scale).astype(low)
            gq_ref[m, :, head] = jnp.dot(
                scores_low, kv[m, 0], preferred_element_type=wide
            ).astype(low)
            grad_keys = grad_keys + contract(scores_low, queries[m, :, head], 0, 0)
            grad_values = grad_values + contract(prob.astype(low), grad_head, 0, 0)
        dkv_near[m, 0, 0] = grad_keys.astype(low)
        dkv_near[m, 0, 1] = grad_values.astype(low)
        for xd in range(1, inner):
            dkv_near_copy(m, xd).start()

        part_group(m, 1, False)

        for xd in range(1, inner):
            dkv_near_copy(m, xd).wait()
        for kind in range(2):
            total = dkv_near[m, 0, kind].astype(wide)
            for xd in range(1, inner):
                total = total + dkv_near[m, xd, kind].astype(wide)
            dkv_far[m, z, kind] = total.astype(low)
        for zd in range(1, outer):
            dkv_far_copy(m, zd).start()

        def middle(i, inner_carry):
            part_group(m, i, False)
            sum_group(m, i - 1)
            return inner_carry

        lax.fori_loop(2, outer, middle, 0)

        for zd in range(1, outer):
            dkv_far_copy(m, zd).wait()
        holders = outer // key_count
        for kind in range(2):
            for k in range(key_count):
                total = dkv_far[m, k * holders, kind].astype(wide)
                for other in range(1, holders):
                    total = total + dkv_far[m, k * holders + other, kind].astype(wide)
                dkv_ref[kind, m, :, k * HEAD_WIDTH : (k + 1) * HEAD_WIDTH] = total.astype(low)
        key_add[:, columns(x * slice_width, slice_width)] = contract(
            dkv_ref[0, m], kw[...], 1, 1
        ) + contract(dkv_ref[1, m], vw[...], 1, 1)
        part_group(m, outer, True)
        sum_group(m, outer - 1)
        sum_group(m, outer)

        for zd in range(1, outer):
            for i in range(1, outer + 1):
                part_far(m, i, lax.rem(z + i, outer), zd).wait_send()
                part_far(m, i, lax.rem(z - zd + i + outer, outer), zd).wait_recv()

        dots = jnp.zeros((rows, 1), wide)
        chunk = 1024
        for k in range(width // chunk):
            cols = slice(k * chunk, (k + 1) * chunk)
            normed_grad = jnp.sum(far_recv[m, :, :, cols].astype(wide), 0)
            unit_part = unit[m, :, cols]
            gain_out_ref[:, cols] = gain_out_ref[:, cols] + jnp.sum(
                normed_grad * unit_part, 0, keepdims=True
            )
            scaled = normed_grad * gain_ref[:, cols].astype(wide)
            grad_unit[:, cols] = scaled
            dots = dots + jnp.sum(scaled * unit_part, -1, keepdims=True)
        dots = dots / width
        inv = inverse[m, :, 0:1]
        for k in range(width // chunk):
            cols = slice(k * chunk, (k + 1) * chunk)
            gin_ref[m, :, cols] = (
                gall[m, me, :, cols].astype(wide)
                + inv * (grad_unit[:, cols] - unit[m, :, cols] * dots)
            ).astype(low)

        @pl.when(feeds)
        def _():
            for zd in range(outer):
                hop(m, zd, sec - 1).start()

        return carry

    lax.fori_loop(0, batch_groups, step, 0)

    def gain_copy(d):
        return remote(
            gain_all.at[me],
            gain_all.at[me],
            t_send.at[d],
            t_recv.at[d],
            sec,
            lax.rem(me + d, tp_count),
        )

    gain_all[me] = gain_out_ref[...]
    for d in range(1, tp_count):
        gain_copy(d).start()
    for d in range(1, tp_count):
        gain_copy(d).wait()
    total = gain_all[0]
    for d in range(1, tp_count):
        total = total + gain_all[d]
    gain_out_ref[...] = total

    @pl.when(feeds)
    def _():
        for m in range(batch_groups):
            for zd in range(outer):
                hop(m, zd, sec - 1).wait_send()


def relay(saved, gain, wq, kw, vw, wo, direction, sums, counts, member, allowed):
    tp_count = lax.axis_size("tp")
    inner = inner_size(tp_count)
    outer = tp_count // inner
    batch_groups, rows, width = saved.shape
    tokens = rows * tp_count
    every = batch_groups * tokens
    head_cols = wq.shape[1]
    key_width = kw.shape[1]
    key_count = key_width // HEAD_WIDTH
    slice_width = kw.shape[0]
    vmem = pl.BlockSpec(memory_space=pltpu.VMEM)
    hbm = pl.BlockSpec(memory_space=pl.ANY)
    dma = pltpu.SemaphoreType.DMA
    groups = batch_groups
    return pl.pallas_call(
        functools.partial(relay_kernel, lax.axis_size("section"), tp_count),
        out_shape=[
            jax.ShapeDtypeStruct((groups, rows, width), low),
            jax.ShapeDtypeStruct((groups, tokens, width), low),
            jax.ShapeDtypeStruct((every, width), low),
            jax.ShapeDtypeStruct((every, head_cols), low),
            jax.ShapeDtypeStruct((groups, tokens, head_cols), low),
            jax.ShapeDtypeStruct((2, groups, tokens, key_width), low),
            jax.ShapeDtypeStruct((1, width), wide),
        ],
        in_specs=[vmem, vmem, hbm, hbm, hbm, hbm] + [vmem] * 5,
        out_specs=[vmem] * 7,
        scratch_shapes=[
            pltpu.VMEM(wq.shape, low),
            pltpu.VMEM(kw.shape, low),
            pltpu.VMEM(vw.shape, low),
            pltpu.VMEM(wo.shape, low),
            pltpu.VMEM((tp_count, groups, rows, width), low),
            pltpu.VMEM((groups, tp_count, rows, width), low),
            pltpu.VMEM((groups, inner, outer, rows, width), low),
            pltpu.VMEM((groups, inner - 1, outer, rows, width), low),
            pltpu.VMEM((groups, outer, rows, width), low),
            pltpu.VMEM((groups, outer, rows, width), low),
            pltpu.VMEM((groups, rows, width), wide),
            pltpu.VMEM((groups, rows, LANES), wide),
            pltpu.VMEM((rows, width), wide),
            pltpu.VMEM((groups, tokens, head_cols), low),
            pltpu.VMEM((groups, 2, tokens, HEAD_WIDTH), low),
            pltpu.VMEM((key_count, 2, every, HEAD_WIDTH), low),
            pltpu.VMEM((outer, 2, every, HEAD_WIDTH), low),
            pltpu.VMEM((inner, 2, every, HEAD_WIDTH), low),
            pltpu.VMEM((groups, head_cols // HEAD_WIDTH, tokens, tokens), wide),
            pltpu.VMEM((tokens, head_cols), low),
            pltpu.VMEM((tokens, inner * slice_width), wide),
            pltpu.VMEM((groups, inner, 2, tokens, HEAD_WIDTH), low),
            pltpu.VMEM((groups, outer, 2, tokens, HEAD_WIDTH), low),
            pltpu.VMEM((tp_count, 8, LANES), wide),
            pltpu.VMEM((tp_count, 1, width), wide),
            dma((4,)),
            dma((tp_count,)),
            dma((tp_count,)),
            dma((outer,)),
            dma((outer,)),
            dma((tp_count,)),
            dma((tp_count,)),
            dma((groups, outer)),
            dma((groups, outer)),
            dma((groups, tp_count)),
            dma((groups, tp_count)),
            dma((groups, outer)),
            dma((outer,)),
            dma((outer,)),
            dma((inner,)),
            dma((inner,)),
            dma((groups, inner)),
            dma((groups, inner)),
            dma((groups, outer)),
            dma((groups, outer)),
            dma((groups, inner, outer)),
            dma((groups, inner, outer)),
            dma((groups, outer, outer)),
            dma((groups, outer, outer)),
            dma((tp_count,)),
            dma((tp_count,)),
        ],
        compiler_params=pltpu.CompilerParams(
            collective_id=0, has_side_effects=True, vmem_limit_bytes=VMEM_LIMIT
        ),
        name="relay",
    )(saved, gain, wq, kw, vw, wo, direction, sums, counts, member, allowed)


def body(
    section_inputs,
    norm_gain,
    w_query,
    key_projection,
    value_projection,
    w_out,
    token_dir,
    tok_logratio,
    segment_ids,
    pair_of_slot,
    pair_counts,
):
    tp_index = lax.axis_index("tp")
    saved = section_inputs[0]
    batch_groups, rows, width = saved.shape
    key_weight = key_projection[0]
    slice_width, key_width = key_weight.shape
    tokens = segment_ids.shape[1]
    every = batch_groups * tokens

    lane = jnp.arange(LANES, dtype=jnp.int32)
    own_ids = lax.dynamic_slice_in_dim(segment_ids, tp_index * rows, rows, 1)
    target = jnp.arange(batch_groups, dtype=jnp.int32)[:, None] * SLOTS + own_ids // 2
    parity = jnp.arange(2, dtype=jnp.int32)[:, None, None, None]
    member = (
        (lane == target[None, :, :, None]) & (own_ids[None, :, :, None] % 2 == parity)
    ).astype(wide)
    sums = jnp.sum(member * tok_logratio[None, :, :, None], (1, 2))
    sums = jnp.pad(sums, ((0, 6), (0, 0)))
    pairs = pair_of_slot.reshape(-1)
    table = pairs[None, :, None] == jnp.arange(pair_counts.shape[0], dtype=jnp.int32)
    counts = jnp.sum(
        jnp.where(table, pair_counts.T[:, None, :].astype(wide), 0.0), -1
    )
    counts = jnp.pad(
        counts, ((0, 6), (0, LANES - pairs.shape[0])), constant_values=1.0
    )
    position = jnp.arange(tokens, dtype=jnp.int32)
    allowed = (
        (segment_ids[:, :, None] == segment_ids[:, None, :])
        & (position[:, None] >= position[None, :])[None]
    ).astype(wide)

    grads, upstream, normed, attended, grad_queries, dkv, gain_total = relay(
        saved,
        norm_gain[0].reshape(1, width),
        w_query[0],
        key_weight,
        value_projection[0],
        w_out[0],
        token_dir,
        sums,
        counts,
        member,
        allowed,
    )
    normed_cols = lax.dynamic_slice_in_dim(normed, tp_index * slice_width, slice_width, 1)
    outer = functools.partial(
        lax.dot_general,
        dimension_numbers=(((0,), (0,)), ((), ())),
        preferred_element_type=wide,
    )
    return (
        grads[None],
        outer(normed, grad_queries.reshape(every, -1)).astype(low)[None],
        outer(normed_cols, dkv[0].reshape(every, key_width)).astype(low)[None],
        outer(normed_cols, dkv[1].reshape(every, key_width)).astype(low)[None],
        outer(attended, upstream.reshape(every, width)).astype(low)[None],
        gain_total,
    )


def solution(mesh):
    placed = (
        P("section", None, "tp", None),
        P("section", None),
        P("section", None, "tp"),
        P("section", "tp", None),
        P("section", "tp", None),
        P("section", "tp", None),
        P(None, "tp", None),
        P(None, "tp"),
        P(),
        P(),
        P(),
    )
    return jax.shard_map(
        body,
        mesh=mesh,
        in_specs=placed,
        out_specs=(
            P("section", None, "tp", None),
            P("section", None, "tp"),
            P("section", "tp", None),
            P("section", "tp", None),
            P("section", "tp", None),
            P("section", None),
        ),
        check_vma=False,
    )
```

```python
import functools
import math

import jax
import jax.numpy as jnp
from jax import lax
from jax.experimental import pallas as pl
from jax.experimental.pallas import tpu as pltpu
from jax.sharding import PartitionSpec as P

HEAD_WIDTH = 128
SLOTS = 4
LANES = 128

norm_epsilon = 1e-05
pair_beta = 4.0
masked_score = -1e30

MESH = pl.DeviceIdType.MESH
VMEM_LIMIT = 56 * 1024 * 1024
low, wide = jnp.bfloat16, jnp.float32


def contract(left, right, left_dim, right_dim):
    return lax.dot_general(
        left, right, (((left_dim,), (right_dim,)), ((), ())), preferred_element_type=wide
    )


def inner_size(tp_count):
    inner = 1
    while 2 * (2 * inner) ** 2 <= tp_count:
        inner *= 2
    return inner


def relay_kernel(
    section_count,
    tp_count,
    saved_ref,
    gain_ref,
    wq_hbm,
    kw_hbm,
    vw_hbm,
    wo_hbm,
    dir_ref,
    ratio_ref,
    ids_ref,
    slot_ref,
    counts_ref,
    gin_ref,
    up_ref,
    normed_ref,
    normed_cols_ref,
    att_ref,
    gq_ref,
    dkv_ref,
    gain_out_ref,
    wq,
    kw,
    vw,
    wo,
    nall,
    gall,
    part,
    near_recv,
    far_send,
    far_recv,
    unit,
    inverse,
    grad_unit,
    queries,
    kv,
    kv_part,
    kv_far,
    kv_near,
    probs,
    grad_heads,
    key_send,
    key_recv,
    dkv_near,
    dkv_far,
    sums_all,
    gain_all,
    w_sem,
    s_send,
    s_recv,
    nf_send,
    nf_recv,
    nn_send,
    nn_recv,
    gf_send,
    gf_recv,
    gn_send,
    gn_recv,
    hop_send,
    kf_send,
    kf_recv,
    kn_send,
    kn_recv,
    dn_send,
    dn_recv,
    df_send,
    df_recv,
    pn_send,
    pn_recv,
    pf_send,
    pf_recv,
    ks_send,
    ks_recv,
    t_send,
    t_recv,
    go,
):
    sec = lax.axis_index("section")
    me = lax.axis_index("tp")
    inner = inner_size(tp_count)
    outer = tp_count // inner
    z, x = me // inner, lax.rem(me, inner)
    batch_groups, rows, width = saved_ref.shape
    tokens = rows * tp_count
    every = batch_groups * tokens
    head_cols = wq.shape[1]
    local_heads = head_cols // HEAD_WIDTH
    slice_width, key_width = kw.shape
    key_count = key_width // HEAD_WIDTH
    sharers = tp_count // key_count
    group_width = inner * slice_width
    step_width = min(1024, group_width)
    scale = 1.0 / math.sqrt(HEAD_WIDTH)
    is_last = sec == section_count - 1
    feeds = sec > 0

    def zpeer(zd):
        return lax.rem(z + zd, outer)

    def xpeer(xd):
        return lax.rem(x + xd, inner)

    def remote(source, target, send, receive, section, index):
        return pltpu.make_async_remote_copy(
            src_ref=source,
            dst_ref=target,
            send_sem=send,
            recv_sem=receive,
            device_id=(section, index),
            device_id_type=MESH,
        )

    def far(source, target, send, receive, zd):
        return remote(source, target, send, receive, sec, zpeer(zd) * inner + x)

    def near(source, target, send, receive, xd):
        return remote(source, target, send, receive, sec, z * inner + xpeer(xd))

    def columns(start, size):
        return pl.ds(pl.multiple_of(start, HEAD_WIDTH), size)

    loads = [
        pltpu.make_async_copy(source, target, w_sem.at[i])
        for i, (source, target) in enumerate(
            ((kw_hbm, kw), (vw_hbm, vw), (wq_hbm, wq), (wo_hbm, wo))
        )
    ]
    for load in loads:
        load.start()

    barrier = pltpu.get_barrier_semaphore()
    for d in range(1, tp_count):
        pl.semaphore_signal(
            barrier, inc=1, device_id=(sec, lax.rem(me + d, tp_count)), device_id_type=MESH
        )

    @pl.when(sec < section_count - 1)
    def _():
        for zd in range(outer):
            pl.semaphore_signal(
                barrier, inc=1, device_id=(sec + 1, zpeer(zd) * inner + x), device_id_type=MESH
            )

    gain_row = gain_ref[...].astype(wide)
    for m in range(batch_groups):
        rows_in = saved_ref[m].astype(wide)
        inv = lax.rsqrt(jnp.mean(rows_in * rows_in, -1, keepdims=True) + norm_epsilon)
        inverse[m] = jnp.broadcast_to(inv, (rows, LANES))
        unit_rows = rows_in * inv
        unit[m] = unit_rows
        nall[me, m] = (unit_rows * gain_row).astype(low)

    @pl.when(feeds)
    def _():
        pl.semaphore_wait(barrier, tp_count - 1 + outer)

    @pl.when(jnp.logical_not(feeds))
    def _():
        pl.semaphore_wait(barrier, tp_count - 1)

    def iota(shape, dim):
        return lax.broadcasted_iota(jnp.int32, shape, dim)

    def to_column(row, count, start):
        span = row.shape[1]
        pick = iota((count, span), 1) == iota((count, span), 0) + start
        return jnp.sum(jnp.where(pick, jnp.broadcast_to(row, (count, span)), 0.0), -1, keepdims=True)

    def own_member(m, kind):
        own = to_column(ids_ref[m : m + 1].astype(wide), rows, me * rows)
        slot = 2 * iota((rows, SLOTS), 1) + kind
        return (own == slot.astype(wide)).astype(wide)

    def slot_counts(m, kind):
        pairs = counts_ref.shape[0]
        table = iota((pairs, SLOTS), 0) == jnp.broadcast_to(slot_ref[m : m + 1], (pairs, SLOTS))
        count = counts_ref[:, kind : kind + 1].astype(wide)
        return jnp.sum(jnp.where(table, count, 0.0), 0, keepdims=True)

    def sums_copy(d):
        return remote(
            sums_all.at[me], sums_all.at[me], s_send.at[d], s_recv.at[d], sec, lax.rem(me + d, tp_count)
        )

    def block_from(zd):
        return lax.rem(z - zd + outer, outer) * inner + x

    def normed_far(zd):
        return far(nall.at[me], nall.at[me], nf_send.at[zd], nf_recv.at[zd], zd)

    def normed_near(zd, xd):
        block = nall.at[block_from(zd)]
        slot = zd * inner + xd
        return near(block, block, nn_send.at[slot], nn_recv.at[slot], xd)

    def top_far(m, zd):
        return far(gall.at[m, me], gall.at[m, me], gf_send.at[m, zd], gf_recv.at[m, zd], zd)

    def hop(m, zd, section):
        return remote(
            gin_ref.at[m],
            gall.at[m, me],
            hop_send.at[m, zd],
            gf_recv.at[m, zd],
            section,
            zpeer(zd) * inner + x,
        )

    def grad_near(m, zd, xd):
        block = gall.at[m, block_from(zd)]
        slot = zd * inner + xd
        return near(block, block, gn_send.at[m, slot], gn_recv.at[m, slot], xd)

    def top_forward(m):
        for zd in range(1, outer):
            top_far(m, zd).wait()
            for xd in range(1, inner):
                grad_near(m, zd, xd).start()

    @pl.when(is_last)
    def _():
        sums_all[me] = jnp.zeros(sums_all.shape[1:], wide)
        for m in range(batch_groups):
            ratio = to_column(ratio_ref[m : m + 1], rows, 0)
            for kind in range(2):
                sums_all[me, 2 * m + kind : 2 * m + kind + 1, 0:SLOTS] = jnp.sum(
                    own_member(m, kind) * ratio, 0, keepdims=True
                )
        for d in range(1, tp_count):
            sums_copy(d).start()

    @pl.when(sec == section_count - 2)
    def _():
        pl.semaphore_wait(go, 1)

    for zd in range(1, outer):
        normed_far(zd).start()
    for xd in range(1, inner):
        normed_near(0, xd).start()

    def top_start(m):
        for zd in range(1, outer):
            top_far(m, zd).start()
        for xd in range(1, inner):
            grad_near(m, 0, xd).start()

    @pl.when(is_last)
    def _():
        for d in range(1, tp_count):
            sums_copy(d).wait()
        total = sums_all[0]
        for d in range(1, tp_count):
            total = total + sums_all[d]
        for m in range(batch_groups):
            chosen, rejected = slot_counts(m, 0), slot_counts(m, 1)
            margin = pair_beta * (
                total[2 * m : 2 * m + 1, 0:SLOTS] / chosen
                - total[2 * m + 1 : 2 * m + 2, 0:SLOTS] / rejected
            )
            weight = pair_beta * jax.nn.sigmoid(-margin)
            token_weight = jnp.sum(
                own_member(m, 0) * (-weight / chosen) + own_member(m, 1) * (weight / rejected),
                -1,
                keepdims=True,
            )
            gall[m, me] = (token_weight * dir_ref[m].astype(wide)).astype(low)
        top_start(0)

    for zd in range(1, outer):
        normed_far(zd).wait()
        for xd in range(1, inner):
            normed_near(zd, xd).start()
    for zd in range(outer):
        for xd in range(1, inner):
            normed_near(zd, xd).wait()

    @pl.when(is_last)
    def _():
        top_forward(0)
        for xd in range(1, inner):
            for zd in range(outer):
                grad_near(0, zd, xd).wait()
        pl.semaphore_signal(go, inc=1, device_id=(sec - 1, me), device_id_type=MESH)

    def merge(k, carry):
        cols = columns(k * step_width, step_width)
        for m in range(batch_groups):
            normed_ref[m * tokens : (m + 1) * tokens, cols] = jnp.concatenate(
                [nall[j, m, :, cols].astype(wide) for j in range(tp_count)], 0
            ).astype(low)
        return carry

    lax.fori_loop(0, width // step_width, merge, 0)

    normed_cols_ref[...] = normed_ref[:, columns(me * slice_width, slice_width)]
    loads[0].wait()
    loads[1].wait()
    for kind, weight_ref in enumerate((kw, vw)):
        product = jnp.dot(normed_cols_ref[...], weight_ref[...], preferred_element_type=wide)
        for k in range(key_count):
            kv_part[k, kind] = product[:, k * HEAD_WIDTH : (k + 1) * HEAD_WIDTH].astype(low)

    def kv_far_copy(zd):
        head = zpeer(zd) * inner // sharers
        return far(kv_part.at[head], kv_far.at[zd], kf_send.at[zd], kf_recv.at[zd], zd)

    def kv_near_copy(xd):
        return near(kv_near.at[0], kv_near.at[xd], kn_send.at[xd], kn_recv.at[xd], xd)

    for zd in range(1, outer):
        kv_far_copy(zd).start()

    loads[2].wait()

    def project(k, total):
        cols = columns(k * step_width, step_width)
        return total + jnp.dot(normed_ref[:, cols], wq[cols, :], preferred_element_type=wide)

    product = lax.fori_loop(
        0, width // step_width, project, jnp.zeros((every, head_cols), wide)
    ).astype(low)
    for m in range(batch_groups):
        queries[m] = product[m * tokens : (m + 1) * tokens]

    for zd in range(1, outer):
        kv_far_copy(zd).wait()
    for kind in range(2):
        total = kv_part[z * inner // sharers, kind].astype(wide)
        for zd in range(1, outer):
            total = total + kv_far[zd, kind].astype(wide)
        kv_near[0, kind] = total.astype(low)
    for xd in range(1, inner):
        kv_near_copy(xd).start()
    for xd in range(1, inner):
        kv_near_copy(xd).wait()

    @pl.when(is_last)
    def _():
        for m in range(1, batch_groups):
            top_start(m)

    for kind in range(2):
        total = kv_near[0, kind].astype(wide)
        for xd in range(1, inner):
            total = total + kv_near[xd, kind].astype(wide)
        total = total.astype(low)
        for m in range(batch_groups):
            kv[m, kind] = total[m * tokens : (m + 1) * tokens]

    for m in range(batch_groups):
        ids = ids_ref[m : m + 1].astype(wide)
        mask = (to_column(ids, tokens, 0) == jnp.broadcast_to(ids, (tokens, tokens))) & (
            iota((tokens, tokens), 0) >= iota((tokens, tokens), 1)
        )
        for h in range(local_heads):
            head = slice(h * HEAD_WIDTH, (h + 1) * HEAD_WIDTH)
            scores = contract(queries[m, :, head], kv[m, 0], 1, 1) * scale
            value = jnp.exp(jnp.where(mask, scores, masked_score))
            value = value / jnp.sum(value, -1, keepdims=True)
            probs[m, h] = value
            att_ref[m * tokens : (m + 1) * tokens, head] = jnp.dot(
                value.astype(low), kv[m, 1], preferred_element_type=wide
            ).astype(low)
    loads[3].wait()
    gain_out_ref[...] = jnp.zeros_like(gain_out_ref)

    @pl.when(is_last)
    def _():
        for m in range(1, batch_groups):
            top_forward(m)

    def dkv_near_copy(m, xd):
        return near(
            dkv_near.at[m, 0], dkv_near.at[m, xd], dn_send.at[m, xd], dn_recv.at[m, xd], xd
        )

    def dkv_far_copy(m, zd):
        block = dkv_far.at[m, z]
        return far(block, block, df_send.at[m, zd], df_recv.at[m, zd], zd)

    def group(i):
        return columns(lax.rem(z + i, outer) * group_width, group_width)

    def part_near(m, i, xd):
        return near(
            part.at[m, xpeer(xd), :, :, group(i)],
            near_recv.at[m, xd - 1, :, :, group(i)],
            pn_send.at[m, xd, i - 1],
            pn_recv.at[m, xd, i - 1],
            xd,
        )

    def part_far(m, i, c, zd):
        cols = columns(c * group_width, group_width)
        return far(
            far_send.at[m, zd, :, cols],
            far_recv.at[m, zd, :, cols],
            pf_send.at[m, zd, i - 1],
            pf_recv.at[m, zd, i - 1],
            zd,
        )

    def key_copy(m, d):
        peer = lax.rem(me + d, tp_count)
        return remote(
            key_send.at[m, peer], key_recv.at[m, me], ks_send.at[m, d], ks_recv.at[m, d], sec, peer
        )

    def part_group(m, i):
        base = lax.rem(z + i, outer) * group_width

        def piece(k, carry):
            start = base + k * step_width
            cols = columns(start, step_width)
            product = contract(gq_ref[m], wq[cols, :], 1, 1)
            for block in range(tp_count):
                part[m, block % inner, block // inner, :, cols] = product[
                    block * rows : (block + 1) * rows
                ].astype(low)
            return carry

        lax.fori_loop(0, group_width // step_width, piece, 0)
        for xd in range(1, inner):
            part_near(m, i, xd).start()

    def sum_group(m, i):
        cols = group(i)
        for xd in range(1, inner):
            part_near(m, i, xd).wait()
        for zd in range(outer):
            total = part[m, x, zpeer(zd), :, cols].astype(wide)
            for xd in range(1, inner):
                total = total + near_recv[m, xd - 1, zpeer(zd), :, cols].astype(wide)
            if zd:
                far_send[m, zd, :, cols] = total.astype(low)
                part_far(m, i, lax.rem(z + i, outer), zd).start()
            else:
                far_recv[m, 0, :, cols] = total.astype(low)

    def step(m, carry):
        @pl.when(jnp.logical_not(is_last))
        def _():
            for zd in range(outer):
                hop(m, zd, sec).wait_recv()
                for xd in range(1, inner):
                    grad_near(m, zd, xd).start()

        @pl.when(jnp.logical_not(is_last) | (m > 0))
        def _():
            for zd in range(outer):
                for xd in range(1, inner):
                    grad_near(m, zd, xd).wait()

        def upstream(k, total):
            cols = columns(k * step_width, step_width)
            piece = jnp.concatenate(
                [gall[m, j, :, cols].astype(wide) for j in range(tp_count)], 0
            ).astype(low)
            up_ref[m, :, cols] = piece
            return total + contract(piece, wo[:, cols], 1, 1)

        grad_heads[...] = lax.fori_loop(
            0, width // step_width, upstream, jnp.zeros((tokens, head_cols), wide)
        ).astype(low)
        grad_keys = jnp.zeros((tokens, HEAD_WIDTH), wide)
        grad_values = jnp.zeros((tokens, HEAD_WIDTH), wide)
        for h in range(local_heads):
            head = slice(h * HEAD_WIDTH, (h + 1) * HEAD_WIDTH)
            grad_head = grad_heads[:, head]
            prob = probs[m, h]
            grad_probs = contract(grad_head, kv[m, 1], 1, 1)
            grad_scores = prob * (grad_probs - jnp.sum(prob * grad_probs, -1, keepdims=True))
            scores_low = (grad_scores * scale).astype(low)
            gq_ref[m, :, head] = jnp.dot(
                scores_low, kv[m, 0], preferred_element_type=wide
            ).astype(low)
            grad_keys = grad_keys + contract(scores_low, queries[m, :, head], 0, 0)
            grad_values = grad_values + contract(prob.astype(low), grad_head, 0, 0)
        dkv_near[m, 0, 0] = grad_keys.astype(low)
        dkv_near[m, 0, 1] = grad_values.astype(low)
        for xd in range(1, inner):
            dkv_near_copy(m, xd).start()

        part_group(m, 1)

        for xd in range(1, inner):
            dkv_near_copy(m, xd).wait()
        for kind in range(2):
            total = dkv_near[m, 0, kind].astype(wide)
            for xd in range(1, inner):
                total = total + dkv_near[m, xd, kind].astype(wide)
            dkv_far[m, z, kind] = total.astype(low)
        for zd in range(1, outer):
            dkv_far_copy(m, zd).start()

        def middle(i, inner_carry):
            part_group(m, i)
            sum_group(m, i - 1)
            return inner_carry

        lax.fori_loop(2, outer + 1, middle, 0)

        for zd in range(1, outer):
            dkv_far_copy(m, zd).wait()
        holders = outer // key_count
        for kind in range(2):
            for k in range(key_count):
                total = dkv_far[m, k * holders, kind].astype(wide)
                for other in range(1, holders):
                    total = total + dkv_far[m, k * holders + other, kind].astype(wide)
                dkv_ref[kind, m, :, k * HEAD_WIDTH : (k + 1) * HEAD_WIDTH] = total.astype(low)
        key_slice = contract(dkv_ref[0, m], kw[...], 1, 1) + contract(
            dkv_ref[1, m], vw[...], 1, 1
        )
        for j in range(tp_count):
            key_send[m, j] = key_slice[j * rows : (j + 1) * rows].astype(low)
        for d in range(1, tp_count):
            key_copy(m, d).start()
        key_recv[m, me] = key_send[m, me]
        sum_group(m, outer)

        for zd in range(1, outer):
            for i in range(1, outer + 1):
                part_far(m, i, lax.rem(z + i, outer), zd).wait_send()
                part_far(m, i, lax.rem(z - zd + i + outer, outer), zd).wait_recv()

        for d in range(1, tp_count):
            key_copy(m, d).wait()

        dots = jnp.zeros((rows, 1), wide)
        chunk = 1024
        for k in range(tp_count):
            cols = slice(k * slice_width, (k + 1) * slice_width)
            normed_grad = key_recv[m, k].astype(wide) + jnp.sum(
                far_recv[m, :, :, cols].astype(wide), 0
            )
            unit_part = unit[m, :, cols]
            gain_out_ref[:, cols] = gain_out_ref[:, cols] + jnp.sum(
                normed_grad * unit_part, 0, keepdims=True
            )
            scaled = normed_grad * gain_ref[:, cols].astype(wide)
            grad_unit[:, cols] = scaled
            dots = dots + jnp.sum(scaled * unit_part, -1, keepdims=True)
        dots = dots / width
        inv = inverse[m, :, 0:1]
        for k in range(width // chunk):
            cols = slice(k * chunk, (k + 1) * chunk)
            gin_ref[m, :, cols] = (
                gall[m, me, :, cols].astype(wide)
                + inv * (grad_unit[:, cols] - unit[m, :, cols] * dots)
            ).astype(low)

        @pl.when(feeds)
        def _():
            for zd in range(outer):
                hop(m, zd, sec - 1).start()

        return carry

    lax.fori_loop(0, batch_groups, step, 0)

    def gain_copy(d):
        return remote(
            gain_all.at[me],
            gain_all.at[me],
            t_send.at[d],
            t_recv.at[d],
            sec,
            lax.rem(me + d, tp_count),
        )

    gain_all[me] = gain_out_ref[...]
    for d in range(1, tp_count):
        gain_copy(d).start()
    for d in range(1, tp_count):
        gain_copy(d).wait()
    total = gain_all[0]
    for d in range(1, tp_count):
        total = total + gain_all[d]
    gain_out_ref[...] = total

    @pl.when(feeds)
    def _():
        for m in range(batch_groups):
            for zd in range(outer):
                hop(m, zd, sec - 1).wait_send()


def relay(saved, gain, wq, kw, vw, wo, direction, ratio, ids, slots, counts):
    tp_count = lax.axis_size("tp")
    inner = inner_size(tp_count)
    outer = tp_count // inner
    batch_groups, rows, width = saved.shape
    tokens = rows * tp_count
    every = batch_groups * tokens
    head_cols = wq.shape[1]
    key_width = kw.shape[1]
    key_count = key_width // HEAD_WIDTH
    slice_width = kw.shape[0]
    vmem = pl.BlockSpec(memory_space=pltpu.VMEM)
    hbm = pl.BlockSpec(memory_space=pl.ANY)
    dma = pltpu.SemaphoreType.DMA
    groups = batch_groups
    return pl.pallas_call(
        functools.partial(relay_kernel, lax.axis_size("section"), tp_count),
        out_shape=[
            jax.ShapeDtypeStruct((groups, rows, width), low),
            jax.ShapeDtypeStruct((groups, tokens, width), low),
            jax.ShapeDtypeStruct((every, width), low),
            jax.ShapeDtypeStruct((every, slice_width), low),
            jax.ShapeDtypeStruct((every, head_cols), low),
            jax.ShapeDtypeStruct((groups, tokens, head_cols), low),
            jax.ShapeDtypeStruct((2, groups, tokens, key_width), low),
            jax.ShapeDtypeStruct((1, width), wide),
        ],
        in_specs=[vmem, vmem, hbm, hbm, hbm, hbm] + [vmem] * 5,
        out_specs=[vmem] * 8,
        scratch_shapes=[
            pltpu.VMEM(wq.shape, low),
            pltpu.VMEM(kw.shape, low),
            pltpu.VMEM(vw.shape, low),
            pltpu.VMEM(wo.shape, low),
            pltpu.VMEM((tp_count, groups, rows, width), low),
            pltpu.VMEM((groups, tp_count, rows, width), low),
            pltpu.VMEM((groups, inner, outer, rows, width), low),
            pltpu.VMEM((groups, inner - 1, outer, rows, width), low),
            pltpu.VMEM((groups, outer, rows, width), low),
            pltpu.VMEM((groups, outer, rows, width), low),
            pltpu.VMEM((groups, rows, width), wide),
            pltpu.VMEM((groups, rows, LANES), wide),
            pltpu.VMEM((rows, width), wide),
            pltpu.VMEM((groups, tokens, head_cols), low),
            pltpu.VMEM((groups, 2, tokens, HEAD_WIDTH), low),
            pltpu.VMEM((key_count, 2, every, HEAD_WIDTH), low),
            pltpu.VMEM((outer, 2, every, HEAD_WIDTH), low),
            pltpu.VMEM((inner, 2, every, HEAD_WIDTH), low),
            pltpu.VMEM((groups, head_cols // HEAD_WIDTH, tokens, tokens), wide),
            pltpu.VMEM((tokens, head_cols), low),
            pltpu.VMEM((groups, tp_count, rows, slice_width), low),
            pltpu.VMEM((groups, tp_count, rows, slice_width), low),
            pltpu.VMEM((groups, inner, 2, tokens, HEAD_WIDTH), low),
            pltpu.VMEM((groups, outer, 2, tokens, HEAD_WIDTH), low),
            pltpu.VMEM((tp_count, 8, LANES), wide),
            pltpu.VMEM((tp_count, 1, width), wide),
            dma((4,)),
            dma((tp_count,)),
            dma((tp_count,)),
            dma((outer,)),
            dma((outer,)),
            dma((tp_count,)),
            dma((tp_count,)),
            dma((groups, outer)),
            dma((groups, outer)),
            dma((groups, tp_count)),
            dma((groups, tp_count)),
            dma((groups, outer)),
            dma((outer,)),
            dma((outer,)),
            dma((inner,)),
            dma((inner,)),
            dma((groups, inner)),
            dma((groups, inner)),
            dma((groups, outer)),
            dma((groups, outer)),
            dma((groups, inner, outer)),
            dma((groups, inner, outer)),
            dma((groups, outer, outer)),
            dma((groups, outer, outer)),
            dma((groups, tp_count)),
            dma((groups, tp_count)),
            dma((tp_count,)),
            dma((tp_count,)),
            pltpu.SemaphoreType.REGULAR,
        ],
        compiler_params=pltpu.CompilerParams(
            collective_id=0, has_side_effects=True, vmem_limit_bytes=VMEM_LIMIT
        ),
        name="relay",
    )(saved, gain, wq, kw, vw, wo, direction, ratio, ids, slots, counts)


def weights_kernel(
    normed_ref,
    normed_cols_ref,
    gq_ref,
    dkv_ref,
    att_ref,
    up_ref,
    grads_in,
    gain_in,
    grads_out,
    of_query,
    of_key,
    of_value,
    of_out,
    gain_out,
):
    @pl.when(pl.program_id(0) == 0)
    def _():
        grads_out[...] = grads_in[...]
        gain_out[...] = gain_in[...]

    of_query[...] = contract(normed_ref[...], gq_ref[...], 0, 0).astype(low)
    of_out[...] = contract(att_ref[...], up_ref[...], 0, 0).astype(low)
    of_key[...] = contract(normed_cols_ref[...], dkv_ref[0], 0, 0).astype(low)
    of_value[...] = contract(normed_cols_ref[...], dkv_ref[1], 0, 0).astype(low)


def weight_gradients(normed, normed_cols, grad_queries, dkv, attended, upstream, grads, gain):
    every, width = normed.shape
    head_cols = grad_queries.shape[1]
    slice_width, key_width = normed_cols.shape[1], dkv.shape[2]
    steps = slice_width // HEAD_WIDTH
    part = width // steps

    def whole(shape):
        return pl.BlockSpec(shape, lambda i: (0,) * len(shape))

    def lanes(shape):
        return pl.BlockSpec(shape, lambda i: (0, i))

    def above(shape):
        return pl.BlockSpec(shape, lambda i: (i, 0))

    return pl.pallas_call(
        weights_kernel,
        grid=(steps,),
        out_shape=[
            jax.ShapeDtypeStruct(grads.shape, low),
            jax.ShapeDtypeStruct((width, head_cols), low),
            jax.ShapeDtypeStruct((slice_width, key_width), low),
            jax.ShapeDtypeStruct((slice_width, key_width), low),
            jax.ShapeDtypeStruct((head_cols, width), low),
            jax.ShapeDtypeStruct(gain.shape, wide),
        ],
        in_specs=[
            lanes((every, part)),
            lanes((every, HEAD_WIDTH)),
            whole(grad_queries.shape),
            whole(dkv.shape),
            whole(attended.shape),
            lanes((every, part)),
            whole(grads.shape),
            whole(gain.shape),
        ],
        out_specs=[
            whole(grads.shape),
            above((part, head_cols)),
            above((HEAD_WIDTH, key_width)),
            above((HEAD_WIDTH, key_width)),
            lanes((head_cols, part)),
            whole(gain.shape),
        ],
        compiler_params=pltpu.CompilerParams(vmem_limit_bytes=32 * 1024 * 1024),
        name="weight_gradients",
    )(normed, normed_cols, grad_queries, dkv, attended, upstream, grads, gain)


def body(
    section_inputs,
    norm_gain,
    w_query,
    key_projection,
    value_projection,
    w_out,
    token_dir,
    tok_logratio,
    segment_ids,
    pair_of_slot,
    pair_counts,
):
    saved = section_inputs[0]
    width = saved.shape[2]
    every = segment_ids.size
    grads, upstream, normed, normed_cols, attended, grad_queries, dkv, gain_total = relay(
        saved,
        norm_gain[0].reshape(1, width),
        w_query[0],
        key_projection[0],
        value_projection[0],
        w_out[0],
        token_dir,
        tok_logratio,
        segment_ids,
        pair_of_slot,
        pair_counts,
    )
    grads, of_query, of_key, of_value, of_out, gain_total = weight_gradients(
        normed,
        normed_cols,
        grad_queries.reshape(every, -1),
        dkv.reshape(2, every, -1),
        attended,
        upstream.reshape(every, width),
        grads,
        gain_total,
    )
    return (
        grads[None],
        of_query[None],
        of_key[None],
        of_value[None],
        of_out[None],
        gain_total,
    )


def solution(mesh):
    placed = (
        P("section", None, "tp", None),
        P("section", None),
        P("section", None, "tp"),
        P("section", "tp", None),
        P("section", "tp", None),
        P("section", "tp", None),
        P(None, "tp", None),
        P(None, "tp"),
        P(),
        P(),
        P(),
    )
    return jax.shard_map(
        body,
        mesh=mesh,
        in_specs=placed,
        out_specs=(
            P("section", None, "tp", None),
            P("section", None, "tp"),
            P("section", "tp", None),
            P("section", "tp", None),
            P("section", "tp", None),
            P("section", None),
        ),
        check_vma=False,
    )
```

```python
import functools
import math

import jax
import jax.numpy as jnp
from jax import lax
from jax.experimental import pallas as pl
from jax.experimental.pallas import tpu as pltpu
from jax.sharding import PartitionSpec as P

HEAD_WIDTH = 128
SLOTS = 4
LANES = 128
CHUNKS = 4

norm_epsilon = 1e-05
pair_beta = 4.0
masked_score = -1e30

MESH = pl.DeviceIdType.MESH
VMEM_LIMIT = 38 * 1024 * 1024
low, wide = jnp.bfloat16, jnp.float32


def contract(left, right, left_dim, right_dim):
    return lax.dot_general(
        left, right, (((left_dim,), (right_dim,)), ((), ())), preferred_element_type=wide
    )


def inner_size(tp_count):
    inner = 1
    while 2 * (2 * inner) ** 2 <= tp_count:
        inner *= 2
    return inner


def relay_kernel(
    section_count,
    tp_count,
    saved_ref,
    gain_ref,
    wq_hbm,
    kw,
    vw,
    wo_hbm,
    dir_ref,
    ratio_ref,
    ids_ref,
    slot_ref,
    counts_ref,
    gin_ref,
    up_ref,
    normed_ref,
    normed_cols_ref,
    att_ref,
    gq_ref,
    dkv_ref,
    gain_out_ref,
    wq,
    wo,
    nall,
    gall,
    part,
    near_recv,
    far_send,
    far_recv,
    unit,
    inverse,
    grad_unit,
    queries,
    kv,
    kv_part,
    kv_far,
    kv_near,
    probs,
    grad_heads,
    key_send,
    key_recv,
    dkv_near,
    dkv_far,
    sums_all,
    gain_all,
    w_sem,
    s_send,
    s_recv,
    nf_send,
    nf_recv,
    nn_send,
    nn_recv,
    gf_send,
    gf_recv,
    gn_send,
    gn_recv,
    hop_send,
    kf_send,
    kf_recv,
    kn_send,
    kn_recv,
    dn_send,
    dn_recv,
    df_send,
    df_recv,
    pn_send,
    pn_recv,
    pf_send,
    pf_recv,
    ks_send,
    ks_recv,
    t_send,
    t_recv,
    go,
):
    sec = lax.axis_index("section")
    me = lax.axis_index("tp")
    inner = inner_size(tp_count)
    outer = tp_count // inner
    z, x = me // inner, lax.rem(me, inner)
    batch_groups, rows, width = saved_ref.shape
    tokens = rows * tp_count
    every = batch_groups * tokens
    head_cols = wq.shape[1]
    local_heads = head_cols // HEAD_WIDTH
    slice_width, key_width = kw.shape
    key_count = key_width // HEAD_WIDTH
    sharers = tp_count // key_count
    group_width = inner * slice_width
    step_width = min(1024, group_width)
    chunk_width = width // CHUNKS
    per_group = CHUNKS // batch_groups
    normed_width = width // per_group
    scale = 1.0 / math.sqrt(HEAD_WIDTH)
    is_last = sec == section_count - 1
    feeds = sec > 0

    def zpeer(zd):
        return lax.rem(z + zd, outer)

    def xpeer(xd):
        return lax.rem(x + xd, inner)

    def remote(source, target, send, receive, section, index):
        return pltpu.make_async_remote_copy(
            src_ref=source,
            dst_ref=target,
            send_sem=send,
            recv_sem=receive,
            device_id=(section, index),
            device_id_type=MESH,
        )

    def far(source, target, send, receive, zd):
        return remote(source, target, send, receive, sec, zpeer(zd) * inner + x)

    def near(source, target, send, receive, xd):
        return remote(source, target, send, receive, sec, z * inner + xpeer(xd))

    def columns(start, size):
        return pl.ds(pl.multiple_of(start, HEAD_WIDTH), size)

    loads = [
        pltpu.make_async_copy(source, target, w_sem.at[i])
        for i, (source, target) in enumerate(
            ((wq_hbm, wq), (wo_hbm, wo))
        )
    ]
    for load in loads:
        load.start()

    barrier = pltpu.get_barrier_semaphore()
    for d in range(1, tp_count):
        pl.semaphore_signal(
            barrier, inc=1, device_id=(sec, lax.rem(me + d, tp_count)), device_id_type=MESH
        )

    @pl.when(sec < section_count - 1)
    def _():
        for zd in range(outer):
            pl.semaphore_signal(
                barrier, inc=1, device_id=(sec + 1, zpeer(zd) * inner + x), device_id_type=MESH
            )

    gain_row = gain_ref[...].astype(wide)
    for m in range(batch_groups):
        rows_in = saved_ref[m].astype(wide)
        inv = lax.rsqrt(jnp.mean(rows_in * rows_in, -1, keepdims=True) + norm_epsilon)
        inverse[m] = jnp.broadcast_to(inv, (rows, LANES))
        unit_rows = rows_in * inv
        unit[m] = unit_rows
        nall[me, m] = (unit_rows * gain_row).astype(low)

    @pl.when(feeds)
    def _():
        pl.semaphore_wait(barrier, tp_count - 1 + outer)

    @pl.when(jnp.logical_not(feeds))
    def _():
        pl.semaphore_wait(barrier, tp_count - 1)

    def iota(shape, dim):
        return lax.broadcasted_iota(jnp.int32, shape, dim)

    def to_column(row, count, start):
        span = row.shape[1]
        pick = iota((count, span), 1) == iota((count, span), 0) + start
        return jnp.sum(jnp.where(pick, jnp.broadcast_to(row, (count, span)), 0.0), -1, keepdims=True)

    def own_member(m, kind):
        own = to_column(ids_ref[m : m + 1].astype(wide), rows, me * rows)
        slot = 2 * iota((rows, SLOTS), 1) + kind
        return (own == slot.astype(wide)).astype(wide)

    def slot_counts(m, kind):
        pairs = counts_ref.shape[0]
        table = iota((pairs, SLOTS), 0) == jnp.broadcast_to(slot_ref[m : m + 1], (pairs, SLOTS))
        count = counts_ref[:, kind : kind + 1].astype(wide)
        return jnp.sum(jnp.where(table, count, 0.0), 0, keepdims=True)

    def sums_copy(d):
        return remote(
            sums_all.at[me], sums_all.at[me], s_send.at[d], s_recv.at[d], sec, lax.rem(me + d, tp_count)
        )

    def block_from(zd):
        return lax.rem(z - zd + outer, outer) * inner + x

    def normed_piece(block, c):
        start = c % per_group * normed_width
        return nall.at[block, c // per_group, :, start : start + normed_width]

    def normed_far(c, zd):
        block = normed_piece(me, c)
        return far(block, block, nf_send.at[c, zd], nf_recv.at[c, zd], zd)

    def normed_near(c, zd, xd):
        block = normed_piece(block_from(zd), c)
        slot = zd * inner + xd
        return near(block, block, nn_send.at[c, slot], nn_recv.at[c, slot], xd)

    def chunk(c):
        return columns(c * chunk_width, chunk_width)

    def top_far(m, c, zd):
        block = gall.at[m, me, :, chunk(c)]
        return far(block, block, gf_send.at[m, c, zd], gf_recv.at[m, c, zd], zd)

    def hop(m, c, zd, section):
        return remote(
            gin_ref.at[m, :, chunk(c)],
            gall.at[m, me, :, chunk(c)],
            hop_send.at[m, c, zd],
            gf_recv.at[m, c, zd],
            section,
            zpeer(zd) * inner + x,
        )

    def grad_near(m, c, zd, xd):
        block = gall.at[m, block_from(zd), :, chunk(c)]
        slot = zd * inner + xd
        return near(block, block, gn_send.at[m, c, slot], gn_recv.at[m, c, slot], xd)

    def top_forward(m):
        for c in range(CHUNKS):
            for zd in range(1, outer):
                top_far(m, c, zd).wait()
                for xd in range(1, inner):
                    grad_near(m, c, zd, xd).start()

    @pl.when(is_last)
    def _():
        sums_all[me] = jnp.zeros(sums_all.shape[1:], wide)
        for m in range(batch_groups):
            ratio = to_column(ratio_ref[m : m + 1], rows, 0)
            for kind in range(2):
                sums_all[me, 2 * m + kind : 2 * m + kind + 1, 0:SLOTS] = jnp.sum(
                    own_member(m, kind) * ratio, 0, keepdims=True
                )
        for d in range(1, tp_count):
            sums_copy(d).start()

    @pl.when(sec == section_count - 2)
    def _():
        pl.semaphore_wait(go, 1)

    for c in range(CHUNKS):
        for zd in range(1, outer):
            normed_far(c, zd).start()
        for xd in range(1, inner):
            normed_near(c, 0, xd).start()

    def top_start(m):
        for c in range(CHUNKS):
            for zd in range(1, outer):
                top_far(m, c, zd).start()
            for xd in range(1, inner):
                grad_near(m, c, 0, xd).start()

    @pl.when(is_last)
    def _():
        for d in range(1, tp_count):
            sums_copy(d).wait()
        total = sums_all[0]
        for d in range(1, tp_count):
            total = total + sums_all[d]
        for m in range(batch_groups):
            chosen, rejected = slot_counts(m, 0), slot_counts(m, 1)
            margin = pair_beta * (
                total[2 * m : 2 * m + 1, 0:SLOTS] / chosen
                - total[2 * m + 1 : 2 * m + 2, 0:SLOTS] / rejected
            )
            weight = pair_beta * jax.nn.sigmoid(-margin)
            token_weight = jnp.sum(
                own_member(m, 0) * (-weight / chosen) + own_member(m, 1) * (weight / rejected),
                -1,
                keepdims=True,
            )
            gall[m, me] = (token_weight * dir_ref[m].astype(wide)).astype(low)
        top_start(0)

    for c in range(CHUNKS):
        for zd in range(1, outer):
            normed_far(c, zd).wait()
            for xd in range(1, inner):
                normed_near(c, zd, xd).start()
    for c in range(CHUNKS):
        for zd in range(outer):
            for xd in range(1, inner):
                normed_near(c, zd, xd).wait()

    @pl.when(is_last)
    def _():
        top_forward(0)
        pl.semaphore_signal(go, inc=1, device_id=(sec - 1, me), device_id_type=MESH)

    def merge(k, carry):
        cols = columns(k * step_width, step_width)
        for m in range(batch_groups):
            normed_ref[m * tokens : (m + 1) * tokens, cols] = jnp.concatenate(
                [nall[j, m, :, cols].astype(wide) for j in range(tp_count)], 0
            ).astype(low)
        return carry

    lax.fori_loop(0, width // step_width, merge, 0)

    normed_cols_ref[...] = normed_ref[:, columns(me * slice_width, slice_width)]
    for kind, weight_ref in enumerate((kw, vw)):
        product = jnp.dot(normed_cols_ref[...], weight_ref[...], preferred_element_type=wide)
        for k in range(key_count):
            kv_part[k, kind] = product[:, k * HEAD_WIDTH : (k + 1) * HEAD_WIDTH].astype(low)

    def kv_far_copy(zd):
        head = zpeer(zd) * inner // sharers
        return far(kv_part.at[head], kv_far.at[zd], kf_send.at[zd], kf_recv.at[zd], zd)

    def kv_near_copy(xd):
        return near(kv_near.at[0], kv_near.at[xd], kn_send.at[xd], kn_recv.at[xd], xd)

    for zd in range(1, outer):
        kv_far_copy(zd).start()

    loads[0].wait()

    def project(k, total):
        cols = columns(k * step_width, step_width)
        return total + jnp.dot(normed_ref[:, cols], wq[cols, :], preferred_element_type=wide)

    product = lax.fori_loop(
        0, width // step_width, project, jnp.zeros((every, head_cols), wide)
    ).astype(low)
    for m in range(batch_groups):
        queries[m] = product[m * tokens : (m + 1) * tokens]

    for zd in range(1, outer):
        kv_far_copy(zd).wait()
    for kind in range(2):
        total = kv_part[z * inner // sharers, kind].astype(wide)
        for zd in range(1, outer):
            total = total + kv_far[zd, kind].astype(wide)
        kv_near[0, kind] = total.astype(low)
    for xd in range(1, inner):
        kv_near_copy(xd).start()
    for xd in range(1, inner):
        kv_near_copy(xd).wait()

    @pl.when(is_last)
    def _():
        for m in range(1, batch_groups):
            top_start(m)

    for kind in range(2):
        total = kv_near[0, kind].astype(wide)
        for xd in range(1, inner):
            total = total + kv_near[xd, kind].astype(wide)
        total = total.astype(low)
        for m in range(batch_groups):
            kv[m, kind] = total[m * tokens : (m + 1) * tokens]

    for m in range(batch_groups):
        ids = ids_ref[m : m + 1].astype(wide)
        mask = (to_column(ids, tokens, 0) == jnp.broadcast_to(ids, (tokens, tokens))) & (
            iota((tokens, tokens), 0) >= iota((tokens, tokens), 1)
        )
        for h in range(local_heads):
            head = slice(h * HEAD_WIDTH, (h + 1) * HEAD_WIDTH)
            scores = contract(queries[m, :, head], kv[m, 0], 1, 1) * scale
            value = jnp.exp(jnp.where(mask, scores, masked_score))
            value = value / jnp.sum(value, -1, keepdims=True)
            probs[m, h] = value
            att_ref[m * tokens : (m + 1) * tokens, head] = jnp.dot(
                value.astype(low), kv[m, 1], preferred_element_type=wide
            ).astype(low)
    loads[1].wait()
    gain_out_ref[...] = jnp.zeros_like(gain_out_ref)

    @pl.when(is_last)
    def _():
        for m in range(1, batch_groups):
            top_forward(m)

    def dkv_near_copy(m, xd):
        return near(
            dkv_near.at[m, 0], dkv_near.at[m, xd], dn_send.at[m, xd], dn_recv.at[m, xd], xd
        )

    def dkv_far_copy(m, zd):
        block = dkv_far.at[m, z]
        return far(block, block, df_send.at[m, zd], df_recv.at[m, zd], zd)

    def group(i):
        return columns(lax.rem(z + i, outer) * group_width, group_width)

    def part_near(m, i, xd):
        return near(
            part.at[m, xpeer(xd), :, :, group(i)],
            near_recv.at[m, xd - 1, :, :, group(i)],
            pn_send.at[m, xd, i - 1],
            pn_recv.at[m, xd, i - 1],
            xd,
        )

    def part_far(m, i, c, zd):
        cols = columns(c * group_width, group_width)
        return far(
            far_send.at[m, zd, :, cols],
            far_recv.at[m, zd, :, cols],
            pf_send.at[m, zd, i - 1],
            pf_recv.at[m, zd, i - 1],
            zd,
        )

    def key_copy(m, d):
        peer = lax.rem(me + d, tp_count)
        return remote(
            key_send.at[m, peer], key_recv.at[m, me], ks_send.at[m, d], ks_recv.at[m, d], sec, peer
        )

    def part_group(m, i):
        base = lax.rem(z + i, outer) * group_width

        def piece(k, carry):
            start = base + k * step_width
            cols = columns(start, step_width)
            product = contract(gq_ref[m], wq[cols, :], 1, 1)
            for block in range(tp_count):
                part[m, block % inner, block // inner, :, cols] = product[
                    block * rows : (block + 1) * rows
                ].astype(low)
            return carry

        lax.fori_loop(0, group_width // step_width, piece, 0)
        for xd in range(1, inner):
            part_near(m, i, xd).start()

    def sum_group(m, i):
        cols = group(i)
        for xd in range(1, inner):
            part_near(m, i, xd).wait()
        for zd in range(outer):
            total = part[m, x, zpeer(zd), :, cols].astype(wide)
            for xd in range(1, inner):
                total = total + near_recv[m, xd - 1, zpeer(zd), :, cols].astype(wide)
            if zd:
                far_send[m, zd, :, cols] = total.astype(low)
                part_far(m, i, lax.rem(z + i, outer), zd).start()
            else:
                far_recv[m, 0, :, cols] = total.astype(low)

    def step(m, carry):
        def forward(c):
            @pl.when(jnp.logical_not(is_last))
            def _():
                for zd in range(outer):
                    hop(m, c, zd, sec).wait_recv()
                    for xd in range(1, inner):
                        grad_near(m, c, zd, xd).start()

        forward(0)

        def upstream(c, total):
            pl.when(c + 1 < CHUNKS)(functools.partial(forward, c + 1))
            for zd in range(outer):
                for xd in range(1, inner):
                    grad_near(m, c, zd, xd).wait()
            for k in range(chunk_width // step_width):
                cols = columns(c * chunk_width + k * step_width, step_width)
                piece = jnp.concatenate(
                    [gall[m, j, :, cols].astype(wide) for j in range(tp_count)], 0
                ).astype(low)
                up_ref[m, :, cols] = piece
                total = total + contract(piece, wo[:, cols], 1, 1)
            return total

        grad_heads[...] = lax.fori_loop(
            0, CHUNKS, upstream, jnp.zeros((tokens, head_cols), wide)
        ).astype(low)
        grad_keys = jnp.zeros((tokens, HEAD_WIDTH), wide)
        grad_values = jnp.zeros((tokens, HEAD_WIDTH), wide)
        for h in range(local_heads):
            head = slice(h * HEAD_WIDTH, (h + 1) * HEAD_WIDTH)
            grad_head = grad_heads[:, head]
            prob = probs[m, h]
            grad_probs = contract(grad_head, kv[m, 1], 1, 1)
            grad_scores = prob * (grad_probs - jnp.sum(prob * grad_probs, -1, keepdims=True))
            scores_low = (grad_scores * scale).astype(low)
            gq_ref[m, :, head] = jnp.dot(
                scores_low, kv[m, 0], preferred_element_type=wide
            ).astype(low)
            grad_keys = grad_keys + contract(scores_low, queries[m, :, head], 0, 0)
            grad_values = grad_values + contract(prob.astype(low), grad_head, 0, 0)
        dkv_near[m, 0, 0] = grad_keys.astype(low)
        dkv_near[m, 0, 1] = grad_values.astype(low)
        for xd in range(1, inner):
            dkv_near_copy(m, xd).start()

        part_group(m, 1)

        for xd in range(1, inner):
            dkv_near_copy(m, xd).wait()
        for kind in range(2):
            total = dkv_near[m, 0, kind].astype(wide)
            for xd in range(1, inner):
                total = total + dkv_near[m, xd, kind].astype(wide)
            dkv_far[m, z, kind] = total.astype(low)
        for zd in range(1, outer):
            dkv_far_copy(m, zd).start()

        def middle(i, inner_carry):
            part_group(m, i)
            sum_group(m, i - 1)
            return inner_carry

        lax.fori_loop(2, outer + 1, middle, 0)

        for zd in range(1, outer):
            dkv_far_copy(m, zd).wait()
        holders = outer // key_count
        for kind in range(2):
            for k in range(key_count):
                total = dkv_far[m, k * holders, kind].astype(wide)
                for other in range(1, holders):
                    total = total + dkv_far[m, k * holders + other, kind].astype(wide)
                dkv_ref[kind, m, :, k * HEAD_WIDTH : (k + 1) * HEAD_WIDTH] = total.astype(low)
        key_slice = contract(dkv_ref[0, m], kw[...], 1, 1) + contract(
            dkv_ref[1, m], vw[...], 1, 1
        )
        for j in range(tp_count):
            key_send[m, j] = key_slice[j * rows : (j + 1) * rows].astype(low)
        for d in range(1, tp_count):
            key_copy(m, d).start()
        key_recv[m, me] = key_send[m, me]
        sum_group(m, outer)

        for zd in range(1, outer):
            for i in range(1, outer + 1):
                part_far(m, i, lax.rem(z + i, outer), zd).wait_send()
                part_far(m, i, lax.rem(z - zd + i + outer, outer), zd).wait_recv()

        for d in range(1, tp_count):
            key_copy(m, d).wait()

        dots = jnp.zeros((rows, 1), wide)
        for k in range(tp_count):
            cols = slice(k * slice_width, (k + 1) * slice_width)
            normed_grad = key_recv[m, k].astype(wide) + jnp.sum(
                far_recv[m, :, :, cols].astype(wide), 0
            )
            unit_part = unit[m, :, cols]
            gain_out_ref[:, cols] = gain_out_ref[:, cols] + jnp.sum(
                normed_grad * unit_part, 0, keepdims=True
            )
            scaled = normed_grad * gain_ref[:, cols].astype(wide)
            grad_unit[:, cols] = scaled
            dots = dots + jnp.sum(scaled * unit_part, -1, keepdims=True)
        dots = dots / width
        inv = inverse[m, :, 0:1]
        for c in range(CHUNKS):
            cols = slice(c * chunk_width, (c + 1) * chunk_width)
            gin_ref[m, :, cols] = (
                gall[m, me, :, cols].astype(wide)
                + inv * (grad_unit[:, cols] - unit[m, :, cols] * dots)
            ).astype(low)

            @pl.when(feeds)
            def _():
                for zd in range(outer):
                    hop(m, c, zd, sec - 1).start()

        return carry

    lax.fori_loop(0, batch_groups, step, 0)

    def gain_copy(d):
        return remote(
            gain_all.at[me],
            gain_all.at[me],
            t_send.at[d],
            t_recv.at[d],
            sec,
            lax.rem(me + d, tp_count),
        )

    gain_all[me] = gain_out_ref[...]
    for d in range(1, tp_count):
        gain_copy(d).start()
    for d in range(1, tp_count):
        gain_copy(d).wait()
    total = gain_all[0]
    for d in range(1, tp_count):
        total = total + gain_all[d]
    gain_out_ref[...] = total

    @pl.when(feeds)
    def _():
        for m in range(batch_groups):
            for c in range(CHUNKS):
                for zd in range(outer):
                    hop(m, c, zd, sec - 1).wait_send()


def relay(saved, gain, wq, kw, vw, wo, direction, ratio, ids, slots, counts):
    tp_count = lax.axis_size("tp")
    inner = inner_size(tp_count)
    outer = tp_count // inner
    batch_groups, rows, width = saved.shape
    tokens = rows * tp_count
    every = batch_groups * tokens
    head_cols = wq.shape[1]
    key_width = kw.shape[1]
    key_count = key_width // HEAD_WIDTH
    slice_width = kw.shape[0]
    vmem = pl.BlockSpec(memory_space=pltpu.VMEM)
    hbm = pl.BlockSpec(memory_space=pltpu.HBM)
    dma = pltpu.SemaphoreType.DMA
    groups = batch_groups
    return pl.pallas_call(
        functools.partial(relay_kernel, lax.axis_size("section"), tp_count),
        out_shape=[
            jax.ShapeDtypeStruct((groups, rows, width), low),
            jax.ShapeDtypeStruct((groups, tokens, width), low),
            jax.ShapeDtypeStruct((every, width), low),
            jax.ShapeDtypeStruct((every, slice_width), low),
            jax.ShapeDtypeStruct((every, head_cols), low),
            jax.ShapeDtypeStruct((groups, tokens, head_cols), low),
            jax.ShapeDtypeStruct((2, groups, tokens, key_width), low),
            jax.ShapeDtypeStruct((1, width), wide),
        ],
        in_specs=[vmem, vmem, hbm, vmem, vmem, hbm, vmem] + [vmem] * 4,
        out_specs=[vmem] * 8,
        scratch_shapes=[
            pltpu.VMEM(wq.shape, low),
            pltpu.VMEM(wo.shape, low),
            pltpu.VMEM((tp_count, groups, rows, width), low),
            pltpu.VMEM((groups, tp_count, rows, width), low),
            pltpu.VMEM((groups, inner, outer, rows, width), low),
            pltpu.VMEM((groups, inner - 1, outer, rows, width), low),
            pltpu.VMEM((groups, outer, rows, width), low),
            pltpu.VMEM((groups, outer, rows, width), low),
            pltpu.VMEM((groups, rows, width), wide),
            pltpu.VMEM((groups, rows, LANES), wide),
            pltpu.VMEM((rows, width), wide),
            pltpu.VMEM((groups, tokens, head_cols), low),
            pltpu.VMEM((groups, 2, tokens, HEAD_WIDTH), low),
            pltpu.VMEM((key_count, 2, every, HEAD_WIDTH), low),
            pltpu.VMEM((outer, 2, every, HEAD_WIDTH), low),
            pltpu.VMEM((inner, 2, every, HEAD_WIDTH), low),
            pltpu.VMEM((groups, head_cols // HEAD_WIDTH, tokens, tokens), wide),
            pltpu.VMEM((tokens, head_cols), low),
            pltpu.VMEM((groups, tp_count, rows, slice_width), low),
            pltpu.VMEM((groups, tp_count, rows, slice_width), low),
            pltpu.VMEM((groups, inner, 2, tokens, HEAD_WIDTH), low),
            pltpu.VMEM((groups, outer, 2, tokens, HEAD_WIDTH), low),
            pltpu.VMEM((tp_count, 8, LANES), wide),
            pltpu.VMEM((tp_count, 1, width), wide),
            dma((2,)),
            dma((tp_count,)),
            dma((tp_count,)),
            dma((CHUNKS, outer)),
            dma((CHUNKS, outer)),
            dma((CHUNKS, tp_count)),
            dma((CHUNKS, tp_count)),
            dma((groups, CHUNKS, outer)),
            dma((groups, CHUNKS, outer)),
            dma((groups, CHUNKS, tp_count)),
            dma((groups, CHUNKS, tp_count)),
            dma((groups, CHUNKS, outer)),
            dma((outer,)),
            dma((outer,)),
            dma((inner,)),
            dma((inner,)),
            dma((groups, inner)),
            dma((groups, inner)),
            dma((groups, outer)),
            dma((groups, outer)),
            dma((groups, inner, outer)),
            dma((groups, inner, outer)),
            dma((groups, outer, outer)),
            dma((groups, outer, outer)),
            dma((groups, tp_count)),
            dma((groups, tp_count)),
            dma((tp_count,)),
            dma((tp_count,)),
            pltpu.SemaphoreType.REGULAR,
        ],
        compiler_params=pltpu.CompilerParams(
            collective_id=0, has_side_effects=True, vmem_limit_bytes=VMEM_LIMIT
        ),
        name="relay",
    )(saved, gain, wq, kw, vw, wo, direction, ratio, ids, slots, counts)


def weights_kernel(
    normed_ref,
    normed_cols_ref,
    gq_ref,
    dkv_ref,
    att_ref,
    up_ref,
    grads_in,
    gain_in,
    grads_out,
    of_query,
    of_key,
    of_value,
    of_out,
    gain_out,
):
    step = pl.program_id(0)

    @pl.when(step == 0)
    def _():
        grads_out[...] = grads_in[...]
        gain_out[...] = gain_in[...]

    part, narrow = of_query.shape[0], of_key.shape[0]
    cols = pl.ds(pl.multiple_of(step * part, part), part)
    own = normed_cols_ref[:, pl.ds(pl.multiple_of(step * narrow, narrow), narrow)]
    of_query[...] = contract(normed_ref[:, cols], gq_ref[...], 0, 0).astype(low)
    of_out[...] = contract(att_ref[...], up_ref[:, cols], 0, 0).astype(low)
    of_key[...] = contract(own, dkv_ref[0], 0, 0).astype(low)
    of_value[...] = contract(own, dkv_ref[1], 0, 0).astype(low)


def weight_gradients(normed, normed_cols, grad_queries, dkv, attended, upstream, grads, gain):
    every, width = normed.shape
    head_cols = grad_queries.shape[1]
    slice_width, key_width = normed_cols.shape[1], dkv.shape[2]
    steps = slice_width // HEAD_WIDTH
    part = width // steps

    def whole(shape):
        return pl.BlockSpec(shape, lambda i: (0,) * len(shape))

    def lanes(shape):
        return pl.BlockSpec(shape, lambda i: (0, i))

    def above(shape):
        return pl.BlockSpec(shape, lambda i: (i, 0))

    return pl.pallas_call(
        weights_kernel,
        grid=(steps,),
        out_shape=[
            jax.ShapeDtypeStruct(grads.shape, low),
            jax.ShapeDtypeStruct((width, head_cols), low),
            jax.ShapeDtypeStruct((slice_width, key_width), low),
            jax.ShapeDtypeStruct((slice_width, key_width), low),
            jax.ShapeDtypeStruct((head_cols, width), low),
            jax.ShapeDtypeStruct(gain.shape, wide),
        ],
        in_specs=[pl.BlockSpec(memory_space=pltpu.VMEM)] * 8,
        out_specs=[
            whole(grads.shape),
            above((part, head_cols)),
            above((HEAD_WIDTH, key_width)),
            above((HEAD_WIDTH, key_width)),
            lanes((head_cols, part)),
            whole(gain.shape),
        ],
        compiler_params=pltpu.CompilerParams(vmem_limit_bytes=32 * 1024 * 1024),
        name="weight_gradients",
    )(normed, normed_cols, grad_queries, dkv, attended, upstream, grads, gain)


def body(
    section_inputs,
    norm_gain,
    w_query,
    key_projection,
    value_projection,
    w_out,
    token_dir,
    tok_logratio,
    segment_ids,
    pair_of_slot,
    pair_counts,
):
    saved = section_inputs[0]
    width = saved.shape[2]
    every = segment_ids.size
    grads, upstream, normed, normed_cols, attended, grad_queries, dkv, gain_total = relay(
        saved,
        norm_gain[0].reshape(1, width),
        w_query[0],
        key_projection[0],
        value_projection[0],
        w_out[0],
        token_dir,
        tok_logratio,
        segment_ids,
        pair_of_slot,
        pair_counts,
    )
    grads, of_query, of_key, of_value, of_out, gain_total = weight_gradients(
        normed,
        normed_cols,
        grad_queries.reshape(every, -1),
        dkv.reshape(2, every, -1),
        attended,
        upstream.reshape(every, width),
        grads,
        gain_total,
    )
    return (
        grads[None],
        of_query[None],
        of_key[None],
        of_value[None],
        of_out[None],
        gain_total,
    )


def solution(mesh):
    placed = (
        P("section", None, "tp", None),
        P("section", None),
        P("section", None, "tp"),
        P("section", "tp", None),
        P("section", "tp", None),
        P("section", "tp", None),
        P(None, "tp", None),
        P(None, "tp"),
        P(),
        P(),
        P(),
    )
    return jax.shard_map(
        body,
        mesh=mesh,
        in_specs=placed,
        out_specs=(
            P("section", None, "tp", None),
            P("section", None, "tp"),
            P("section", "tp", None),
            P("section", "tp", None),
            P("section", "tp", None),
            P("section", None),
        ),
        check_vma=False,
    )
```

```python
import functools
import math

import jax
import jax.numpy as jnp
from jax import lax
from jax.experimental import pallas as pl
from jax.experimental.pallas import tpu as pltpu
from jax.sharding import PartitionSpec as P

HEAD_WIDTH = 128
SLOTS = 4
LANES = 128
CHUNKS = 4

norm_epsilon = 1e-05
pair_beta = 4.0
masked_score = -1e30

MESH = pl.DeviceIdType.MESH
VMEM_LIMIT = 56 * 1024 * 1024
low, wide = jnp.bfloat16, jnp.float32


def contract(left, right, left_dim, right_dim):
    return lax.dot_general(
        left, right, (((left_dim,), (right_dim,)), ((), ())), preferred_element_type=wide
    )


def inner_size(tp_count):
    inner = 1
    while 2 * (2 * inner) ** 2 <= tp_count:
        inner *= 2
    return inner


def relay_kernel(
    section_count,
    tp_count,
    saved_hbm,
    gain_ref,
    wq_hbm,
    kw_hbm,
    vw_hbm,
    wo_hbm,
    dir_hbm,
    ratio_ref,
    ids_ref,
    slot_ref,
    counts_ref,
    gin_ref,
    up_hbm,
    normed_hbm,
    normed_cols_ref,
    att_ref,
    gq_ref,
    dkv_ref,
    gain_out_ref,
    saved_ref,
    dir_ref,
    kw,
    vw,
    wq,
    wo,
    up_ref,
    normed_ref,
    nall,
    top,
    gall,
    part,
    near_recv,
    far_send,
    far_recv,
    unit,
    inverse,
    grad_unit,
    queries,
    kv,
    kv_part,
    kv_far,
    kv_near,
    probs,
    grad_heads,
    key_send,
    key_recv,
    dkv_near,
    dkv_far,
    sums_all,
    gain_all,
    w_sem,
    o_sem,
    s_send,
    s_recv,
    nf_send,
    nf_recv,
    nn_send,
    nn_recv,
    tf_send,
    tf_recv,
    tn_send,
    tn_recv,
    ty_send,
    ty_recv,
    gf_recv,
    gn_send,
    gn_recv,
    hop_send,
    kf_send,
    kf_recv,
    kn_send,
    kn_recv,
    dn_send,
    dn_recv,
    df_send,
    df_recv,
    pn_send,
    pn_recv,
    pf_send,
    pf_recv,
    ks_send,
    ks_recv,
    t_send,
    t_recv,
    go,
):
    sec = lax.axis_index("section")
    me = lax.axis_index("tp")
    inner = inner_size(tp_count)
    outer = tp_count // inner
    z, x = me // inner, lax.rem(me, inner)
    batch_groups, rows, width = saved_ref.shape
    tokens = rows * tp_count
    every = batch_groups * tokens
    head_cols = wq.shape[1]
    local_heads = head_cols // HEAD_WIDTH
    slice_width, key_width = kw.shape
    key_count = key_width // HEAD_WIDTH
    sharers = tp_count // key_count
    group_width = inner * slice_width
    step_width = min(2048, group_width)
    merge_width = min(1024, width)
    chunk_width = width // CHUNKS
    per_group = CHUNKS // batch_groups
    normed_width = width // per_group
    scale = 1.0 / math.sqrt(HEAD_WIDTH)
    is_last = sec == section_count - 1
    feeds = sec > 0
    helps = sec == section_count - 3

    def zpeer(zd):
        return lax.rem(z + zd, outer)

    def xpeer(xd):
        return lax.rem(x + xd, inner)

    def remote(source, target, send, receive, section, index):
        return pltpu.make_async_remote_copy(
            src_ref=source,
            dst_ref=target,
            send_sem=send,
            recv_sem=receive,
            device_id=(section, index),
            device_id_type=MESH,
        )

    def far(source, target, send, receive, zd):
        return remote(source, target, send, receive, sec, zpeer(zd) * inner + x)

    def near(source, target, send, receive, xd):
        return remote(source, target, send, receive, sec, z * inner + xpeer(xd))

    def columns(start, size):
        return pl.ds(pl.multiple_of(start, HEAD_WIDTH), size)

    loads = [
        pltpu.make_async_copy(source, target, w_sem.at[i])
        for i, (source, target) in enumerate(
            (
                (saved_hbm, saved_ref),
                (dir_hbm, dir_ref),
                (kw_hbm, kw),
                (vw_hbm, vw),
                (wq_hbm, wq),
                (wo_hbm, wo),
            )
        )
    ]
    for load in loads:
        load.start()

    barrier = pltpu.get_barrier_semaphore()
    for d in range(1, tp_count):
        pl.semaphore_signal(
            barrier, inc=1, device_id=(sec, lax.rem(me + d, tp_count)), device_id_type=MESH
        )

    @pl.when(sec < section_count - 1)
    def _():
        for zd in range(outer):
            pl.semaphore_signal(
                barrier, inc=1, device_id=(sec + 1, zpeer(zd) * inner + x), device_id_type=MESH
            )

    @pl.when(is_last)
    def _():
        pl.semaphore_signal(barrier, inc=1, device_id=(sec - 2, me), device_id_type=MESH)

    loads[0].wait()
    gain_row = gain_ref[...].astype(wide)
    for m in range(batch_groups):
        rows_in = saved_ref[m].astype(wide)
        inv = lax.rsqrt(jnp.mean(rows_in * rows_in, -1, keepdims=True) + norm_epsilon)
        inverse[m] = jnp.broadcast_to(inv, (rows, LANES))
        unit_rows = rows_in * inv
        unit[m] = unit_rows
        nall[me, m] = (unit_rows * gain_row).astype(low)

    @pl.when(helps)
    def _():
        pl.semaphore_wait(barrier, tp_count + outer)

    @pl.when(feeds & jnp.logical_not(helps))
    def _():
        pl.semaphore_wait(barrier, tp_count - 1 + outer)

    @pl.when(jnp.logical_not(feeds))
    def _():
        pl.semaphore_wait(barrier, tp_count - 1)

    def iota(shape, dim):
        return lax.broadcasted_iota(jnp.int32, shape, dim)

    def to_column(row, count, start):
        span = row.shape[1]
        pick = iota((count, span), 1) == iota((count, span), 0) + start
        return jnp.sum(jnp.where(pick, jnp.broadcast_to(row, (count, span)), 0.0), -1, keepdims=True)

    def own_member(m, kind):
        own = to_column(ids_ref[m : m + 1].astype(wide), rows, me * rows)
        slot = 2 * iota((rows, SLOTS), 1) + kind
        return (own == slot.astype(wide)).astype(wide)

    def slot_counts(m, kind):
        pairs = counts_ref.shape[0]
        table = iota((pairs, SLOTS), 0) == jnp.broadcast_to(slot_ref[m : m + 1], (pairs, SLOTS))
        count = counts_ref[:, kind : kind + 1].astype(wide)
        return jnp.sum(jnp.where(table, count, 0.0), 0, keepdims=True)

    def sums_copy(d):
        return remote(
            sums_all.at[me], sums_all.at[me], s_send.at[d], s_recv.at[d], sec, lax.rem(me + d, tp_count)
        )

    def block_from(zd):
        return lax.rem(z - zd + outer, outer) * inner + x

    def normed_piece(block, c):
        start = c % per_group * normed_width
        return nall.at[block, c // per_group, :, start : start + normed_width]

    def normed_far(c, zd):
        block = normed_piece(me, c)
        return far(block, block, nf_send.at[c, zd], nf_recv.at[c, zd], zd)

    def normed_near(c, zd, xd):
        block = normed_piece(block_from(zd), c)
        slot = zd * inner + xd
        return near(block, block, nn_send.at[c, slot], nn_recv.at[c, slot], xd)

    def chunk(c):
        return columns(c * chunk_width, chunk_width)

    def top_far(m, c, zd):
        block = top.at[m, me, :, chunk(c)]
        return far(block, block, tf_send.at[m, c, zd], tf_recv.at[m, c, zd], zd)

    def top_near(m, c, zd, xd):
        block = top.at[m, block_from(zd), :, chunk(c)]
        slot = zd * inner + xd
        return near(block, block, tn_send.at[m, c, slot], tn_recv.at[m, c, slot], xd)

    def top_move(m, c, section):
        return remote(
            top.at[m, :, :, chunk(c)],
            gall.at[m, :, :, chunk(c)],
            ty_send.at[m, c],
            ty_recv.at[m, c],
            section,
            me,
        )

    def hop(m, c, zd, section):
        return remote(
            gin_ref.at[m, :, chunk(c)],
            gall.at[m, me, :, chunk(c)],
            hop_send.at[m, c, zd],
            gf_recv.at[m, c, zd],
            section,
            zpeer(zd) * inner + x,
        )

    def grad_near(m, c, zd, xd):
        block = gall.at[m, block_from(zd), :, chunk(c)]
        slot = zd * inner + xd
        return near(block, block, gn_send.at[m, c, slot], gn_recv.at[m, c, slot], xd)

    loads[1].wait()

    @pl.when(helps)
    def _():
        sums_all[me] = jnp.zeros(sums_all.shape[1:], wide)
        for m in range(batch_groups):
            ratio = to_column(ratio_ref[m : m + 1], rows, 0)
            for kind in range(2):
                sums_all[me, 2 * m + kind : 2 * m + kind + 1, 0:SLOTS] = jnp.sum(
                    own_member(m, kind) * ratio, 0, keepdims=True
                )
        for d in range(1, tp_count):
            sums_copy(d).start()

    @pl.when(helps)
    def _():
        for d in range(1, tp_count):
            sums_copy(d).wait()
        total = sums_all[0]
        for d in range(1, tp_count):
            total = total + sums_all[d]
        for m in range(batch_groups):
            chosen, rejected = slot_counts(m, 0), slot_counts(m, 1)
            margin = pair_beta * (
                total[2 * m : 2 * m + 1, 0:SLOTS] / chosen
                - total[2 * m + 1 : 2 * m + 2, 0:SLOTS] / rejected
            )
            weight = pair_beta * jax.nn.sigmoid(-margin)
            token_weight = jnp.sum(
                own_member(m, 0) * (-weight / chosen) + own_member(m, 1) * (weight / rejected),
                -1,
                keepdims=True,
            )
            top[m, me] = (token_weight * dir_ref[m].astype(wide)).astype(low)
            for c in range(CHUNKS):
                for zd in range(1, outer):
                    top_far(m, c, zd).start()
                for xd in range(1, inner):
                    top_near(m, c, 0, xd).start()

    @pl.when(helps)
    def _():
        order = [(m, c) for m in range(batch_groups) for c in range(CHUNKS)]

        def top_forward(m, c):
            for zd in range(1, outer):
                top_far(m, c, zd).wait()
                for xd in range(1, inner):
                    top_near(m, c, zd, xd).start()

        top_forward(*order[0])
        for at, (m, c) in enumerate(order):
            if at + 1 < len(order):
                top_forward(*order[at + 1])
            for zd in range(outer):
                for xd in range(1, inner):
                    top_near(m, c, zd, xd).wait()
            top_move(m, c, sec + 2).start()

        @pl.when(feeds)
        def _():
            pl.semaphore_signal(go, inc=1, device_id=(sec - 1, me), device_id_type=MESH)

    @pl.when((sec == section_count - 2) | (sec == section_count - 4))
    def _():
        pl.semaphore_wait(go, 1)

    for c in range(CHUNKS):
        for zd in range(1, outer):
            normed_far(c, zd).start()
        for xd in range(1, inner):
            normed_near(c, 0, xd).start()

    for c in range(CHUNKS):
        for zd in range(1, outer):
            normed_far(c, zd).wait()
            for xd in range(1, inner):
                normed_near(c, zd, xd).start()
    for c in range(CHUNKS):
        for zd in range(outer):
            for xd in range(1, inner):
                normed_near(c, zd, xd).wait()

    @pl.when(is_last)
    def _():
        pl.semaphore_signal(go, inc=1, device_id=(sec - 1, me), device_id_type=MESH)

    def merge(k, carry):
        cols = columns(k * merge_width, merge_width)
        for m in range(batch_groups):
            normed_ref[m * tokens : (m + 1) * tokens, cols] = jnp.concatenate(
                [nall[j, m, :, cols].astype(wide) for j in range(tp_count)], 0
            ).astype(low)
        return carry

    lax.fori_loop(0, width // merge_width, merge, 0)
    normed_out = pltpu.make_async_copy(normed_ref, normed_hbm, o_sem.at[0])
    normed_out.start()

    def up_out(m):
        return pltpu.make_async_copy(up_ref.at[m], up_hbm.at[m], o_sem.at[1 + m])

    normed_cols_ref[...] = normed_ref[:, columns(me * slice_width, slice_width)]
    loads[2].wait()
    loads[3].wait()
    for kind, weight_ref in enumerate((kw, vw)):
        product = jnp.dot(normed_cols_ref[...], weight_ref[...], preferred_element_type=wide)
        for k in range(key_count):
            kv_part[k, kind] = product[:, k * HEAD_WIDTH : (k + 1) * HEAD_WIDTH].astype(low)

    def kv_far_copy(zd):
        head = zpeer(zd) * inner // sharers
        return far(kv_part.at[head], kv_far.at[zd], kf_send.at[zd], kf_recv.at[zd], zd)

    def kv_near_copy(xd):
        return near(kv_near.at[0], kv_near.at[xd], kn_send.at[xd], kn_recv.at[xd], xd)

    for zd in range(1, outer):
        kv_far_copy(zd).start()

    loads[4].wait()

    def project(k, total):
        cols = columns(k * step_width, step_width)
        return total + jnp.dot(normed_ref[:, cols], wq[cols, :], preferred_element_type=wide)

    product = lax.fori_loop(
        0, width // step_width, project, jnp.zeros((every, head_cols), wide)
    ).astype(low)
    for m in range(batch_groups):
        queries[m] = product[m * tokens : (m + 1) * tokens]

    for zd in range(1, outer):
        kv_far_copy(zd).wait()
    for kind in range(2):
        total = kv_part[z * inner // sharers, kind].astype(wide)
        for zd in range(1, outer):
            total = total + kv_far[zd, kind].astype(wide)
        kv_near[0, kind] = total.astype(low)
    for xd in range(1, inner):
        kv_near_copy(xd).start()
    for xd in range(1, inner):
        kv_near_copy(xd).wait()
    for kind in range(2):
        total = kv_near[0, kind].astype(wide)
        for xd in range(1, inner):
            total = total + kv_near[xd, kind].astype(wide)
        total = total.astype(low)
        for m in range(batch_groups):
            kv[m, kind] = total[m * tokens : (m + 1) * tokens]

    for m in range(batch_groups):
        ids = ids_ref[m : m + 1].astype(wide)
        mask = (to_column(ids, tokens, 0) == jnp.broadcast_to(ids, (tokens, tokens))) & (
            iota((tokens, tokens), 0) >= iota((tokens, tokens), 1)
        )
        for h in range(local_heads):
            head = slice(h * HEAD_WIDTH, (h + 1) * HEAD_WIDTH)
            scores = contract(queries[m, :, head], kv[m, 0], 1, 1) * scale
            value = jnp.exp(jnp.where(mask, scores, masked_score))
            value = value / jnp.sum(value, -1, keepdims=True)
            probs[m, h] = value
            att_ref[m * tokens : (m + 1) * tokens, head] = jnp.dot(
                value.astype(low), kv[m, 1], preferred_element_type=wide
            ).astype(low)
    loads[5].wait()
    gain_out_ref[...] = jnp.zeros_like(gain_out_ref)

    def dkv_near_copy(m, xd):
        return near(
            dkv_near.at[m, 0], dkv_near.at[m, xd], dn_send.at[m, xd], dn_recv.at[m, xd], xd
        )

    def dkv_far_copy(m, zd):
        block = dkv_far.at[m, z]
        return far(block, block, df_send.at[m, zd], df_recv.at[m, zd], zd)

    def group(i):
        return columns(lax.rem(z + i, outer) * group_width, group_width)

    def part_near(m, i, xd):
        return near(
            part.at[m, xpeer(xd), :, :, group(i)],
            near_recv.at[m, xd - 1, :, :, group(i)],
            pn_send.at[m, xd, i - 1],
            pn_recv.at[m, xd, i - 1],
            xd,
        )

    def part_far(m, i, c, zd):
        cols = columns(c * group_width, group_width)
        return far(
            far_send.at[m, zd, :, cols],
            far_recv.at[m, zd, :, cols],
            pf_send.at[m, zd, i - 1],
            pf_recv.at[m, zd, i - 1],
            zd,
        )

    def key_copy(m, d):
        peer = lax.rem(me + d, tp_count)
        return remote(
            key_send.at[m, peer], key_recv.at[m, me], ks_send.at[m, d], ks_recv.at[m, d], sec, peer
        )

    def part_group(m, i):
        base = lax.rem(z + i, outer) * group_width

        def piece(k, carry):
            start = base + k * step_width
            cols = columns(start, step_width)
            product = contract(gq_ref[m], wq[cols, :], 1, 1)
            for block in range(tp_count):
                part[m, block % inner, block // inner, :, cols] = product[
                    block * rows : (block + 1) * rows
                ].astype(low)
            return carry

        lax.fori_loop(0, group_width // step_width, piece, 0)
        for xd in range(1, inner):
            part_near(m, i, xd).start()

    def sum_group(m, i):
        cols = group(i)
        for xd in range(1, inner):
            part_near(m, i, xd).wait()
        for zd in range(outer):
            total = part[m, x, zpeer(zd), :, cols].astype(wide)
            for xd in range(1, inner):
                total = total + near_recv[m, xd - 1, zpeer(zd), :, cols].astype(wide)
            if zd:
                far_send[m, zd, :, cols] = total.astype(low)
                part_far(m, i, lax.rem(z + i, outer), zd).start()
            else:
                far_recv[m, 0, :, cols] = total.astype(low)

    def begin(m):
        def forward(c):
            @pl.when(jnp.logical_not(is_last))
            def _():
                for zd in range(outer):
                    hop(m, c, zd, sec).wait_recv()
                    for xd in range(1, inner):
                        grad_near(m, c, zd, xd).start()

        forward(0)

        def upstream(c, total):
            pl.when(c + 1 < CHUNKS)(functools.partial(forward, c + 1))

            @pl.when(is_last)
            def _():
                top_move(m, c, sec).wait_recv()

            @pl.when(jnp.logical_not(is_last))
            def _():
                for zd in range(outer):
                    for xd in range(1, inner):
                        grad_near(m, c, zd, xd).wait()

            for k in range(chunk_width // step_width):
                cols = columns(c * chunk_width + k * step_width, step_width)
                piece = jnp.concatenate(
                    [gall[m, j, :, cols].astype(wide) for j in range(tp_count)], 0
                ).astype(low)
                up_ref[m, :, cols] = piece
                total = total + contract(piece, wo[:, cols], 1, 1)
            return total

        grad_heads[...] = lax.fori_loop(
            0, CHUNKS, upstream, jnp.zeros((tokens, head_cols), wide)
        ).astype(low)
        up_out(m).start()
        grad_keys = jnp.zeros((tokens, HEAD_WIDTH), wide)
        grad_values = jnp.zeros((tokens, HEAD_WIDTH), wide)
        for h in range(local_heads):
            head = slice(h * HEAD_WIDTH, (h + 1) * HEAD_WIDTH)
            grad_head = grad_heads[:, head]
            prob = probs[m, h]
            grad_probs = contract(grad_head, kv[m, 1], 1, 1)
            grad_scores = prob * (grad_probs - jnp.sum(prob * grad_probs, -1, keepdims=True))
            scores_low = (grad_scores * scale).astype(low)
            gq_ref[m, :, head] = jnp.dot(
                scores_low, kv[m, 0], preferred_element_type=wide
            ).astype(low)
            grad_keys = grad_keys + contract(scores_low, queries[m, :, head], 0, 0)
            grad_values = grad_values + contract(prob.astype(low), grad_head, 0, 0)
        dkv_near[m, 0, 0] = grad_keys.astype(low)
        dkv_near[m, 0, 1] = grad_values.astype(low)
        for xd in range(1, inner):
            dkv_near_copy(m, xd).start()

    def spread(m):
        part_group(m, 1)

        for xd in range(1, inner):
            dkv_near_copy(m, xd).wait()
        for kind in range(2):
            total = dkv_near[m, 0, kind].astype(wide)
            for xd in range(1, inner):
                total = total + dkv_near[m, xd, kind].astype(wide)
            dkv_far[m, z, kind] = total.astype(low)
        for zd in range(1, outer):
            dkv_far_copy(m, zd).start()

        def middle(i, inner_carry):
            part_group(m, i)
            sum_group(m, i - 1)
            return inner_carry

        lax.fori_loop(2, outer + 1, middle, 0)

        for zd in range(1, outer):
            dkv_far_copy(m, zd).wait()
        holders = outer // key_count
        for kind in range(2):
            for k in range(key_count):
                total = dkv_far[m, k * holders, kind].astype(wide)
                for other in range(1, holders):
                    total = total + dkv_far[m, k * holders + other, kind].astype(wide)
                dkv_ref[kind, m, :, k * HEAD_WIDTH : (k + 1) * HEAD_WIDTH] = total.astype(low)
        key_slice = contract(dkv_ref[0, m], kw[...], 1, 1) + contract(
            dkv_ref[1, m], vw[...], 1, 1
        )
        for j in range(tp_count):
            key_send[m, j] = key_slice[j * rows : (j + 1) * rows].astype(low)
        for d in range(1, tp_count):
            key_copy(m, d).start()
        key_recv[m, me] = key_send[m, me]
        sum_group(m, outer)

    def finish(m):
        for zd in range(1, outer):
            for i in range(1, outer + 1):
                part_far(m, i, lax.rem(z + i, outer), zd).wait_send()
                part_far(m, i, lax.rem(z - zd + i + outer, outer), zd).wait_recv()

        for d in range(1, tp_count):
            key_copy(m, d).wait()

        dots = jnp.zeros((rows, 1), wide)
        for k in range(tp_count):
            cols = slice(k * slice_width, (k + 1) * slice_width)
            normed_grad = key_recv[m, k].astype(wide) + jnp.sum(
                far_recv[m, :, :, cols].astype(wide), 0
            )
            unit_part = unit[m, :, cols]
            gain_out_ref[:, cols] = gain_out_ref[:, cols] + jnp.sum(
                normed_grad * unit_part, 0, keepdims=True
            )
            scaled = normed_grad * gain_ref[:, cols].astype(wide)
            grad_unit[:, cols] = scaled
            dots = dots + jnp.sum(scaled * unit_part, -1, keepdims=True)
        dots = dots / width
        inv = inverse[m, :, 0:1]
        for c in range(CHUNKS):
            cols = slice(c * chunk_width, (c + 1) * chunk_width)
            gin_ref[m, :, cols] = (
                gall[m, me, :, cols].astype(wide)
                + inv * (grad_unit[:, cols] - unit[m, :, cols] * dots)
            ).astype(low)

            @pl.when(feeds)
            def _():
                for zd in range(outer):
                    hop(m, c, zd, sec - 1).start()

    begin(0)
    for m in range(batch_groups):
        spread(m)
        if m + 1 < batch_groups:
            pl.when(is_last)(functools.partial(begin, m + 1))
        finish(m)
        if m + 1 < batch_groups:
            pl.when(jnp.logical_not(is_last))(functools.partial(begin, m + 1))

    def gain_copy(d):
        return remote(
            gain_all.at[me],
            gain_all.at[me],
            t_send.at[d],
            t_recv.at[d],
            sec,
            lax.rem(me + d, tp_count),
        )

    gain_all[me] = gain_out_ref[...]
    for d in range(1, tp_count):
        gain_copy(d).start()
    for d in range(1, tp_count):
        gain_copy(d).wait()
    total = gain_all[0]
    for d in range(1, tp_count):
        total = total + gain_all[d]
    gain_out_ref[...] = total
    normed_out.wait()
    for m in range(batch_groups):
        up_out(m).wait()

    @pl.when(helps)
    def _():
        for m in range(batch_groups):
            for c in range(CHUNKS):
                top_move(m, c, sec + 2).wait_send()

    @pl.when(feeds)
    def _():
        for m in range(batch_groups):
            for c in range(CHUNKS):
                for zd in range(outer):
                    hop(m, c, zd, sec - 1).wait_send()


def relay(saved, gain, wq, kw, vw, wo, direction, ratio, ids, slots, counts):
    tp_count = lax.axis_size("tp")
    inner = inner_size(tp_count)
    outer = tp_count // inner
    batch_groups, rows, width = saved.shape
    tokens = rows * tp_count
    every = batch_groups * tokens
    head_cols = wq.shape[1]
    key_width = kw.shape[1]
    key_count = key_width // HEAD_WIDTH
    slice_width = kw.shape[0]
    vmem = pl.BlockSpec(memory_space=pltpu.VMEM)
    hbm = pl.BlockSpec(memory_space=pltpu.HBM)
    dma = pltpu.SemaphoreType.DMA
    groups = batch_groups
    return pl.pallas_call(
        functools.partial(relay_kernel, lax.axis_size("section"), tp_count),
        out_shape=[
            jax.ShapeDtypeStruct((groups, rows, width), low),
            jax.ShapeDtypeStruct((groups, tokens, width), low),
            jax.ShapeDtypeStruct((every, width), low),
            jax.ShapeDtypeStruct((every, slice_width), low),
            jax.ShapeDtypeStruct((every, head_cols), low),
            jax.ShapeDtypeStruct((groups, tokens, head_cols), low),
            jax.ShapeDtypeStruct((2, groups, tokens, key_width), low),
            jax.ShapeDtypeStruct((1, width), wide),
        ],
        in_specs=[hbm, vmem, hbm, hbm, hbm, hbm, hbm] + [vmem] * 4,
        out_specs=[vmem, hbm, hbm] + [vmem] * 5,
        scratch_shapes=[
            pltpu.VMEM(saved.shape, low),
            pltpu.VMEM(direction.shape, low),
            pltpu.VMEM(kw.shape, low),
            pltpu.VMEM(vw.shape, low),
            pltpu.VMEM(wq.shape, low),
            pltpu.VMEM(wo.shape, low),
            pltpu.VMEM((groups, tokens, width), low),
            pltpu.VMEM((every, width), low),
            pltpu.VMEM((tp_count, groups, rows, width), low),
            pltpu.VMEM((groups, tp_count, rows, width), low),
            pltpu.VMEM((groups, tp_count, rows, width), low),
            pltpu.VMEM((groups, inner, outer, rows, width), low),
            pltpu.VMEM((groups, inner - 1, outer, rows, width), low),
            pltpu.VMEM((groups, outer, rows, width), low),
            pltpu.VMEM((groups, outer, rows, width), low),
            pltpu.VMEM((groups, rows, width), wide),
            pltpu.VMEM((groups, rows, LANES), wide),
            pltpu.VMEM((rows, width), wide),
            pltpu.VMEM((groups, tokens, head_cols), low),
            pltpu.VMEM((groups, 2, tokens, HEAD_WIDTH), low),
            pltpu.VMEM((key_count, 2, every, HEAD_WIDTH), low),
            pltpu.VMEM((outer, 2, every, HEAD_WIDTH), low),
            pltpu.VMEM((inner, 2, every, HEAD_WIDTH), low),
            pltpu.VMEM((groups, head_cols // HEAD_WIDTH, tokens, tokens), wide),
            pltpu.VMEM((tokens, head_cols), low),
            pltpu.VMEM((groups, tp_count, rows, slice_width), low),
            pltpu.VMEM((groups, tp_count, rows, slice_width), low),
            pltpu.VMEM((groups, inner, 2, tokens, HEAD_WIDTH), low),
            pltpu.VMEM((groups, outer, 2, tokens, HEAD_WIDTH), low),
            pltpu.VMEM((tp_count, 8, LANES), wide),
            pltpu.VMEM((tp_count, 1, width), wide),
            dma((6,)),
            dma((1 + groups,)),
            dma((tp_count,)),
            dma((tp_count,)),
            dma((CHUNKS, outer)),
            dma((CHUNKS, outer)),
            dma((CHUNKS, tp_count)),
            dma((CHUNKS, tp_count)),
            dma((groups, CHUNKS, outer)),
            dma((groups, CHUNKS, outer)),
            dma((groups, CHUNKS, tp_count)),
            dma((groups, CHUNKS, tp_count)),
            dma((groups, CHUNKS)),
            dma((groups, CHUNKS)),
            dma((groups, CHUNKS, outer)),
            dma((groups, CHUNKS, tp_count)),
            dma((groups, CHUNKS, tp_count)),
            dma((groups, CHUNKS, outer)),
            dma((outer,)),
            dma((outer,)),
            dma((inner,)),
            dma((inner,)),
            dma((groups, inner)),
            dma((groups, inner)),
            dma((groups, outer)),
            dma((groups, outer)),
            dma((groups, inner, outer)),
            dma((groups, inner, outer)),
            dma((groups, outer, outer)),
            dma((groups, outer, outer)),
            dma((groups, tp_count)),
            dma((groups, tp_count)),
            dma((tp_count,)),
            dma((tp_count,)),
            pltpu.SemaphoreType.REGULAR,
        ],
        compiler_params=pltpu.CompilerParams(
            collective_id=0, has_side_effects=True, vmem_limit_bytes=VMEM_LIMIT
        ),
        name="relay",
    )(saved, gain, wq, kw, vw, wo, direction, ratio, ids, slots, counts)


def weights_kernel(
    normed_ref,
    normed_cols_ref,
    gq_ref,
    dkv_ref,
    att_ref,
    up_ref,
    grads_in,
    gain_in,
    grads_out,
    of_query,
    of_key,
    of_value,
    of_out,
    gain_out,
):
    step = pl.program_id(0)

    @pl.when(step == 0)
    def _():
        grads_out[...] = grads_in[...]
        gain_out[...] = gain_in[...]

    narrow = of_key.shape[0]
    own = normed_cols_ref[:, pl.ds(pl.multiple_of(step * narrow, narrow), narrow)]
    of_query[...] = contract(normed_ref[...], gq_ref[...], 0, 0).astype(low)
    of_out[...] = contract(att_ref[...], up_ref[...], 0, 0).astype(low)
    of_key[...] = contract(own, dkv_ref[0], 0, 0).astype(low)
    of_value[...] = contract(own, dkv_ref[1], 0, 0).astype(low)


def weight_gradients(normed, normed_cols, grad_queries, dkv, attended, upstream, grads, gain):
    every, width = normed.shape
    head_cols = grad_queries.shape[1]
    slice_width, key_width = normed_cols.shape[1], dkv.shape[2]
    steps = slice_width // HEAD_WIDTH
    part = width // steps

    def whole(shape):
        return pl.BlockSpec(shape, lambda i: (0,) * len(shape))

    def lanes(shape):
        return pl.BlockSpec(shape, lambda i: (0, i))

    def above(shape):
        return pl.BlockSpec(shape, lambda i: (i, 0))

    return pl.pallas_call(
        weights_kernel,
        grid=(steps,),
        out_shape=[
            jax.ShapeDtypeStruct(grads.shape, low),
            jax.ShapeDtypeStruct((width, head_cols), low),
            jax.ShapeDtypeStruct((slice_width, key_width), low),
            jax.ShapeDtypeStruct((slice_width, key_width), low),
            jax.ShapeDtypeStruct((head_cols, width), low),
            jax.ShapeDtypeStruct(gain.shape, wide),
        ],
        in_specs=[
            lanes((every, part)),
            whole(normed_cols.shape),
            whole(grad_queries.shape),
            whole(dkv.shape),
            whole(attended.shape),
            lanes((every, part)),
            whole(grads.shape),
            whole(gain.shape),
        ],
        out_specs=[
            whole(grads.shape),
            above((part, head_cols)),
            above((HEAD_WIDTH, key_width)),
            above((HEAD_WIDTH, key_width)),
            lanes((head_cols, part)),
            whole(gain.shape),
        ],
        compiler_params=pltpu.CompilerParams(vmem_limit_bytes=VMEM_LIMIT),
        name="weight_gradients",
    )(normed, normed_cols, grad_queries, dkv, attended, upstream, grads, gain)


def body(
    section_inputs,
    norm_gain,
    w_query,
    key_projection,
    value_projection,
    w_out,
    token_dir,
    tok_logratio,
    segment_ids,
    pair_of_slot,
    pair_counts,
):
    saved = section_inputs[0]
    width = saved.shape[2]
    every = segment_ids.size
    grads, upstream, normed, normed_cols, attended, grad_queries, dkv, gain_total = relay(
        saved,
        norm_gain[0].reshape(1, width),
        w_query[0],
        key_projection[0],
        value_projection[0],
        w_out[0],
        token_dir,
        tok_logratio,
        segment_ids,
        pair_of_slot,
        pair_counts,
    )
    grads, of_query, of_key, of_value, of_out, gain_total = weight_gradients(
        normed,
        normed_cols,
        grad_queries.reshape(every, -1),
        dkv.reshape(2, every, -1),
        attended,
        upstream.reshape(every, width),
        grads,
        gain_total,
    )
    return (
        grads[None],
        of_query[None],
        of_key[None],
        of_value[None],
        of_out[None],
        gain_total,
    )


def solution(mesh):
    placed = (
        P("section", None, "tp", None),
        P("section", None),
        P("section", None, "tp"),
        P("section", "tp", None),
        P("section", "tp", None),
        P("section", "tp", None),
        P(None, "tp", None),
        P(None, "tp"),
        P(),
        P(),
        P(),
    )
    return jax.shard_map(
        body,
        mesh=mesh,
        in_specs=placed,
        out_specs=(
            P("section", None, "tp", None),
            P("section", None, "tp"),
            P("section", "tp", None),
            P("section", "tp", None),
            P("section", "tp", None),
            P("section", None),
        ),
        check_vma=False,
    )
```

```python
import functools
import math

import jax
import jax.numpy as jnp
from jax import lax
from jax.experimental import pallas as pl
from jax.experimental.pallas import tpu as pltpu
from jax.sharding import PartitionSpec as P

HEAD_WIDTH = 128
SLOTS = 4
LANES = 128
CHUNKS = 4

norm_epsilon = 1e-05
pair_beta = 4.0
masked_score = -1e30

MESH = pl.DeviceIdType.MESH
VMEM_LIMIT = 56 * 1024 * 1024
low, wide = jnp.bfloat16, jnp.float32


def contract(left, right, left_dim, right_dim):
    return lax.dot_general(
        left, right, (((left_dim,), (right_dim,)), ((), ())), preferred_element_type=wide
    )


def inner_size(tp_count):
    inner = 1
    while 2 * (2 * inner) ** 2 <= tp_count:
        inner *= 2
    return inner


def relay_kernel(
    section_count,
    tp_count,
    saved_hbm,
    gain_ref,
    wq_hbm,
    kw_hbm,
    vw_hbm,
    wo_hbm,
    dir_hbm,
    ratio_ref,
    ids_ref,
    slot_ref,
    counts_ref,
    gin_ref,
    up_hbm,
    normed_hbm,
    normed_cols_ref,
    att_ref,
    gq_ref,
    dkv_ref,
    gain_out_ref,
    saved_ref,
    dir_ref,
    kw,
    vw,
    wq,
    wo,
    up_ref,
    normed_ref,
    nall,
    top,
    gall,
    part,
    near_recv,
    far_send,
    far_recv,
    unit,
    inverse,
    grad_unit,
    queries,
    kv,
    kv_part,
    kv_far,
    kv_near,
    probs,
    grad_heads,
    key_send,
    key_recv,
    dkv_near,
    dkv_far,
    sums_all,
    gain_all,
    w_sem,
    o_sem,
    s_send,
    s_recv,
    nf_send,
    nf_recv,
    nn_send,
    nn_recv,
    tf_send,
    tf_recv,
    tn_send,
    tn_recv,
    ty_send,
    ty_recv,
    gf_recv,
    gn_send,
    gn_recv,
    hop_send,
    kf_send,
    kf_recv,
    kn_send,
    kn_recv,
    dn_send,
    dn_recv,
    df_send,
    df_recv,
    pn_send,
    pn_recv,
    pf_send,
    pf_recv,
    ks_send,
    ks_recv,
    t_send,
    t_recv,
    go,
):
    sec = lax.axis_index("section")
    me = lax.axis_index("tp")
    inner = inner_size(tp_count)
    outer = tp_count // inner
    z, x = me // inner, lax.rem(me, inner)
    batch_groups, rows, width = saved_ref.shape
    tokens = rows * tp_count
    every = batch_groups * tokens
    head_cols = wq.shape[1]
    local_heads = head_cols // HEAD_WIDTH
    slice_width, key_width = kw.shape
    key_count = key_width // HEAD_WIDTH
    sharers = tp_count // key_count
    group_width = inner * slice_width
    step_width = min(2048, group_width)
    merge_width = min(1024, width)
    chunk_width = width // CHUNKS
    per_group = CHUNKS // batch_groups
    normed_width = width // per_group
    scale = 1.0 / math.sqrt(HEAD_WIDTH)
    is_last = sec == section_count - 1
    feeds = sec > 0
    helps = sec == section_count - 3

    def zpeer(zd):
        return lax.rem(z + zd, outer)

    def xpeer(xd):
        return lax.rem(x + xd, inner)

    def remote(source, target, send, receive, section, index):
        return pltpu.make_async_remote_copy(
            src_ref=source,
            dst_ref=target,
            send_sem=send,
            recv_sem=receive,
            device_id=(section, index),
            device_id_type=MESH,
        )

    def far(source, target, send, receive, zd):
        return remote(source, target, send, receive, sec, zpeer(zd) * inner + x)

    def near(source, target, send, receive, xd):
        return remote(source, target, send, receive, sec, z * inner + xpeer(xd))

    def columns(start, size):
        return pl.ds(pl.multiple_of(start, HEAD_WIDTH), size)

    loads = [
        pltpu.make_async_copy(source, target, w_sem.at[i])
        for i, (source, target) in enumerate(
            (
                (saved_hbm, saved_ref),
                (dir_hbm, dir_ref),
                (kw_hbm, kw),
                (vw_hbm, vw),
                (wq_hbm, wq),
                (wo_hbm, wo),
            )
        )
    ]
    for load in loads:
        load.start()

    barrier = pltpu.get_barrier_semaphore()
    for d in range(1, tp_count):
        pl.semaphore_signal(
            barrier, inc=1, device_id=(sec, lax.rem(me + d, tp_count)), device_id_type=MESH
        )

    @pl.when(sec < section_count - 1)
    def _():
        for zd in range(outer):
            pl.semaphore_signal(
                barrier, inc=1, device_id=(sec + 1, zpeer(zd) * inner + x), device_id_type=MESH
            )

    @pl.when(is_last)
    def _():
        pl.semaphore_signal(barrier, inc=1, device_id=(sec - 2, me), device_id_type=MESH)

    loads[0].wait()
    gain_row = gain_ref[...].astype(wide)
    for m in range(batch_groups):
        rows_in = saved_ref[m].astype(wide)
        inv = lax.rsqrt(jnp.mean(rows_in * rows_in, -1, keepdims=True) + norm_epsilon)
        inverse[m] = jnp.broadcast_to(inv, (rows, LANES))
        unit_rows = rows_in * inv
        unit[m] = unit_rows
        nall[me, m] = (unit_rows * gain_row).astype(low)

    @pl.when(helps)
    def _():
        pl.semaphore_wait(barrier, tp_count + outer)

    @pl.when(feeds & jnp.logical_not(helps))
    def _():
        pl.semaphore_wait(barrier, tp_count - 1 + outer)

    @pl.when(jnp.logical_not(feeds))
    def _():
        pl.semaphore_wait(barrier, tp_count - 1)

    def iota(shape, dim):
        return lax.broadcasted_iota(jnp.int32, shape, dim)

    def to_column(row, count, start):
        span = row.shape[1]
        pick = iota((count, span), 1) == iota((count, span), 0) + start
        return jnp.sum(jnp.where(pick, jnp.broadcast_to(row, (count, span)), 0.0), -1, keepdims=True)

    def own_member(m, kind):
        own = to_column(ids_ref[m : m + 1].astype(wide), rows, me * rows)
        slot = 2 * iota((rows, SLOTS), 1) + kind
        return (own == slot.astype(wide)).astype(wide)

    def slot_counts(m, kind):
        pairs = counts_ref.shape[1]
        table = iota((pairs, SLOTS), 0) == jnp.broadcast_to(slot_ref[m : m + 1], (pairs, SLOTS))
        count = to_column(counts_ref[kind : kind + 1].astype(wide), pairs, 0)
        return jnp.sum(jnp.where(table, count, 0.0), 0, keepdims=True)

    def sums_copy(d):
        return remote(
            sums_all.at[me], sums_all.at[me], s_send.at[d], s_recv.at[d], sec, lax.rem(me + d, tp_count)
        )

    def block_from(zd):
        return lax.rem(z - zd + outer, outer) * inner + x

    def normed_piece(block, c):
        start = c % per_group * normed_width
        return nall.at[block, c // per_group, :, start : start + normed_width]

    def normed_far(c, zd):
        block = normed_piece(me, c)
        return far(block, block, nf_send.at[c, zd], nf_recv.at[c, zd], zd)

    def normed_near(c, zd, xd):
        block = normed_piece(block_from(zd), c)
        slot = zd * inner + xd
        return near(block, block, nn_send.at[c, slot], nn_recv.at[c, slot], xd)

    def chunk(c):
        return columns(c * chunk_width, chunk_width)

    def top_far(m, c, zd):
        block = top.at[m, me, :, chunk(c)]
        return far(block, block, tf_send.at[m, c, zd], tf_recv.at[m, c, zd], zd)

    def top_near(m, c, zd, xd):
        block = top.at[m, block_from(zd), :, chunk(c)]
        slot = zd * inner + xd
        return near(block, block, tn_send.at[m, c, slot], tn_recv.at[m, c, slot], xd)

    def top_move(m, c, section):
        return remote(
            top.at[m, :, :, chunk(c)],
            gall.at[m, :, :, chunk(c)],
            ty_send.at[m, c],
            ty_recv.at[m, c],
            section,
            me,
        )

    def hop(m, c, zd, section):
        return remote(
            gin_ref.at[m, :, chunk(c)],
            gall.at[m, me, :, chunk(c)],
            hop_send.at[m, c, zd],
            gf_recv.at[m, c, zd],
            section,
            zpeer(zd) * inner + x,
        )

    def grad_near(m, c, zd, xd):
        block = gall.at[m, block_from(zd), :, chunk(c)]
        slot = zd * inner + xd
        return near(block, block, gn_send.at[m, c, slot], gn_recv.at[m, c, slot], xd)

    loads[1].wait()

    @pl.when(helps)
    def _():
        sums_all[me] = jnp.zeros(sums_all.shape[1:], wide)
        for m in range(batch_groups):
            ratio = to_column(ratio_ref[m : m + 1], rows, 0)
            for kind in range(2):
                sums_all[me, 2 * m + kind : 2 * m + kind + 1, 0:SLOTS] = jnp.sum(
                    own_member(m, kind) * ratio, 0, keepdims=True
                )
        for d in range(1, tp_count):
            sums_copy(d).start()

    @pl.when(helps)
    def _():
        for d in range(1, tp_count):
            sums_copy(d).wait()
        total = sums_all[0]
        for d in range(1, tp_count):
            total = total + sums_all[d]
        for m in range(batch_groups):
            chosen, rejected = slot_counts(m, 0), slot_counts(m, 1)
            margin = pair_beta * (
                total[2 * m : 2 * m + 1, 0:SLOTS] / chosen
                - total[2 * m + 1 : 2 * m + 2, 0:SLOTS] / rejected
            )
            weight = pair_beta * jax.nn.sigmoid(-margin)
            token_weight = jnp.sum(
                own_member(m, 0) * (-weight / chosen) + own_member(m, 1) * (weight / rejected),
                -1,
                keepdims=True,
            )
            top[m, me] = (token_weight * dir_ref[m].astype(wide)).astype(low)
            for c in range(CHUNKS):
                for zd in range(1, outer):
                    top_far(m, c, zd).start()
                for xd in range(1, inner):
                    top_near(m, c, 0, xd).start()

    @pl.when(helps)
    def _():
        order = [(m, c) for m in range(batch_groups) for c in range(CHUNKS)]

        def top_forward(m, c):
            for zd in range(1, outer):
                top_far(m, c, zd).wait()
                for xd in range(1, inner):
                    top_near(m, c, zd, xd).start()

        top_forward(*order[0])
        for at, (m, c) in enumerate(order):
            if at + 1 < len(order):
                top_forward(*order[at + 1])
            for zd in range(outer):
                for xd in range(1, inner):
                    top_near(m, c, zd, xd).wait()
            top_move(m, c, sec + 2).start()

        @pl.when(feeds)
        def _():
            pl.semaphore_signal(go, inc=1, device_id=(sec - 1, me), device_id_type=MESH)

    @pl.when((sec == section_count - 2) | (sec == section_count - 4))
    def _():
        pl.semaphore_wait(go, 1)

    for c in range(CHUNKS):
        for zd in range(1, outer):
            normed_far(c, zd).start()
        for xd in range(1, inner):
            normed_near(c, 0, xd).start()

    for c in range(CHUNKS):
        for zd in range(1, outer):
            normed_far(c, zd).wait()
            for xd in range(1, inner):
                normed_near(c, zd, xd).start()
    for c in range(CHUNKS):
        for zd in range(outer):
            for xd in range(1, inner):
                normed_near(c, zd, xd).wait()

    @pl.when(is_last)
    def _():
        pl.semaphore_signal(go, inc=1, device_id=(sec - 1, me), device_id_type=MESH)

    def merge(k, carry):
        cols = columns(k * merge_width, merge_width)
        for m in range(batch_groups):
            normed_ref[m * tokens : (m + 1) * tokens, cols] = jnp.concatenate(
                [nall[j, m, :, cols].astype(wide) for j in range(tp_count)], 0
            ).astype(low)
        return carry

    lax.fori_loop(0, width // merge_width, merge, 0)
    normed_out = pltpu.make_async_copy(normed_ref, normed_hbm, o_sem.at[0])
    normed_out.start()

    def up_out(m):
        return pltpu.make_async_copy(up_ref.at[m], up_hbm.at[m], o_sem.at[1 + m])

    normed_cols_ref[...] = normed_ref[:, columns(me * slice_width, slice_width)]
    loads[2].wait()
    loads[3].wait()
    for kind, weight_ref in enumerate((kw, vw)):
        product = jnp.dot(normed_cols_ref[...], weight_ref[...], preferred_element_type=wide)
        for k in range(key_count):
            kv_part[k, kind] = product[:, k * HEAD_WIDTH : (k + 1) * HEAD_WIDTH].astype(low)

    def kv_far_copy(zd):
        head = zpeer(zd) * inner // sharers
        return far(kv_part.at[head], kv_far.at[zd], kf_send.at[zd], kf_recv.at[zd], zd)

    def kv_near_copy(xd):
        return near(kv_near.at[0], kv_near.at[xd], kn_send.at[xd], kn_recv.at[xd], xd)

    for zd in range(1, outer):
        kv_far_copy(zd).start()

    loads[4].wait()

    def project(k, total):
        cols = columns(k * step_width, step_width)
        return total + jnp.dot(normed_ref[:, cols], wq[cols, :], preferred_element_type=wide)

    product = lax.fori_loop(
        0, width // step_width, project, jnp.zeros((every, head_cols), wide)
    ).astype(low)
    for m in range(batch_groups):
        queries[m] = product[m * tokens : (m + 1) * tokens]

    for zd in range(1, outer):
        kv_far_copy(zd).wait()
    for kind in range(2):
        total = kv_part[z * inner // sharers, kind].astype(wide)
        for zd in range(1, outer):
            total = total + kv_far[zd, kind].astype(wide)
        kv_near[0, kind] = total.astype(low)
    for xd in range(1, inner):
        kv_near_copy(xd).start()
    for xd in range(1, inner):
        kv_near_copy(xd).wait()
    for kind in range(2):
        total = kv_near[0, kind].astype(wide)
        for xd in range(1, inner):
            total = total + kv_near[xd, kind].astype(wide)
        total = total.astype(low)
        for m in range(batch_groups):
            kv[m, kind] = total[m * tokens : (m + 1) * tokens]

    for m in range(batch_groups):
        ids = ids_ref[m : m + 1].astype(wide)
        mask = (to_column(ids, tokens, 0) == jnp.broadcast_to(ids, (tokens, tokens))) & (
            iota((tokens, tokens), 0) >= iota((tokens, tokens), 1)
        )
        for h in range(local_heads):
            head = slice(h * HEAD_WIDTH, (h + 1) * HEAD_WIDTH)
            scores = contract(queries[m, :, head], kv[m, 0], 1, 1) * scale
            value = jnp.exp(jnp.where(mask, scores, masked_score))
            value = value / jnp.sum(value, -1, keepdims=True)
            probs[m, h] = value
            att_ref[m * tokens : (m + 1) * tokens, head] = jnp.dot(
                value.astype(low), kv[m, 1], preferred_element_type=wide
            ).astype(low)
    loads[5].wait()
    gain_out_ref[...] = jnp.zeros_like(gain_out_ref)

    def dkv_near_copy(m, xd):
        return near(
            dkv_near.at[m, 0], dkv_near.at[m, xd], dn_send.at[m, xd], dn_recv.at[m, xd], xd
        )

    def dkv_far_copy(m, zd):
        block = dkv_far.at[m, z]
        return far(block, block, df_send.at[m, zd], df_recv.at[m, zd], zd)

    def group(i):
        return columns(lax.rem(z + i, outer) * group_width, group_width)

    def part_near(m, i, xd):
        return near(
            part.at[m, xpeer(xd), :, :, group(i)],
            near_recv.at[m, xd - 1, :, :, group(i)],
            pn_send.at[m, xd, i - 1],
            pn_recv.at[m, xd, i - 1],
            xd,
        )

    def part_far(m, i, c, zd):
        cols = columns(c * group_width, group_width)
        return far(
            far_send.at[m, zd, :, cols],
            far_recv.at[m, zd, :, cols],
            pf_send.at[m, zd, i - 1],
            pf_recv.at[m, zd, i - 1],
            zd,
        )

    def key_copy(m, d):
        peer = lax.rem(me + d, tp_count)
        return remote(
            key_send.at[m, peer], key_recv.at[m, me], ks_send.at[m, d], ks_recv.at[m, d], sec, peer
        )

    def part_group(m, i):
        base = lax.rem(z + i, outer) * group_width

        def piece(k, carry):
            start = base + k * step_width
            cols = columns(start, step_width)
            product = contract(gq_ref[m], wq[cols, :], 1, 1)
            for block in range(tp_count):
                part[m, block % inner, block // inner, :, cols] = product[
                    block * rows : (block + 1) * rows
                ].astype(low)
            return carry

        lax.fori_loop(0, group_width // step_width, piece, 0)
        for xd in range(1, inner):
            part_near(m, i, xd).start()

    def sum_group(m, i):
        cols = group(i)
        for xd in range(1, inner):
            part_near(m, i, xd).wait()
        for zd in range(outer):
            total = part[m, x, zpeer(zd), :, cols].astype(wide)
            for xd in range(1, inner):
                total = total + near_recv[m, xd - 1, zpeer(zd), :, cols].astype(wide)
            if zd:
                far_send[m, zd, :, cols] = total.astype(low)
                part_far(m, i, lax.rem(z + i, outer), zd).start()
            else:
                far_recv[m, 0, :, cols] = total.astype(low)

    def forward(m, c):
        @pl.when(jnp.logical_not(is_last))
        def _():
            for zd in range(outer):
                hop(m, c, zd, sec).wait_recv()
                for xd in range(1, inner):
                    grad_near(m, c, zd, xd).start()

    def begin(m):
        def upstream(c, total):
            if m == 0:
                pl.when(c + 1 < CHUNKS)(functools.partial(forward, m, c + 1))

            @pl.when(is_last)
            def _():
                top_move(m, c, sec).wait_recv()

            @pl.when(jnp.logical_not(is_last))
            def _():
                for zd in range(outer):
                    for xd in range(1, inner):
                        grad_near(m, c, zd, xd).wait()

            for k in range(chunk_width // step_width):
                cols = columns(c * chunk_width + k * step_width, step_width)
                piece = jnp.concatenate(
                    [gall[m, j, :, cols].astype(wide) for j in range(tp_count)], 0
                ).astype(low)
                up_ref[m, :, cols] = piece
                total = total + contract(piece, wo[:, cols], 1, 1)
            return total

        grad_heads[...] = lax.fori_loop(
            0, CHUNKS, upstream, jnp.zeros((tokens, head_cols), wide)
        ).astype(low)
        up_out(m).start()
        grad_keys = jnp.zeros((tokens, HEAD_WIDTH), wide)
        grad_values = jnp.zeros((tokens, HEAD_WIDTH), wide)
        for h in range(local_heads):
            head = slice(h * HEAD_WIDTH, (h + 1) * HEAD_WIDTH)
            grad_head = grad_heads[:, head]
            prob = probs[m, h]
            grad_probs = contract(grad_head, kv[m, 1], 1, 1)
            grad_scores = prob * (grad_probs - jnp.sum(prob * grad_probs, -1, keepdims=True))
            scores_low = (grad_scores * scale).astype(low)
            gq_ref[m, :, head] = jnp.dot(
                scores_low, kv[m, 0], preferred_element_type=wide
            ).astype(low)
            grad_keys = grad_keys + contract(scores_low, queries[m, :, head], 0, 0)
            grad_values = grad_values + contract(prob.astype(low), grad_head, 0, 0)
        dkv_near[m, 0, 0] = grad_keys.astype(low)
        dkv_near[m, 0, 1] = grad_values.astype(low)
        for xd in range(1, inner):
            dkv_near_copy(m, xd).start()

    def spread(m):
        part_group(m, 1)

        for xd in range(1, inner):
            dkv_near_copy(m, xd).wait()
        for kind in range(2):
            total = dkv_near[m, 0, kind].astype(wide)
            for xd in range(1, inner):
                total = total + dkv_near[m, xd, kind].astype(wide)
            dkv_far[m, z, kind] = total.astype(low)
        for zd in range(1, outer):
            dkv_far_copy(m, zd).start()

        def middle(i, inner_carry):
            part_group(m, i)
            sum_group(m, i - 1)
            return inner_carry

        lax.fori_loop(2, outer + 1, middle, 0)

        for zd in range(1, outer):
            dkv_far_copy(m, zd).wait()
        holders = outer // key_count
        for kind in range(2):
            for k in range(key_count):
                total = dkv_far[m, k * holders, kind].astype(wide)
                for other in range(1, holders):
                    total = total + dkv_far[m, k * holders + other, kind].astype(wide)
                dkv_ref[kind, m, :, k * HEAD_WIDTH : (k + 1) * HEAD_WIDTH] = total.astype(low)
        key_slice = contract(dkv_ref[0, m], kw[...], 1, 1) + contract(
            dkv_ref[1, m], vw[...], 1, 1
        )
        for j in range(tp_count):
            key_send[m, j] = key_slice[j * rows : (j + 1) * rows].astype(low)
        for d in range(1, tp_count):
            key_copy(m, d).start()
        key_recv[m, me] = key_send[m, me]
        sum_group(m, outer)

    def gain_copy(d):
        return remote(
            gain_all.at[me],
            gain_all.at[me],
            t_send.at[d],
            t_recv.at[d],
            sec,
            lax.rem(me + d, tp_count),
        )

    def finish(m):
        for zd in range(1, outer):
            for i in range(1, outer + 1):
                part_far(m, i, lax.rem(z + i, outer), zd).wait_send()
                part_far(m, i, lax.rem(z - zd + i + outer, outer), zd).wait_recv()

        for d in range(1, tp_count):
            key_copy(m, d).wait()

        products = jnp.zeros((rows, slice_width), wide)
        for k in range(tp_count):
            cols = slice(k * slice_width, (k + 1) * slice_width)
            normed_grad = key_recv[m, k].astype(wide) + jnp.sum(
                far_recv[m, :, :, cols].astype(wide), 0
            )
            unit_part = unit[m, :, cols]
            gain_out_ref[:, cols] = gain_out_ref[:, cols] + jnp.sum(
                normed_grad * unit_part, 0, keepdims=True
            )
            scaled = normed_grad * gain_ref[:, cols].astype(wide)
            grad_unit[:, cols] = scaled
            products = products + scaled * unit_part
        if m + 1 == batch_groups:
            gain_all[me] = gain_out_ref[...].astype(low)
            for d in range(1, tp_count):
                gain_copy(d).start()
        dots = jnp.sum(products, -1, keepdims=True) / width
        inv = inverse[m, :, 0:1]
        for c in range(CHUNKS):
            cols = slice(c * chunk_width, (c + 1) * chunk_width)
            gin_ref[m, :, cols] = (
                gall[m, me, :, cols].astype(wide)
                + inv * (grad_unit[:, cols] - unit[m, :, cols] * dots)
            ).astype(low)

            @pl.when(feeds)
            def _():
                for zd in range(outer):
                    hop(m, c, zd, sec - 1).start()

    forward(0, 0)
    begin(0)
    for m in range(batch_groups):
        spread(m)
        if m + 1 < batch_groups:
            for c in range(CHUNKS):
                forward(m + 1, c)
        if m + 1 < batch_groups:
            pl.when(is_last)(functools.partial(begin, m + 1))
        finish(m)
        if m + 1 < batch_groups:
            pl.when(jnp.logical_not(is_last))(functools.partial(begin, m + 1))

    for d in range(1, tp_count):
        gain_copy(d).wait()
    total = gain_all[0].astype(wide)
    for d in range(1, tp_count):
        total = total + gain_all[d].astype(wide)
    gain_out_ref[...] = total
    normed_out.wait()
    for m in range(batch_groups):
        up_out(m).wait()

    @pl.when(helps)
    def _():
        for m in range(batch_groups):
            for c in range(CHUNKS):
                top_move(m, c, sec + 2).wait_send()

    @pl.when(feeds)
    def _():
        for m in range(batch_groups):
            for c in range(CHUNKS):
                for zd in range(outer):
                    hop(m, c, zd, sec - 1).wait_send()


def relay(saved, gain, wq, kw, vw, wo, direction, ratio, ids, slots, counts):
    tp_count = lax.axis_size("tp")
    inner = inner_size(tp_count)
    outer = tp_count // inner
    batch_groups, rows, width = saved.shape
    tokens = rows * tp_count
    every = batch_groups * tokens
    head_cols = wq.shape[1]
    key_width = kw.shape[1]
    key_count = key_width // HEAD_WIDTH
    slice_width = kw.shape[0]
    vmem = pl.BlockSpec(memory_space=pltpu.VMEM)
    hbm = pl.BlockSpec(memory_space=pltpu.HBM)
    dma = pltpu.SemaphoreType.DMA
    groups = batch_groups
    return pl.pallas_call(
        functools.partial(relay_kernel, lax.axis_size("section"), tp_count),
        out_shape=[
            jax.ShapeDtypeStruct((groups, rows, width), low),
            jax.ShapeDtypeStruct((groups, tokens, width), low),
            jax.ShapeDtypeStruct((every, width), low),
            jax.ShapeDtypeStruct((every, slice_width), low),
            jax.ShapeDtypeStruct((every, head_cols), low),
            jax.ShapeDtypeStruct((groups, tokens, head_cols), low),
            jax.ShapeDtypeStruct((2, groups, tokens, key_width), low),
            jax.ShapeDtypeStruct((1, width), wide),
        ],
        in_specs=[hbm, vmem, hbm, hbm, hbm, hbm, hbm] + [vmem] * 4,
        out_specs=[vmem, hbm, hbm] + [vmem] * 5,
        scratch_shapes=[
            pltpu.VMEM(saved.shape, low),
            pltpu.VMEM(direction.shape, low),
            pltpu.VMEM(kw.shape, low),
            pltpu.VMEM(vw.shape, low),
            pltpu.VMEM(wq.shape, low),
            pltpu.VMEM(wo.shape, low),
            pltpu.VMEM((groups, tokens, width), low),
            pltpu.VMEM((every, width), low),
            pltpu.VMEM((tp_count, groups, rows, width), low),
            pltpu.VMEM((groups, tp_count, rows, width), low),
            pltpu.VMEM((groups, tp_count, rows, width), low),
            pltpu.VMEM((groups, inner, outer, rows, width), low),
            pltpu.VMEM((groups, inner - 1, outer, rows, width), low),
            pltpu.VMEM((groups, outer, rows, width), low),
            pltpu.VMEM((groups, outer, rows, width), low),
            pltpu.VMEM((groups, rows, width), wide),
            pltpu.VMEM((groups, rows, LANES), wide),
            pltpu.VMEM((rows, width), wide),
            pltpu.VMEM((groups, tokens, head_cols), low),
            pltpu.VMEM((groups, 2, tokens, HEAD_WIDTH), low),
            pltpu.VMEM((key_count, 2, every, HEAD_WIDTH), low),
            pltpu.VMEM((outer, 2, every, HEAD_WIDTH), low),
            pltpu.VMEM((inner, 2, every, HEAD_WIDTH), low),
            pltpu.VMEM((groups, head_cols // HEAD_WIDTH, tokens, tokens), wide),
            pltpu.VMEM((tokens, head_cols), low),
            pltpu.VMEM((groups, tp_count, rows, slice_width), low),
            pltpu.VMEM((groups, tp_count, rows, slice_width), low),
            pltpu.VMEM((groups, inner, 2, tokens, HEAD_WIDTH), low),
            pltpu.VMEM((groups, outer, 2, tokens, HEAD_WIDTH), low),
            pltpu.VMEM((tp_count, 8, LANES), wide),
            pltpu.VMEM((tp_count, 1, width), low),
            dma((6,)),
            dma((1 + groups,)),
            dma((tp_count,)),
            dma((tp_count,)),
            dma((CHUNKS, outer)),
            dma((CHUNKS, outer)),
            dma((CHUNKS, tp_count)),
            dma((CHUNKS, tp_count)),
            dma((groups, CHUNKS, outer)),
            dma((groups, CHUNKS, outer)),
            dma((groups, CHUNKS, tp_count)),
            dma((groups, CHUNKS, tp_count)),
            dma((groups, CHUNKS)),
            dma((groups, CHUNKS)),
            dma((groups, CHUNKS, outer)),
            dma((groups, CHUNKS, tp_count)),
            dma((groups, CHUNKS, tp_count)),
            dma((groups, CHUNKS, outer)),
            dma((outer,)),
            dma((outer,)),
            dma((inner,)),
            dma((inner,)),
            dma((groups, inner)),
            dma((groups, inner)),
            dma((groups, outer)),
            dma((groups, outer)),
            dma((groups, inner, outer)),
            dma((groups, inner, outer)),
            dma((groups, outer, outer)),
            dma((groups, outer, outer)),
            dma((groups, tp_count)),
            dma((groups, tp_count)),
            dma((tp_count,)),
            dma((tp_count,)),
            pltpu.SemaphoreType.REGULAR,
        ],
        compiler_params=pltpu.CompilerParams(
            collective_id=0, has_side_effects=True, vmem_limit_bytes=VMEM_LIMIT
        ),
        name="relay",
    )(saved, gain, wq, kw, vw, wo, direction, ratio, ids, slots, counts)


def weights_kernel(
    normed_ref,
    normed_cols_ref,
    gq_ref,
    dkv_ref,
    att_ref,
    up_ref,
    grads_in,
    gain_in,
    grads_out,
    of_query,
    of_key,
    of_value,
    of_out,
    gain_out,
):
    step = pl.program_id(0)

    @pl.when(step == 0)
    def _():
        grads_out[...] = grads_in[...]
        gain_out[...] = gain_in[...]

    narrow = of_key.shape[0]
    own = normed_cols_ref[:, pl.ds(pl.multiple_of(step * narrow, narrow), narrow)]
    of_query[...] = contract(normed_ref[...], gq_ref[...], 0, 0).astype(low)
    of_out[...] = contract(att_ref[...], up_ref[...], 0, 0).astype(low)
    of_key[...] = contract(own, dkv_ref[0], 0, 0).astype(low)
    of_value[...] = contract(own, dkv_ref[1], 0, 0).astype(low)


def weight_gradients(normed, normed_cols, grad_queries, dkv, attended, upstream, grads, gain):
    every, width = normed.shape
    head_cols = grad_queries.shape[1]
    slice_width, key_width = normed_cols.shape[1], dkv.shape[2]
    steps = slice_width // HEAD_WIDTH
    part = width // steps

    def whole(shape):
        return pl.BlockSpec(shape, lambda i: (0,) * len(shape))

    def lanes(shape):
        return pl.BlockSpec(shape, lambda i: (0, i))

    def above(shape):
        return pl.BlockSpec(shape, lambda i: (i, 0))

    return pl.pallas_call(
        weights_kernel,
        grid=(steps,),
        out_shape=[
            jax.ShapeDtypeStruct(grads.shape, low),
            jax.ShapeDtypeStruct((width, head_cols), low),
            jax.ShapeDtypeStruct((slice_width, key_width), low),
            jax.ShapeDtypeStruct((slice_width, key_width), low),
            jax.ShapeDtypeStruct((head_cols, width), low),
            jax.ShapeDtypeStruct(gain.shape, wide),
        ],
        in_specs=[
            lanes((every, part)),
            whole(normed_cols.shape),
            whole(grad_queries.shape),
            whole(dkv.shape),
            whole(attended.shape),
            lanes((every, part)),
            whole(grads.shape),
            whole(gain.shape),
        ],
        out_specs=[
            whole(grads.shape),
            above((part, head_cols)),
            above((HEAD_WIDTH, key_width)),
            above((HEAD_WIDTH, key_width)),
            lanes((head_cols, part)),
            whole(gain.shape),
        ],
        compiler_params=pltpu.CompilerParams(vmem_limit_bytes=VMEM_LIMIT),
        name="weight_gradients",
    )(normed, normed_cols, grad_queries, dkv, attended, upstream, grads, gain)


def body(
    section_inputs,
    norm_gain,
    w_query,
    key_projection,
    value_projection,
    w_out,
    token_dir,
    tok_logratio,
    segment_ids,
    pair_of_slot,
    pair_counts,
):
    saved = section_inputs[0]
    width = saved.shape[2]
    every = segment_ids.size
    grads, upstream, normed, normed_cols, attended, grad_queries, dkv, gain_total = relay(
        saved,
        norm_gain[0].reshape(1, width),
        w_query[0],
        key_projection[0],
        value_projection[0],
        w_out[0],
        token_dir,
        tok_logratio,
        segment_ids,
        pair_of_slot,
        pair_counts.T,
    )
    grads, of_query, of_key, of_value, of_out, gain_total = weight_gradients(
        normed,
        normed_cols,
        grad_queries.reshape(every, -1),
        dkv.reshape(2, every, -1),
        attended,
        upstream.reshape(every, width),
        grads,
        gain_total,
    )
    return (
        grads[None],
        of_query[None],
        of_key[None],
        of_value[None],
        of_out[None],
        gain_total,
    )


def solution(mesh):
    placed = (
        P("section", None, "tp", None),
        P("section", None),
        P("section", None, "tp"),
        P("section", "tp", None),
        P("section", "tp", None),
        P("section", "tp", None),
        P(None, "tp", None),
        P(None, "tp"),
        P(),
        P(),
        P(),
    )
    return jax.shard_map(
        body,
        mesh=mesh,
        in_specs=placed,
        out_specs=(
            P("section", None, "tp", None),
            P("section", None, "tp"),
            P("section", "tp", None),
            P("section", "tp", None),
            P("section", "tp", None),
            P("section", None),
        ),
        check_vma=False,
    )
```

```python
import functools
import math

import jax
import jax.numpy as jnp
from jax import lax
from jax.experimental import pallas as pl
from jax.experimental.pallas import tpu as pltpu
from jax.sharding import PartitionSpec as P

HEAD_WIDTH = 128
SLOTS = 4
LANES = 128
CHUNKS = 4

norm_epsilon = 1e-05
pair_beta = 4.0
masked_score = -1e30

MESH = pl.DeviceIdType.MESH
VMEM_LIMIT = 56 * 1024 * 1024
low, wide = jnp.bfloat16, jnp.float32


def contract(left, right, left_dim, right_dim):
    return lax.dot_general(
        left, right, (((left_dim,), (right_dim,)), ((), ())), preferred_element_type=wide
    )


def inner_size(tp_count):
    inner = 1
    while 2 * (2 * inner) ** 2 <= tp_count:
        inner *= 2
    return inner


def relay_kernel(
    section_count,
    tp_count,
    saved_hbm,
    gain_ref,
    wq_hbm,
    kw_hbm,
    vw_hbm,
    wo_hbm,
    dir_hbm,
    ratio_ref,
    ids_ref,
    slot_ref,
    counts_ref,
    gin_ref,
    up_hbm,
    normed_hbm,
    normed_cols_ref,
    att_ref,
    gq_ref,
    dkv_ref,
    gain_out_ref,
    saved_ref,
    dir_ref,
    kw,
    vw,
    wq,
    wo,
    up_ref,
    normed_ref,
    nall,
    slices,
    top,
    gall,
    part,
    near_recv,
    far_send,
    far_recv,
    unit,
    inverse,
    grad_unit,
    queries,
    kv,
    kv_part,
    kv_far,
    kv_near,
    probs,
    grad_heads,
    key_send,
    key_recv,
    dkv_near,
    dkv_far,
    sums_all,
    gain_all,
    w_sem,
    o_sem,
    s_send,
    s_recv,
    nf_send,
    nf_recv,
    nn_send,
    nn_recv,
    tf_send,
    tf_recv,
    tn_send,
    tn_recv,
    ty_send,
    ty_recv,
    gf_recv,
    gn_send,
    gn_recv,
    hop_send,
    kf_send,
    kf_recv,
    kn_send,
    kn_recv,
    dn_send,
    dn_recv,
    df_send,
    df_recv,
    pn_send,
    pn_recv,
    pf_send,
    pf_recv,
    ks_send,
    ks_recv,
    t_send,
    t_recv,
    sl_send,
    sl_recv,
    go,
):
    sec = lax.axis_index("section")
    me = lax.axis_index("tp")
    inner = inner_size(tp_count)
    outer = tp_count // inner
    z, x = me // inner, lax.rem(me, inner)
    batch_groups, rows, width = saved_ref.shape
    tokens = rows * tp_count
    every = batch_groups * tokens
    head_cols = wq.shape[1]
    local_heads = head_cols // HEAD_WIDTH
    slice_width, key_width = kw.shape
    key_count = key_width // HEAD_WIDTH
    sharers = tp_count // key_count
    group_width = inner * slice_width
    step_width = min(2048, group_width)
    merge_width = min(1024, width)
    chunk_width = width // CHUNKS
    per_group = CHUNKS // batch_groups
    normed_width = width // per_group
    scale = 1.0 / math.sqrt(HEAD_WIDTH)
    is_last = sec == section_count - 1
    feeds = sec > 0
    helps = sec == section_count - 3

    def zpeer(zd):
        return lax.rem(z + zd, outer)

    def xpeer(xd):
        return lax.rem(x + xd, inner)

    def remote(source, target, send, receive, section, index):
        return pltpu.make_async_remote_copy(
            src_ref=source,
            dst_ref=target,
            send_sem=send,
            recv_sem=receive,
            device_id=(section, index),
            device_id_type=MESH,
        )

    def far(source, target, send, receive, zd):
        return remote(source, target, send, receive, sec, zpeer(zd) * inner + x)

    def near(source, target, send, receive, xd):
        return remote(source, target, send, receive, sec, z * inner + xpeer(xd))

    def columns(start, size):
        return pl.ds(pl.multiple_of(start, HEAD_WIDTH), size)

    loads = [
        pltpu.make_async_copy(source, target, w_sem.at[i])
        for i, (source, target) in enumerate(
            (
                (saved_hbm, saved_ref),
                (dir_hbm, dir_ref),
                (kw_hbm, kw),
                (vw_hbm, vw),
                (wq_hbm, wq),
                (wo_hbm, wo),
            )
        )
    ]
    for load in loads:
        load.start()

    barrier = pltpu.get_barrier_semaphore()
    for d in range(1, tp_count):
        pl.semaphore_signal(
            barrier, inc=1, device_id=(sec, lax.rem(me + d, tp_count)), device_id_type=MESH
        )

    @pl.when(sec < section_count - 1)
    def _():
        for zd in range(outer):
            pl.semaphore_signal(
                barrier, inc=1, device_id=(sec + 1, zpeer(zd) * inner + x), device_id_type=MESH
            )

    @pl.when(is_last)
    def _():
        pl.semaphore_signal(barrier, inc=1, device_id=(sec - 2, me), device_id_type=MESH)

    loads[0].wait()
    gain_row = gain_ref[...].astype(wide)
    for m in range(batch_groups):
        rows_in = saved_ref[m].astype(wide)
        inv = lax.rsqrt(jnp.mean(rows_in * rows_in, -1, keepdims=True) + norm_epsilon)
        inverse[m] = jnp.broadcast_to(inv, (rows, LANES))
        unit_rows = rows_in * inv
        unit[m] = unit_rows
        nall[me, m] = (unit_rows * gain_row).astype(low)

    @pl.when(helps)
    def _():
        pl.semaphore_wait(barrier, tp_count + outer)

    @pl.when(feeds & jnp.logical_not(helps))
    def _():
        pl.semaphore_wait(barrier, tp_count - 1 + outer)

    @pl.when(jnp.logical_not(feeds))
    def _():
        pl.semaphore_wait(barrier, tp_count - 1)

    def iota(shape, dim):
        return lax.broadcasted_iota(jnp.int32, shape, dim)

    def to_column(row, count, start):
        span = row.shape[1]
        pick = iota((count, span), 1) == iota((count, span), 0) + start
        return jnp.sum(jnp.where(pick, jnp.broadcast_to(row, (count, span)), 0.0), -1, keepdims=True)

    def own_member(m, kind):
        own = to_column(ids_ref[m : m + 1].astype(wide), rows, me * rows)
        slot = 2 * iota((rows, SLOTS), 1) + kind
        return (own == slot.astype(wide)).astype(wide)

    def slot_counts(m, kind):
        pairs = counts_ref.shape[1]
        table = iota((pairs, SLOTS), 0) == jnp.broadcast_to(slot_ref[m : m + 1], (pairs, SLOTS))
        count = to_column(counts_ref[kind : kind + 1].astype(wide), pairs, 0)
        return jnp.sum(jnp.where(table, count, 0.0), 0, keepdims=True)

    def sums_copy(d):
        return remote(
            sums_all.at[me], sums_all.at[me], s_send.at[d], s_recv.at[d], sec, lax.rem(me + d, tp_count)
        )

    def block_from(zd):
        return lax.rem(z - zd + outer, outer) * inner + x

    def normed_piece(block, c):
        start = c % per_group * normed_width
        return nall.at[block, c // per_group, :, start : start + normed_width]

    def normed_far(c, zd):
        block = normed_piece(me, c)
        return far(block, block, nf_send.at[c, zd], nf_recv.at[c, zd], zd)

    def normed_near(c, zd, xd):
        block = normed_piece(block_from(zd), c)
        slot = zd * inner + xd
        return near(block, block, nn_send.at[c, slot], nn_recv.at[c, slot], xd)

    def chunk(c):
        return columns(c * chunk_width, chunk_width)

    def top_far(m, c, zd):
        block = top.at[m, me, :, chunk(c)]
        return far(block, block, tf_send.at[m, c, zd], tf_recv.at[m, c, zd], zd)

    def top_near(m, c, zd, xd):
        block = top.at[m, block_from(zd), :, chunk(c)]
        slot = zd * inner + xd
        return near(block, block, tn_send.at[m, c, slot], tn_recv.at[m, c, slot], xd)

    def top_move(m, c, section):
        return remote(
            top.at[m, :, :, chunk(c)],
            gall.at[m, :, :, chunk(c)],
            ty_send.at[m, c],
            ty_recv.at[m, c],
            section,
            me,
        )

    def hop(m, c, zd, section):
        return remote(
            gin_ref.at[m, :, chunk(c)],
            gall.at[m, me, :, chunk(c)],
            hop_send.at[m, c, zd],
            gf_recv.at[m, c, zd],
            section,
            zpeer(zd) * inner + x,
        )

    def grad_near(m, c, zd, xd):
        block = gall.at[m, block_from(zd), :, chunk(c)]
        slot = zd * inner + xd
        return near(block, block, gn_send.at[m, c, slot], gn_recv.at[m, c, slot], xd)

    loads[1].wait()

    @pl.when(helps)
    def _():
        sums_all[me] = jnp.zeros(sums_all.shape[1:], wide)
        for m in range(batch_groups):
            ratio = to_column(ratio_ref[m : m + 1], rows, 0)
            for kind in range(2):
                sums_all[me, 2 * m + kind : 2 * m + kind + 1, 0:SLOTS] = jnp.sum(
                    own_member(m, kind) * ratio, 0, keepdims=True
                )
        for d in range(1, tp_count):
            sums_copy(d).start()

    @pl.when(helps)
    def _():
        for d in range(1, tp_count):
            sums_copy(d).wait()
        total = sums_all[0]
        for d in range(1, tp_count):
            total = total + sums_all[d]
        for m in range(batch_groups):
            chosen, rejected = slot_counts(m, 0), slot_counts(m, 1)
            margin = pair_beta * (
                total[2 * m : 2 * m + 1, 0:SLOTS] / chosen
                - total[2 * m + 1 : 2 * m + 2, 0:SLOTS] / rejected
            )
            weight = pair_beta * jax.nn.sigmoid(-margin)
            token_weight = jnp.sum(
                own_member(m, 0) * (-weight / chosen) + own_member(m, 1) * (weight / rejected),
                -1,
                keepdims=True,
            )
            top[m, me] = (token_weight * dir_ref[m].astype(wide)).astype(low)
            for c in range(CHUNKS):
                for zd in range(1, outer):
                    top_far(m, c, zd).start()
                for xd in range(1, inner):
                    top_near(m, c, 0, xd).start()

    @pl.when(helps)
    def _():
        order = [(m, c) for m in range(batch_groups) for c in range(CHUNKS)]

        def top_forward(m, c):
            for zd in range(1, outer):
                top_far(m, c, zd).wait()
                for xd in range(1, inner):
                    top_near(m, c, zd, xd).start()

        top_forward(*order[0])
        for at, (m, c) in enumerate(order):
            if at + 1 < len(order):
                top_forward(*order[at + 1])
            for zd in range(outer):
                for xd in range(1, inner):
                    top_near(m, c, zd, xd).wait()
            top_move(m, c, sec + 2).start()

        @pl.when(feeds)
        def _():
            pl.semaphore_signal(go, inc=1, device_id=(sec - 1, me), device_id_type=MESH)

    @pl.when((sec == section_count - 2) | (sec == section_count - 4))
    def _():
        pl.semaphore_wait(go, 1)

    def slice_copy(d):
        peer = lax.rem(me + d, tp_count)
        return remote(
            nall.at[me, :, :, columns(peer * slice_width, slice_width)],
            slices.at[me],
            sl_send.at[d],
            sl_recv.at[d],
            sec,
            peer,
        )

    for d in range(1, tp_count):
        slice_copy(d).start()
    for c in range(CHUNKS):
        for zd in range(1, outer):
            normed_far(c, zd).start()
        for xd in range(1, inner):
            normed_near(c, 0, xd).start()

    for d in range(1, tp_count):
        slice_copy(d).wait()
    slices[me] = nall[me, :, :, columns(me * slice_width, slice_width)]
    for m in range(batch_groups):
        normed_cols_ref[m * tokens : (m + 1) * tokens] = jnp.concatenate(
            [slices[j, m].astype(wide) for j in range(tp_count)], 0
        ).astype(low)
    loads[2].wait()
    loads[3].wait()
    for kind, weight_ref in enumerate((kw, vw)):
        product = jnp.dot(normed_cols_ref[...], weight_ref[...], preferred_element_type=wide)
        for k in range(key_count):
            kv_part[k, kind] = product[:, k * HEAD_WIDTH : (k + 1) * HEAD_WIDTH].astype(low)

    def kv_far_copy(zd):
        head = zpeer(zd) * inner // sharers
        return far(kv_part.at[head], kv_far.at[zd], kf_send.at[zd], kf_recv.at[zd], zd)

    def kv_near_copy(xd):
        return near(kv_near.at[0], kv_near.at[xd], kn_send.at[xd], kn_recv.at[xd], xd)

    for zd in range(1, outer):
        kv_far_copy(zd).start()

    for c in range(CHUNKS):
        for zd in range(1, outer):
            normed_far(c, zd).wait()
            for xd in range(1, inner):
                normed_near(c, zd, xd).start()
    for zd in range(1, outer):
        kv_far_copy(zd).wait()
    for kind in range(2):
        total = kv_part[z * inner // sharers, kind].astype(wide)
        for zd in range(1, outer):
            total = total + kv_far[zd, kind].astype(wide)
        kv_near[0, kind] = total.astype(low)
    for xd in range(1, inner):
        kv_near_copy(xd).start()
    for c in range(CHUNKS):
        for zd in range(outer):
            for xd in range(1, inner):
                normed_near(c, zd, xd).wait()

    @pl.when(is_last)
    def _():
        pl.semaphore_signal(go, inc=1, device_id=(sec - 1, me), device_id_type=MESH)

    def merge(k, carry):
        cols = columns(k * merge_width, merge_width)
        for m in range(batch_groups):
            normed_ref[m * tokens : (m + 1) * tokens, cols] = jnp.concatenate(
                [nall[j, m, :, cols].astype(wide) for j in range(tp_count)], 0
            ).astype(low)
        return carry

    lax.fori_loop(0, width // merge_width, merge, 0)
    normed_out = pltpu.make_async_copy(normed_ref, normed_hbm, o_sem.at[0])
    normed_out.start()

    def up_out(m):
        return pltpu.make_async_copy(up_ref.at[m], up_hbm.at[m], o_sem.at[1 + m])

    loads[4].wait()

    def project(k, total):
        cols = columns(k * step_width, step_width)
        return total + jnp.dot(normed_ref[:, cols], wq[cols, :], preferred_element_type=wide)

    product = lax.fori_loop(
        0, width // step_width, project, jnp.zeros((every, head_cols), wide)
    ).astype(low)
    for m in range(batch_groups):
        queries[m] = product[m * tokens : (m + 1) * tokens]

    for xd in range(1, inner):
        kv_near_copy(xd).wait()
    for kind in range(2):
        total = kv_near[0, kind].astype(wide)
        for xd in range(1, inner):
            total = total + kv_near[xd, kind].astype(wide)
        total = total.astype(low)
        for m in range(batch_groups):
            kv[m, kind] = total[m * tokens : (m + 1) * tokens]

    for m in range(batch_groups):
        ids = ids_ref[m : m + 1].astype(wide)
        mask = (to_column(ids, tokens, 0) == jnp.broadcast_to(ids, (tokens, tokens))) & (
            iota((tokens, tokens), 0) >= iota((tokens, tokens), 1)
        )
        for h in range(local_heads):
            head = slice(h * HEAD_WIDTH, (h + 1) * HEAD_WIDTH)
            scores = contract(queries[m, :, head], kv[m, 0], 1, 1) * scale
            value = jnp.exp(jnp.where(mask, scores, masked_score))
            value = value / jnp.sum(value, -1, keepdims=True)
            probs[m, h] = value
            att_ref[m * tokens : (m + 1) * tokens, head] = jnp.dot(
                value.astype(low), kv[m, 1], preferred_element_type=wide
            ).astype(low)
    loads[5].wait()
    gain_out_ref[...] = jnp.zeros_like(gain_out_ref)

    def dkv_near_copy(m, xd):
        return near(
            dkv_near.at[m, 0], dkv_near.at[m, xd], dn_send.at[m, xd], dn_recv.at[m, xd], xd
        )

    def dkv_far_copy(m, zd):
        block = dkv_far.at[m, z]
        return far(block, block, df_send.at[m, zd], df_recv.at[m, zd], zd)

    def group(i):
        return columns(lax.rem(z + i, outer) * group_width, group_width)

    def part_near(m, i, xd):
        return near(
            part.at[m, xpeer(xd), :, :, group(i)],
            near_recv.at[m, xd - 1, :, :, group(i)],
            pn_send.at[m, xd, i - 1],
            pn_recv.at[m, xd, i - 1],
            xd,
        )

    def part_far(m, i, c, zd):
        cols = columns(c * group_width, group_width)
        return far(
            far_send.at[m, zd, :, cols],
            far_recv.at[m, zd, :, cols],
            pf_send.at[m, zd, i - 1],
            pf_recv.at[m, zd, i - 1],
            zd,
        )

    def key_copy(m, d):
        peer = lax.rem(me + d, tp_count)
        return remote(
            key_send.at[m, peer], key_recv.at[m, me], ks_send.at[m, d], ks_recv.at[m, d], sec, peer
        )

    def part_group(m, i):
        base = lax.rem(z + i, outer) * group_width

        def piece(k, carry):
            start = base + k * step_width
            cols = columns(start, step_width)
            product = contract(gq_ref[m], wq[cols, :], 1, 1)
            for block in range(tp_count):
                part[m, block % inner, block // inner, :, cols] = product[
                    block * rows : (block + 1) * rows
                ].astype(low)
            return carry

        lax.fori_loop(0, group_width // step_width, piece, 0)
        for xd in range(1, inner):
            part_near(m, i, xd).start()

    def sum_group(m, i):
        cols = group(i)
        for xd in range(1, inner):
            part_near(m, i, xd).wait()
        for zd in range(outer):
            total = part[m, x, zpeer(zd), :, cols].astype(wide)
            for xd in range(1, inner):
                total = total + near_recv[m, xd - 1, zpeer(zd), :, cols].astype(wide)
            if zd:
                far_send[m, zd, :, cols] = total.astype(low)
                part_far(m, i, lax.rem(z + i, outer), zd).start()
            else:
                far_recv[m, 0, :, cols] = total.astype(low)

    def forward(m, c):
        @pl.when(jnp.logical_not(is_last))
        def _():
            for zd in range(outer):
                hop(m, c, zd, sec).wait_recv()
                for xd in range(1, inner):
                    grad_near(m, c, zd, xd).start()

    def begin(m):
        def upstream(c, total):
            if m == 0:
                pl.when(c + 1 < CHUNKS)(functools.partial(forward, m, c + 1))

            @pl.when(is_last)
            def _():
                top_move(m, c, sec).wait_recv()

            @pl.when(jnp.logical_not(is_last))
            def _():
                for zd in range(outer):
                    for xd in range(1, inner):
                        grad_near(m, c, zd, xd).wait()

            for k in range(chunk_width // step_width):
                cols = columns(c * chunk_width + k * step_width, step_width)
                piece = jnp.concatenate(
                    [gall[m, j, :, cols].astype(wide) for j in range(tp_count)], 0
                ).astype(low)
                up_ref[m, :, cols] = piece
                total = total + contract(piece, wo[:, cols], 1, 1)
            return total

        grad_heads[...] = lax.fori_loop(
            0, CHUNKS, upstream, jnp.zeros((tokens, head_cols), wide)
        ).astype(low)
        up_out(m).start()
        grad_keys = jnp.zeros((tokens, HEAD_WIDTH), wide)
        grad_values = jnp.zeros((tokens, HEAD_WIDTH), wide)
        for h in range(local_heads):
            head = slice(h * HEAD_WIDTH, (h + 1) * HEAD_WIDTH)
            grad_head = grad_heads[:, head]
            prob = probs[m, h]
            grad_probs = contract(grad_head, kv[m, 1], 1, 1)
            grad_scores = prob * (grad_probs - jnp.sum(prob * grad_probs, -1, keepdims=True))
            scores_low = (grad_scores * scale).astype(low)
            gq_ref[m, :, head] = jnp.dot(
                scores_low, kv[m, 0], preferred_element_type=wide
            ).astype(low)
            grad_keys = grad_keys + contract(scores_low, queries[m, :, head], 0, 0)
            grad_values = grad_values + contract(prob.astype(low), grad_head, 0, 0)
        dkv_near[m, 0, 0] = grad_keys.astype(low)
        dkv_near[m, 0, 1] = grad_values.astype(low)
        for xd in range(1, inner):
            dkv_near_copy(m, xd).start()

    def spread(m):
        part_group(m, 1)

        for xd in range(1, inner):
            dkv_near_copy(m, xd).wait()
        for kind in range(2):
            total = dkv_near[m, 0, kind].astype(wide)
            for xd in range(1, inner):
                total = total + dkv_near[m, xd, kind].astype(wide)
            dkv_far[m, z, kind] = total.astype(low)
        for zd in range(1, outer):
            dkv_far_copy(m, zd).start()

        def middle(i, inner_carry):
            part_group(m, i)
            sum_group(m, i - 1)
            return inner_carry

        lax.fori_loop(2, outer + 1, middle, 0)

        for zd in range(1, outer):
            dkv_far_copy(m, zd).wait()
        holders = outer // key_count
        for kind in range(2):
            for k in range(key_count):
                total = dkv_far[m, k * holders, kind].astype(wide)
                for other in range(1, holders):
                    total = total + dkv_far[m, k * holders + other, kind].astype(wide)
                dkv_ref[kind, m, :, k * HEAD_WIDTH : (k + 1) * HEAD_WIDTH] = total.astype(low)
        key_slice = contract(dkv_ref[0, m], kw[...], 1, 1) + contract(
            dkv_ref[1, m], vw[...], 1, 1
        )
        for j in range(tp_count):
            key_send[m, j] = key_slice[j * rows : (j + 1) * rows].astype(low)
        for d in range(1, tp_count):
            key_copy(m, d).start()
        key_recv[m, me] = key_send[m, me]
        sum_group(m, outer)

    def gain_copy(d):
        return remote(
            gain_all.at[me],
            gain_all.at[me],
            t_send.at[d],
            t_recv.at[d],
            sec,
            lax.rem(me + d, tp_count),
        )

    def finish(m):
        for zd in range(1, outer):
            for i in range(1, outer + 1):
                part_far(m, i, lax.rem(z + i, outer), zd).wait_send()
                part_far(m, i, lax.rem(z - zd + i + outer, outer), zd).wait_recv()

        for d in range(1, tp_count):
            key_copy(m, d).wait()

        products = jnp.zeros((rows, slice_width), wide)
        for k in range(tp_count):
            cols = slice(k * slice_width, (k + 1) * slice_width)
            normed_grad = key_recv[m, k].astype(wide) + jnp.sum(
                far_recv[m, :, :, cols].astype(wide), 0
            )
            unit_part = unit[m, :, cols]
            gain_out_ref[:, cols] = gain_out_ref[:, cols] + jnp.sum(
                normed_grad * unit_part, 0, keepdims=True
            )
            scaled = normed_grad * gain_ref[:, cols].astype(wide)
            grad_unit[:, cols] = scaled
            products = products + scaled * unit_part
        if m + 1 == batch_groups:
            gain_all[me] = gain_out_ref[...].astype(low)
            for d in range(1, tp_count):
                gain_copy(d).start()
        dots = jnp.sum(products, -1, keepdims=True) / width
        inv = inverse[m, :, 0:1]
        for c in range(CHUNKS):
            cols = slice(c * chunk_width, (c + 1) * chunk_width)
            gin_ref[m, :, cols] = (
                gall[m, me, :, cols].astype(wide)
                + inv * (grad_unit[:, cols] - unit[m, :, cols] * dots)
            ).astype(low)

            @pl.when(feeds)
            def _():
                for zd in (*range(1, outer), 0):
                    hop(m, c, zd, sec - 1).start()

    forward(0, 0)
    begin(0)
    for m in range(batch_groups):
        spread(m)
        if m + 1 < batch_groups:
            for c in range(CHUNKS):
                forward(m + 1, c)
        if m + 1 < batch_groups:
            pl.when(is_last)(functools.partial(begin, m + 1))
        finish(m)
        if m + 1 < batch_groups:
            pl.when(jnp.logical_not(is_last))(functools.partial(begin, m + 1))

    for d in range(1, tp_count):
        gain_copy(d).wait()
    total = gain_all[0].astype(wide)
    for d in range(1, tp_count):
        total = total + gain_all[d].astype(wide)
    gain_out_ref[...] = total
    normed_out.wait()
    for m in range(batch_groups):
        up_out(m).wait()

    @pl.when(helps)
    def _():
        for m in range(batch_groups):
            for c in range(CHUNKS):
                top_move(m, c, sec + 2).wait_send()

    @pl.when(feeds)
    def _():
        for m in range(batch_groups):
            for c in range(CHUNKS):
                for zd in range(outer):
                    hop(m, c, zd, sec - 1).wait_send()


def relay(saved, gain, wq, kw, vw, wo, direction, ratio, ids, slots, counts):
    tp_count = lax.axis_size("tp")
    inner = inner_size(tp_count)
    outer = tp_count // inner
    batch_groups, rows, width = saved.shape
    tokens = rows * tp_count
    every = batch_groups * tokens
    head_cols = wq.shape[1]
    key_width = kw.shape[1]
    key_count = key_width // HEAD_WIDTH
    slice_width = kw.shape[0]
    vmem = pl.BlockSpec(memory_space=pltpu.VMEM)
    hbm = pl.BlockSpec(memory_space=pltpu.HBM)
    dma = pltpu.SemaphoreType.DMA
    groups = batch_groups
    return pl.pallas_call(
        functools.partial(relay_kernel, lax.axis_size("section"), tp_count),
        out_shape=[
            jax.ShapeDtypeStruct((groups, rows, width), low),
            jax.ShapeDtypeStruct((groups, tokens, width), low),
            jax.ShapeDtypeStruct((every, width), low),
            jax.ShapeDtypeStruct((every, slice_width), low),
            jax.ShapeDtypeStruct((every, head_cols), low),
            jax.ShapeDtypeStruct((groups, tokens, head_cols), low),
            jax.ShapeDtypeStruct((2, groups, tokens, key_width), low),
            jax.ShapeDtypeStruct((1, width), wide),
        ],
        in_specs=[hbm, vmem, hbm, hbm, hbm, hbm, hbm] + [vmem] * 4,
        out_specs=[vmem, hbm, hbm] + [vmem] * 5,
        scratch_shapes=[
            pltpu.VMEM(saved.shape, low),
            pltpu.VMEM(direction.shape, low),
            pltpu.VMEM(kw.shape, low),
            pltpu.VMEM(vw.shape, low),
            pltpu.VMEM(wq.shape, low),
            pltpu.VMEM(wo.shape, low),
            pltpu.VMEM((groups, tokens, width), low),
            pltpu.VMEM((every, width), low),
            pltpu.VMEM((tp_count, groups, rows, width), low),
            pltpu.VMEM((tp_count, groups, rows, slice_width), low),
            pltpu.VMEM((groups, tp_count, rows, width), low),
            pltpu.VMEM((groups, tp_count, rows, width), low),
            pltpu.VMEM((groups, inner, outer, rows, width), low),
            pltpu.VMEM((groups, inner - 1, outer, rows, width), low),
            pltpu.VMEM((groups, outer, rows, width), low),
            pltpu.VMEM((groups, outer, rows, width), low),
            pltpu.VMEM((groups, rows, width), wide),
            pltpu.VMEM((groups, rows, LANES), wide),
            pltpu.VMEM((rows, width), wide),
            pltpu.VMEM((groups, tokens, head_cols), low),
            pltpu.VMEM((groups, 2, tokens, HEAD_WIDTH), low),
            pltpu.VMEM((key_count, 2, every, HEAD_WIDTH), low),
            pltpu.VMEM((outer, 2, every, HEAD_WIDTH), low),
            pltpu.VMEM((inner, 2, every, HEAD_WIDTH), low),
            pltpu.VMEM((groups, head_cols // HEAD_WIDTH, tokens, tokens), wide),
            pltpu.VMEM((tokens, head_cols), low),
            pltpu.VMEM((groups, tp_count, rows, slice_width), low),
            pltpu.VMEM((groups, tp_count, rows, slice_width), low),
            pltpu.VMEM((groups, inner, 2, tokens, HEAD_WIDTH), low),
            pltpu.VMEM((groups, outer, 2, tokens, HEAD_WIDTH), low),
            pltpu.VMEM((tp_count, 8, LANES), wide),
            pltpu.VMEM((tp_count, 1, width), low),
            dma((6,)),
            dma((1 + groups,)),
            dma((tp_count,)),
            dma((tp_count,)),
            dma((CHUNKS, outer)),
            dma((CHUNKS, outer)),
            dma((CHUNKS, tp_count)),
            dma((CHUNKS, tp_count)),
            dma((groups, CHUNKS, outer)),
            dma((groups, CHUNKS, outer)),
            dma((groups, CHUNKS, tp_count)),
            dma((groups, CHUNKS, tp_count)),
            dma((groups, CHUNKS)),
            dma((groups, CHUNKS)),
            dma((groups, CHUNKS, outer)),
            dma((groups, CHUNKS, tp_count)),
            dma((groups, CHUNKS, tp_count)),
            dma((groups, CHUNKS, outer)),
            dma((outer,)),
            dma((outer,)),
            dma((inner,)),
            dma((inner,)),
            dma((groups, inner)),
            dma((groups, inner)),
            dma((groups, outer)),
            dma((groups, outer)),
            dma((groups, inner, outer)),
            dma((groups, inner, outer)),
            dma((groups, outer, outer)),
            dma((groups, outer, outer)),
            dma((groups, tp_count)),
            dma((groups, tp_count)),
            dma((tp_count,)),
            dma((tp_count,)),
            dma((tp_count,)),
            dma((tp_count,)),
            pltpu.SemaphoreType.REGULAR,
        ],
        compiler_params=pltpu.CompilerParams(
            collective_id=0, has_side_effects=True, vmem_limit_bytes=VMEM_LIMIT
        ),
        name="relay",
    )(saved, gain, wq, kw, vw, wo, direction, ratio, ids, slots, counts)


def weights_kernel(
    normed_ref,
    normed_cols_ref,
    gq_ref,
    dkv_ref,
    att_ref,
    up_ref,
    grads_in,
    gain_in,
    grads_out,
    of_query,
    of_key,
    of_value,
    of_out,
    gain_out,
):
    step = pl.program_id(0)

    @pl.when(step == 0)
    def _():
        grads_out[...] = grads_in[...]
        gain_out[...] = gain_in[...]

    narrow = of_key.shape[0]
    own = normed_cols_ref[:, pl.ds(pl.multiple_of(step * narrow, narrow), narrow)]
    of_query[...] = contract(normed_ref[...], gq_ref[...], 0, 0).astype(low)
    of_out[...] = contract(att_ref[...], up_ref[...], 0, 0).astype(low)
    of_key[...] = contract(own, dkv_ref[0], 0, 0).astype(low)
    of_value[...] = contract(own, dkv_ref[1], 0, 0).astype(low)


def weight_gradients(normed, normed_cols, grad_queries, dkv, attended, upstream, grads, gain):
    every, width = normed.shape
    head_cols = grad_queries.shape[1]
    slice_width, key_width = normed_cols.shape[1], dkv.shape[2]
    steps = slice_width // HEAD_WIDTH
    part = width // steps

    def whole(shape):
        return pl.BlockSpec(shape, lambda i: (0,) * len(shape))

    def lanes(shape):
        return pl.BlockSpec(shape, lambda i: (0, i))

    def above(shape):
        return pl.BlockSpec(shape, lambda i: (i, 0))

    return pl.pallas_call(
        weights_kernel,
        grid=(steps,),
        out_shape=[
            jax.ShapeDtypeStruct(grads.shape, low),
            jax.ShapeDtypeStruct((width, head_cols), low),
            jax.ShapeDtypeStruct((slice_width, key_width), low),
            jax.ShapeDtypeStruct((slice_width, key_width), low),
            jax.ShapeDtypeStruct((head_cols, width), low),
            jax.ShapeDtypeStruct(gain.shape, wide),
        ],
        in_specs=[
            lanes((every, part)),
            whole(normed_cols.shape),
            whole(grad_queries.shape),
            whole(dkv.shape),
            whole(attended.shape),
            lanes((every, part)),
            whole(grads.shape),
            whole(gain.shape),
        ],
        out_specs=[
            whole(grads.shape),
            above((part, head_cols)),
            above((HEAD_WIDTH, key_width)),
            above((HEAD_WIDTH, key_width)),
            lanes((head_cols, part)),
            whole(gain.shape),
        ],
        compiler_params=pltpu.CompilerParams(vmem_limit_bytes=VMEM_LIMIT),
        name="weight_gradients",
    )(normed, normed_cols, grad_queries, dkv, attended, upstream, grads, gain)


def body(
    section_inputs,
    norm_gain,
    w_query,
    key_projection,
    value_projection,
    w_out,
    token_dir,
    tok_logratio,
    segment_ids,
    pair_of_slot,
    pair_counts,
):
    saved = section_inputs[0]
    width = saved.shape[2]
    every = segment_ids.size
    grads, upstream, normed, normed_cols, attended, grad_queries, dkv, gain_total = relay(
        saved,
        norm_gain[0].reshape(1, width),
        w_query[0],
        key_projection[0],
        value_projection[0],
        w_out[0],
        token_dir,
        tok_logratio,
        segment_ids,
        pair_of_slot,
        pair_counts.T,
    )
    grads, of_query, of_key, of_value, of_out, gain_total = weight_gradients(
        normed,
        normed_cols,
        grad_queries.reshape(every, -1),
        dkv.reshape(2, every, -1),
        attended,
        upstream.reshape(every, width),
        grads,
        gain_total,
    )
    return (
        grads[None],
        of_query[None],
        of_key[None],
        of_value[None],
        of_out[None],
        gain_total,
    )


def solution(mesh):
    placed = (
        P("section", None, "tp", None),
        P("section", None),
        P("section", None, "tp"),
        P("section", "tp", None),
        P("section", "tp", None),
        P("section", "tp", None),
        P(None, "tp", None),
        P(None, "tp"),
        P(),
        P(),
        P(),
    )
    return jax.shard_map(
        body,
        mesh=mesh,
        in_specs=placed,
        out_specs=(
            P("section", None, "tp", None),
            P("section", None, "tp"),
            P("section", "tp", None),
            P("section", "tp", None),
            P("section", "tp", None),
            P("section", None),
        ),
        check_vma=False,
    )
```

```python
import functools
import math

import jax
import jax.numpy as jnp
from jax import lax
from jax.experimental import pallas as pl
from jax.experimental.pallas import tpu as pltpu
from jax.sharding import PartitionSpec as P

HEAD_WIDTH = 128
SLOTS = 4
LANES = 128
CHUNKS = 4

norm_epsilon = 1e-05
pair_beta = 4.0
masked_score = -1e30

MESH = pl.DeviceIdType.MESH
VMEM_LIMIT = 56 * 1024 * 1024
low, wide = jnp.bfloat16, jnp.float32


def contract(left, right, left_dim, right_dim):
    return lax.dot_general(
        left, right, (((left_dim,), (right_dim,)), ((), ())), preferred_element_type=wide
    )


def inner_size(tp_count):
    inner = 1
    while 2 * (2 * inner) ** 2 <= tp_count:
        inner *= 2
    return inner


def relay_kernel(
    section_count,
    tp_count,
    saved_hbm,
    gain_ref,
    wq_hbm,
    kw_hbm,
    vw_hbm,
    wo_hbm,
    dir_hbm,
    ratio_ref,
    ids_ref,
    slot_ref,
    counts_ref,
    gin_ref,
    up_hbm,
    normed_hbm,
    normed_cols_ref,
    att_ref,
    gq_ref,
    dkv_ref,
    gain_out_ref,
    saved_ref,
    dir_ref,
    kw,
    vw,
    wq,
    wo,
    up_ref,
    normed_ref,
    nall,
    slices,
    top,
    gall,
    part,
    near_recv,
    far_send,
    far_recv,
    unit,
    inverse,
    grad_unit,
    queries,
    kv,
    kv_part,
    kv_far,
    kv_near,
    probs,
    grad_heads,
    key_send,
    key_recv,
    dkv_near,
    dkv_far,
    sums_all,
    gain_all,
    w_sem,
    o_sem,
    s_send,
    s_recv,
    nf_send,
    nf_recv,
    nn_send,
    nn_recv,
    tf_send,
    tf_recv,
    tn_send,
    tn_recv,
    ty_send,
    ty_recv,
    gf_recv,
    gn_send,
    gn_recv,
    hop_send,
    kf_send,
    kf_recv,
    kn_send,
    kn_recv,
    dn_send,
    dn_recv,
    df_send,
    df_recv,
    pn_send,
    pn_recv,
    pf_send,
    pf_recv,
    ks_send,
    ks_recv,
    t_send,
    t_recv,
    sl_send,
    sl_recv,
    go,
):
    sec = lax.axis_index("section")
    me = lax.axis_index("tp")
    inner = inner_size(tp_count)
    outer = tp_count // inner
    z, x = me // inner, lax.rem(me, inner)
    batch_groups, rows, width = saved_ref.shape
    tokens = rows * tp_count
    every = batch_groups * tokens
    head_cols = wq.shape[1]
    local_heads = head_cols // HEAD_WIDTH
    slice_width, key_width = kw.shape
    key_count = key_width // HEAD_WIDTH
    sharers = tp_count // key_count
    group_width = inner * slice_width
    step_width = min(2048, group_width)
    merge_width = min(1024, width)
    chunk_width = width // CHUNKS
    per_group = CHUNKS // batch_groups
    normed_width = width // per_group
    scale = 1.0 / math.sqrt(HEAD_WIDTH)
    is_last = sec == section_count - 1
    feeds = sec > 0
    helps = sec == section_count - 3

    def zpeer(zd):
        return lax.rem(z + zd, outer)

    def xpeer(xd):
        return lax.rem(x + xd, inner)

    def remote(source, target, send, receive, section, index):
        return pltpu.make_async_remote_copy(
            src_ref=source,
            dst_ref=target,
            send_sem=send,
            recv_sem=receive,
            device_id=(section, index),
            device_id_type=MESH,
        )

    def far(source, target, send, receive, zd):
        return remote(source, target, send, receive, sec, zpeer(zd) * inner + x)

    def near(source, target, send, receive, xd):
        return remote(source, target, send, receive, sec, z * inner + xpeer(xd))

    def columns(start, size):
        return pl.ds(pl.multiple_of(start, HEAD_WIDTH), size)

    loads = [
        pltpu.make_async_copy(source, target, w_sem.at[i])
        for i, (source, target) in enumerate(
            (
                (saved_hbm, saved_ref),
                (dir_hbm, dir_ref),
                (kw_hbm, kw),
                (vw_hbm, vw),
                (wq_hbm, wq),
                (wo_hbm, wo),
            )
        )
    ]
    for load in loads:
        load.start()

    barrier = pltpu.get_barrier_semaphore()
    for d in range(1, tp_count):
        pl.semaphore_signal(
            barrier, inc=1, device_id=(sec, lax.rem(me + d, tp_count)), device_id_type=MESH
        )

    @pl.when(sec < section_count - 1)
    def _():
        for zd in range(outer):
            pl.semaphore_signal(
                barrier, inc=1, device_id=(sec + 1, zpeer(zd) * inner + x), device_id_type=MESH
            )

    @pl.when(is_last)
    def _():
        pl.semaphore_signal(barrier, inc=1, device_id=(sec - 2, me), device_id_type=MESH)

    loads[0].wait()
    gain_row = gain_ref[...].astype(wide)
    for m in range(batch_groups):
        rows_in = saved_ref[m].astype(wide)
        inv = lax.rsqrt(jnp.mean(rows_in * rows_in, -1, keepdims=True) + norm_epsilon)
        inverse[m] = jnp.broadcast_to(inv, (rows, LANES))
        unit_rows = rows_in * inv
        unit[m] = unit_rows
        nall[me, m] = (unit_rows * gain_row).astype(low)

    @pl.when(helps)
    def _():
        pl.semaphore_wait(barrier, tp_count + outer)

    @pl.when(feeds & jnp.logical_not(helps))
    def _():
        pl.semaphore_wait(barrier, tp_count - 1 + outer)

    @pl.when(jnp.logical_not(feeds))
    def _():
        pl.semaphore_wait(barrier, tp_count - 1)

    def iota(shape, dim):
        return lax.broadcasted_iota(jnp.int32, shape, dim)

    def to_column(row, count, start):
        span = row.shape[1]
        pick = iota((count, span), 1) == iota((count, span), 0) + start
        return jnp.sum(jnp.where(pick, jnp.broadcast_to(row, (count, span)), 0.0), -1, keepdims=True)

    def own_member(m, kind):
        own = to_column(ids_ref[m : m + 1].astype(wide), rows, me * rows)
        slot = 2 * iota((rows, SLOTS), 1) + kind
        return (own == slot.astype(wide)).astype(wide)

    def slot_counts(m, kind):
        pairs = counts_ref.shape[1]
        table = iota((pairs, SLOTS), 0) == jnp.broadcast_to(slot_ref[m : m + 1], (pairs, SLOTS))
        count = to_column(counts_ref[kind : kind + 1].astype(wide), pairs, 0)
        return jnp.sum(jnp.where(table, count, 0.0), 0, keepdims=True)

    def sums_copy(d):
        return remote(
            sums_all.at[me], sums_all.at[me], s_send.at[d], s_recv.at[d], sec, lax.rem(me + d, tp_count)
        )

    def block_from(zd):
        return lax.rem(z - zd + outer, outer) * inner + x

    def normed_piece(block, c):
        start = c % per_group * normed_width
        return nall.at[block, c // per_group, :, start : start + normed_width]

    def normed_far(c, zd):
        block = normed_piece(me, c)
        return far(block, block, nf_send.at[c, zd], nf_recv.at[c, zd], zd)

    def normed_near(c, zd, xd):
        block = normed_piece(block_from(zd), c)
        slot = zd * inner + xd
        return near(block, block, nn_send.at[c, slot], nn_recv.at[c, slot], xd)

    def chunk(c):
        return columns(c * chunk_width, chunk_width)

    def top_far(m, c, zd):
        block = top.at[m, me, :, chunk(c)]
        return far(block, block, tf_send.at[m, c, zd], tf_recv.at[m, c, zd], zd)

    def top_near(m, c, zd, xd):
        block = top.at[m, block_from(zd), :, chunk(c)]
        slot = zd * inner + xd
        return near(block, block, tn_send.at[m, c, slot], tn_recv.at[m, c, slot], xd)

    def top_move(m, c, section):
        return remote(
            top.at[m, :, :, chunk(c)],
            gall.at[m, :, :, chunk(c)],
            ty_send.at[m, c],
            ty_recv.at[m, c],
            section,
            me,
        )

    def hop(m, c, zd, section):
        return remote(
            gin_ref.at[m, :, chunk(c)],
            gall.at[m, me, :, chunk(c)],
            hop_send.at[m, c, zd],
            gf_recv.at[m, c, zd],
            section,
            zpeer(zd) * inner + x,
        )

    def grad_near(m, c, zd, xd):
        block = gall.at[m, block_from(zd), :, chunk(c)]
        slot = zd * inner + xd
        return near(block, block, gn_send.at[m, c, slot], gn_recv.at[m, c, slot], xd)

    loads[1].wait()

    @pl.when(helps)
    def _():
        sums_all[me] = jnp.zeros(sums_all.shape[1:], wide)
        for m in range(batch_groups):
            ratio = to_column(ratio_ref[m : m + 1], rows, 0)
            for kind in range(2):
                sums_all[me, 2 * m + kind : 2 * m + kind + 1, 0:SLOTS] = jnp.sum(
                    own_member(m, kind) * ratio, 0, keepdims=True
                )
        for d in range(1, tp_count):
            sums_copy(d).start()

    @pl.when(helps)
    def _():
        for d in range(1, tp_count):
            sums_copy(d).wait()
        total = sums_all[0]
        for d in range(1, tp_count):
            total = total + sums_all[d]
        for m in range(batch_groups):
            chosen, rejected = slot_counts(m, 0), slot_counts(m, 1)
            margin = pair_beta * (
                total[2 * m : 2 * m + 1, 0:SLOTS] / chosen
                - total[2 * m + 1 : 2 * m + 2, 0:SLOTS] / rejected
            )
            weight = pair_beta * jax.nn.sigmoid(-margin)
            token_weight = jnp.sum(
                own_member(m, 0) * (-weight / chosen) + own_member(m, 1) * (weight / rejected),
                -1,
                keepdims=True,
            )
            top[m, me] = (token_weight * dir_ref[m].astype(wide)).astype(low)
            for c in range(CHUNKS):
                for zd in range(1, outer):
                    top_far(m, c, zd).start()
                for xd in range(1, inner):
                    top_near(m, c, 0, xd).start()

    @pl.when(helps)
    def _():
        order = [(m, c) for m in range(batch_groups) for c in range(CHUNKS)]

        def top_forward(m, c):
            for zd in range(1, outer):
                top_far(m, c, zd).wait()
                for xd in range(1, inner):
                    top_near(m, c, zd, xd).start()

        top_forward(*order[0])
        for at, (m, c) in enumerate(order):
            if at + 1 < len(order):
                top_forward(*order[at + 1])
            for zd in range(outer):
                for xd in range(1, inner):
                    top_near(m, c, zd, xd).wait()
            top_move(m, c, sec + 2).start()

        @pl.when(feeds)
        def _():
            pl.semaphore_signal(go, inc=1, device_id=(sec - 1, me), device_id_type=MESH)

    @pl.when((sec == section_count - 2) | (sec == section_count - 4))
    def _():
        pl.semaphore_wait(go, 1)

    def slice_copy(d):
        peer = lax.rem(me + d, tp_count)
        return remote(
            nall.at[me, :, :, columns(peer * slice_width, slice_width)],
            slices.at[me],
            sl_send.at[d],
            sl_recv.at[d],
            sec,
            peer,
        )

    for d in range(1, tp_count):
        slice_copy(d).start()
    for c in range(CHUNKS):
        for zd in range(1, outer):
            normed_far(c, zd).start()
        for xd in range(1, inner):
            normed_near(c, 0, xd).start()

    for d in range(1, tp_count):
        slice_copy(d).wait()
    slices[me] = nall[me, :, :, columns(me * slice_width, slice_width)]
    for m in range(batch_groups):
        normed_cols_ref[m * tokens : (m + 1) * tokens] = jnp.concatenate(
            [slices[j, m].astype(wide) for j in range(tp_count)], 0
        ).astype(low)
    loads[2].wait()
    loads[3].wait()
    for kind, weight_ref in enumerate((kw, vw)):
        product = jnp.dot(normed_cols_ref[...], weight_ref[...], preferred_element_type=wide)
        for k in range(key_count):
            kv_part[k, kind] = product[:, k * HEAD_WIDTH : (k + 1) * HEAD_WIDTH].astype(low)

    def kv_far_copy(zd):
        head = zpeer(zd) * inner // sharers
        return far(kv_part.at[head], kv_far.at[zd], kf_send.at[zd], kf_recv.at[zd], zd)

    def kv_near_copy(xd):
        return near(kv_near.at[0], kv_near.at[xd], kn_send.at[xd], kn_recv.at[xd], xd)

    for zd in range(1, outer):
        kv_far_copy(zd).start()

    for c in range(CHUNKS):
        for zd in range(1, outer):
            normed_far(c, zd).wait()
            for xd in range(1, inner):
                normed_near(c, zd, xd).start()
    for zd in range(1, outer):
        kv_far_copy(zd).wait()
    for kind in range(2):
        total = kv_part[z * inner // sharers, kind].astype(wide)
        for zd in range(1, outer):
            total = total + kv_far[zd, kind].astype(wide)
        kv_near[0, kind] = total.astype(low)
    for xd in range(1, inner):
        kv_near_copy(xd).start()
    for c in range(CHUNKS):
        for zd in range(outer):
            for xd in range(1, inner):
                normed_near(c, zd, xd).wait()

    @pl.when(is_last)
    def _():
        pl.semaphore_signal(go, inc=1, device_id=(sec - 1, me), device_id_type=MESH)

    def merge(k, carry):
        cols = columns(k * merge_width, merge_width)
        for m in range(batch_groups):
            normed_ref[m * tokens : (m + 1) * tokens, cols] = jnp.concatenate(
                [nall[j, m, :, cols].astype(wide) for j in range(tp_count)], 0
            ).astype(low)
        return carry

    lax.fori_loop(0, width // merge_width, merge, 0)
    normed_out = pltpu.make_async_copy(normed_ref, normed_hbm, o_sem.at[0])
    normed_out.start()

    def up_out(m):
        return pltpu.make_async_copy(up_ref.at[m], up_hbm.at[m], o_sem.at[1 + m])

    loads[4].wait()

    def project(k, total):
        cols = columns(k * step_width, step_width)
        return total + jnp.dot(normed_ref[:, cols], wq[cols, :], preferred_element_type=wide)

    product = lax.fori_loop(
        0, width // step_width, project, jnp.zeros((every, head_cols), wide)
    ).astype(low)
    for m in range(batch_groups):
        queries[m] = product[m * tokens : (m + 1) * tokens]

    for xd in range(1, inner):
        kv_near_copy(xd).wait()
    for kind in range(2):
        total = kv_near[0, kind].astype(wide)
        for xd in range(1, inner):
            total = total + kv_near[xd, kind].astype(wide)
        total = total.astype(low)
        for m in range(batch_groups):
            kv[m, kind] = total[m * tokens : (m + 1) * tokens]

    for m in range(batch_groups):
        ids = ids_ref[m : m + 1].astype(wide)
        mask = (to_column(ids, tokens, 0) == jnp.broadcast_to(ids, (tokens, tokens))) & (
            iota((tokens, tokens), 0) >= iota((tokens, tokens), 1)
        )
        for h in range(local_heads):
            head = slice(h * HEAD_WIDTH, (h + 1) * HEAD_WIDTH)
            scores = contract(queries[m, :, head], kv[m, 0], 1, 1) * scale
            value = jnp.exp(jnp.where(mask, scores, masked_score))
            value = value / jnp.sum(value, -1, keepdims=True)
            probs[m, h] = value
            att_ref[m * tokens : (m + 1) * tokens, head] = jnp.dot(
                value.astype(low), kv[m, 1], preferred_element_type=wide
            ).astype(low)
    loads[5].wait()
    gain_out_ref[...] = jnp.zeros_like(gain_out_ref)

    def dkv_near_copy(m, xd):
        return near(
            dkv_near.at[m, 0], dkv_near.at[m, xd], dn_send.at[m, xd], dn_recv.at[m, xd], xd
        )

    def dkv_far_copy(m, zd):
        block = dkv_far.at[m, z]
        return far(block, block, df_send.at[m, zd], df_recv.at[m, zd], zd)

    def group(i):
        return columns(lax.rem(z + i, outer) * group_width, group_width)

    def part_near(m, i, xd):
        return near(
            part.at[m, xpeer(xd), :, :, group(i)],
            near_recv.at[m, xd - 1, :, :, group(i)],
            pn_send.at[m, xd, i - 1],
            pn_recv.at[m, xd, i - 1],
            xd,
        )

    def part_far(m, i, c, zd):
        cols = columns(c * group_width, group_width)
        return far(
            far_send.at[m, zd, :, cols],
            far_recv.at[m, zd, :, cols],
            pf_send.at[m, zd, i - 1],
            pf_recv.at[m, zd, i - 1],
            zd,
        )

    def key_copy(m, d):
        peer = lax.rem(me + d, tp_count)
        return remote(
            key_send.at[m, peer], key_recv.at[m, me], ks_send.at[m, d], ks_recv.at[m, d], sec, peer
        )

    def part_group(m, i):
        base = lax.rem(z + i, outer) * group_width

        def piece(k, carry):
            start = base + k * step_width
            cols = columns(start, step_width)
            product = contract(gq_ref[m], wq[cols, :], 1, 1)
            for block in range(tp_count):
                part[m, block % inner, block // inner, :, cols] = product[
                    block * rows : (block + 1) * rows
                ].astype(low)
            return carry

        lax.fori_loop(0, group_width // step_width, piece, 0)
        for xd in range(1, inner):
            part_near(m, i, xd).start()

    def sum_group(m, i):
        cols = group(i)
        for xd in range(1, inner):
            part_near(m, i, xd).wait()
        for zd in range(outer):
            total = part[m, x, zpeer(zd), :, cols].astype(wide)
            for xd in range(1, inner):
                total = total + near_recv[m, xd - 1, zpeer(zd), :, cols].astype(wide)
            if zd:
                far_send[m, zd, :, cols] = total.astype(low)
                part_far(m, i, lax.rem(z + i, outer), zd).start()
            else:
                far_recv[m, 0, :, cols] = total.astype(low)

    def forward(m, c):
        @pl.when(jnp.logical_not(is_last))
        def _():
            for zd in range(outer):
                hop(m, c, zd, sec).wait_recv()
                for xd in range(1, inner):
                    grad_near(m, c, zd, xd).start()

    def begin(m):
        def upstream(c, total):
            if m == 0:
                pl.when(c + 1 < CHUNKS)(functools.partial(forward, m, c + 1))

            @pl.when(is_last)
            def _():
                top_move(m, c, sec).wait_recv()

            @pl.when(jnp.logical_not(is_last))
            def _():
                for zd in range(outer):
                    for xd in range(1, inner):
                        grad_near(m, c, zd, xd).wait()

            for k in range(chunk_width // step_width):
                cols = columns(c * chunk_width + k * step_width, step_width)
                piece = jnp.concatenate(
                    [gall[m, j, :, cols].astype(wide) for j in range(tp_count)], 0
                ).astype(low)
                up_ref[m, :, cols] = piece
                total = total + contract(piece, wo[:, cols], 1, 1)
            return total

        grad_heads[...] = lax.fori_loop(
            0, CHUNKS, upstream, jnp.zeros((tokens, head_cols), wide)
        ).astype(low)
        up_out(m).start()
        grad_keys = jnp.zeros((tokens, HEAD_WIDTH), wide)
        grad_values = jnp.zeros((tokens, HEAD_WIDTH), wide)
        for h in range(local_heads):
            head = slice(h * HEAD_WIDTH, (h + 1) * HEAD_WIDTH)
            grad_head = grad_heads[:, head]
            prob = probs[m, h]
            grad_probs = contract(grad_head, kv[m, 1], 1, 1)
            grad_scores = prob * (grad_probs - jnp.sum(prob * grad_probs, -1, keepdims=True))
            scores_low = (grad_scores * scale).astype(low)
            gq_ref[m, :, head] = jnp.dot(
                scores_low, kv[m, 0], preferred_element_type=wide
            ).astype(low)
            grad_keys = grad_keys + contract(scores_low, queries[m, :, head], 0, 0)
            grad_values = grad_values + contract(prob.astype(low), grad_head, 0, 0)
        dkv_near[m, 0, 0] = grad_keys.astype(low)
        dkv_near[m, 0, 1] = grad_values.astype(low)
        for xd in range(1, inner):
            dkv_near_copy(m, xd).start()

    def spread(m):
        part_group(m, 1)

        for xd in range(1, inner):
            dkv_near_copy(m, xd).wait()
        for kind in range(2):
            total = dkv_near[m, 0, kind].astype(wide)
            for xd in range(1, inner):
                total = total + dkv_near[m, xd, kind].astype(wide)
            dkv_far[m, z, kind] = total.astype(low)
        for zd in range(1, outer):
            dkv_far_copy(m, zd).start()

        def middle(i, inner_carry):
            part_group(m, i)
            sum_group(m, i - 1)
            return inner_carry

        lax.fori_loop(2, outer + 1, middle, 0)

        for zd in range(1, outer):
            dkv_far_copy(m, zd).wait()
        holders = outer // key_count
        for kind in range(2):
            for k in range(key_count):
                total = dkv_far[m, k * holders, kind].astype(wide)
                for other in range(1, holders):
                    total = total + dkv_far[m, k * holders + other, kind].astype(wide)
                dkv_ref[kind, m, :, k * HEAD_WIDTH : (k + 1) * HEAD_WIDTH] = total.astype(low)
        key_slice = contract(dkv_ref[0, m], kw[...], 1, 1) + contract(
            dkv_ref[1, m], vw[...], 1, 1
        )
        for j in range(tp_count):
            key_send[m, j] = key_slice[j * rows : (j + 1) * rows].astype(low)
        for d in range(1, tp_count):
            key_copy(m, d).start()
        key_recv[m, me] = key_send[m, me]
        sum_group(m, outer)

    def gain_copy(d):
        return remote(
            gain_all.at[me],
            gain_all.at[me],
            t_send.at[d],
            t_recv.at[d],
            sec,
            lax.rem(me + d, tp_count),
        )

    def finish(m):
        for zd in range(1, outer):
            for i in range(1, outer + 1):
                part_far(m, i, lax.rem(z - zd + i + outer, outer), zd).wait_recv()

        for d in range(1, tp_count):
            key_copy(m, d).wait()

        products = jnp.zeros((rows, slice_width), wide)
        for k in range(tp_count):
            cols = slice(k * slice_width, (k + 1) * slice_width)
            normed_grad = key_recv[m, k].astype(wide) + jnp.sum(
                far_recv[m, :, :, cols].astype(wide), 0
            )
            unit_part = unit[m, :, cols]
            gain_out_ref[:, cols] = gain_out_ref[:, cols] + jnp.sum(
                normed_grad * unit_part, 0, keepdims=True
            )
            scaled = normed_grad * gain_ref[:, cols].astype(wide)
            grad_unit[:, cols] = scaled
            products = products + scaled * unit_part
        if m + 1 == batch_groups:
            gain_all[me] = gain_out_ref[...].astype(low)
            for d in range(1, tp_count):
                gain_copy(d).start()
        dots = jnp.sum(products, -1, keepdims=True) / width
        inv = inverse[m, :, 0:1]
        for c in range(CHUNKS):
            cols = slice(c * chunk_width, (c + 1) * chunk_width)
            gin_ref[m, :, cols] = (
                gall[m, me, :, cols].astype(wide)
                + inv * (grad_unit[:, cols] - unit[m, :, cols] * dots)
            ).astype(low)

            @pl.when(feeds)
            def _():
                for zd in (*range(1, outer), 0):
                    hop(m, c, zd, sec - 1).start()

        for zd in range(1, outer):
            for i in range(1, outer + 1):
                part_far(m, i, lax.rem(z + i, outer), zd).wait_send()

    forward(0, 0)
    begin(0)
    for m in range(batch_groups):
        spread(m)
        if m + 1 < batch_groups:
            for c in range(CHUNKS):
                forward(m + 1, c)
        if m + 1 < batch_groups:
            pl.when(is_last)(functools.partial(begin, m + 1))
        finish(m)
        if m + 1 < batch_groups:
            pl.when(jnp.logical_not(is_last))(functools.partial(begin, m + 1))

    for d in range(1, tp_count):
        gain_copy(d).wait()
    total = gain_all[0].astype(wide)
    for d in range(1, tp_count):
        total = total + gain_all[d].astype(wide)
    gain_out_ref[...] = total
    normed_out.wait()
    for m in range(batch_groups):
        up_out(m).wait()

    @pl.when(helps)
    def _():
        for m in range(batch_groups):
            for c in range(CHUNKS):
                top_move(m, c, sec + 2).wait_send()

    @pl.when(feeds)
    def _():
        for m in range(batch_groups):
            for c in range(CHUNKS):
                for zd in range(outer):
                    hop(m, c, zd, sec - 1).wait_send()


def relay(saved, gain, wq, kw, vw, wo, direction, ratio, ids, slots, counts):
    tp_count = lax.axis_size("tp")
    inner = inner_size(tp_count)
    outer = tp_count // inner
    batch_groups, rows, width = saved.shape
    tokens = rows * tp_count
    every = batch_groups * tokens
    head_cols = wq.shape[1]
    key_width = kw.shape[1]
    key_count = key_width // HEAD_WIDTH
    slice_width = kw.shape[0]
    vmem = pl.BlockSpec(memory_space=pltpu.VMEM)
    hbm = pl.BlockSpec(memory_space=pltpu.HBM)
    dma = pltpu.SemaphoreType.DMA
    groups = batch_groups
    return pl.pallas_call(
        functools.partial(relay_kernel, lax.axis_size("section"), tp_count),
        out_shape=[
            jax.ShapeDtypeStruct((groups, rows, width), low),
            jax.ShapeDtypeStruct((groups, tokens, width), low),
            jax.ShapeDtypeStruct((every, width), low),
            jax.ShapeDtypeStruct((every, slice_width), low),
            jax.ShapeDtypeStruct((every, head_cols), low),
            jax.ShapeDtypeStruct((groups, tokens, head_cols), low),
            jax.ShapeDtypeStruct((2, groups, tokens, key_width), low),
            jax.ShapeDtypeStruct((1, width), wide),
        ],
        in_specs=[hbm, vmem, hbm, hbm, hbm, hbm, hbm] + [vmem] * 4,
        out_specs=[vmem, hbm, hbm] + [vmem] * 5,
        scratch_shapes=[
            pltpu.VMEM(saved.shape, low),
            pltpu.VMEM(direction.shape, low),
            pltpu.VMEM(kw.shape, low),
            pltpu.VMEM(vw.shape, low),
            pltpu.VMEM(wq.shape, low),
            pltpu.VMEM(wo.shape, low),
            pltpu.VMEM((groups, tokens, width), low),
            pltpu.VMEM((every, width), low),
            pltpu.VMEM((tp_count, groups, rows, width), low),
            pltpu.VMEM((tp_count, groups, rows, slice_width), low),
            pltpu.VMEM((groups, tp_count, rows, width), low),
            pltpu.VMEM((groups, tp_count, rows, width), low),
            pltpu.VMEM((groups, inner, outer, rows, width), low),
            pltpu.VMEM((groups, inner - 1, outer, rows, width), low),
            pltpu.VMEM((groups, outer, rows, width), low),
            pltpu.VMEM((groups, outer, rows, width), low),
            pltpu.VMEM((groups, rows, width), wide),
            pltpu.VMEM((groups, rows, LANES), wide),
            pltpu.VMEM((rows, width), wide),
            pltpu.VMEM((groups, tokens, head_cols), low),
            pltpu.VMEM((groups, 2, tokens, HEAD_WIDTH), low),
            pltpu.VMEM((key_count, 2, every, HEAD_WIDTH), low),
            pltpu.VMEM((outer, 2, every, HEAD_WIDTH), low),
            pltpu.VMEM((inner, 2, every, HEAD_WIDTH), low),
            pltpu.VMEM((groups, head_cols // HEAD_WIDTH, tokens, tokens), wide),
            pltpu.VMEM((tokens, head_cols), low),
            pltpu.VMEM((groups, tp_count, rows, slice_width), low),
            pltpu.VMEM((groups, tp_count, rows, slice_width), low),
            pltpu.VMEM((groups, inner, 2, tokens, HEAD_WIDTH), low),
            pltpu.VMEM((groups, outer, 2, tokens, HEAD_WIDTH), low),
            pltpu.VMEM((tp_count, 8, LANES), wide),
            pltpu.VMEM((tp_count, 1, width), low),
            dma((6,)),
            dma((1 + groups,)),
            dma((tp_count,)),
            dma((tp_count,)),
            dma((CHUNKS, outer)),
            dma((CHUNKS, outer)),
            dma((CHUNKS, tp_count)),
            dma((CHUNKS, tp_count)),
            dma((groups, CHUNKS, outer)),
            dma((groups, CHUNKS, outer)),
            dma((groups, CHUNKS, tp_count)),
            dma((groups, CHUNKS, tp_count)),
            dma((groups, CHUNKS)),
            dma((groups, CHUNKS)),
            dma((groups, CHUNKS, outer)),
            dma((groups, CHUNKS, tp_count)),
            dma((groups, CHUNKS, tp_count)),
            dma((groups, CHUNKS, outer)),
            dma((outer,)),
            dma((outer,)),
            dma((inner,)),
            dma((inner,)),
            dma((groups, inner)),
            dma((groups, inner)),
            dma((groups, outer)),
            dma((groups, outer)),
            dma((groups, inner, outer)),
            dma((groups, inner, outer)),
            dma((groups, outer, outer)),
            dma((groups, outer, outer)),
            dma((groups, tp_count)),
            dma((groups, tp_count)),
            dma((tp_count,)),
            dma((tp_count,)),
            dma((tp_count,)),
            dma((tp_count,)),
            pltpu.SemaphoreType.REGULAR,
        ],
        compiler_params=pltpu.CompilerParams(
            collective_id=0, has_side_effects=True, vmem_limit_bytes=VMEM_LIMIT
        ),
        name="relay",
    )(saved, gain, wq, kw, vw, wo, direction, ratio, ids, slots, counts)


def weights_kernel(
    normed_ref,
    normed_cols_ref,
    gq_ref,
    dkv_ref,
    att_ref,
    up_ref,
    grads_in,
    gain_in,
    grads_out,
    of_query,
    of_key,
    of_value,
    of_out,
    gain_out,
):
    step = pl.program_id(0)

    @pl.when(step == 0)
    def _():
        grads_out[...] = grads_in[...]
        gain_out[...] = gain_in[...]

    narrow = of_key.shape[0]
    own = normed_cols_ref[:, pl.ds(pl.multiple_of(step * narrow, narrow), narrow)]
    of_query[...] = contract(normed_ref[...], gq_ref[...], 0, 0).astype(low)
    of_out[...] = contract(att_ref[...], up_ref[...], 0, 0).astype(low)
    of_key[...] = contract(own, dkv_ref[0], 0, 0).astype(low)
    of_value[...] = contract(own, dkv_ref[1], 0, 0).astype(low)


def weight_gradients(normed, normed_cols, grad_queries, dkv, attended, upstream, grads, gain):
    every, width = normed.shape
    head_cols = grad_queries.shape[1]
    slice_width, key_width = normed_cols.shape[1], dkv.shape[2]
    steps = slice_width // HEAD_WIDTH
    part = width // steps

    def whole(shape):
        return pl.BlockSpec(shape, lambda i: (0,) * len(shape))

    def lanes(shape):
        return pl.BlockSpec(shape, lambda i: (0, i))

    def above(shape):
        return pl.BlockSpec(shape, lambda i: (i, 0))

    return pl.pallas_call(
        weights_kernel,
        grid=(steps,),
        out_shape=[
            jax.ShapeDtypeStruct(grads.shape, low),
            jax.ShapeDtypeStruct((width, head_cols), low),
            jax.ShapeDtypeStruct((slice_width, key_width), low),
            jax.ShapeDtypeStruct((slice_width, key_width), low),
            jax.ShapeDtypeStruct((head_cols, width), low),
            jax.ShapeDtypeStruct(gain.shape, wide),
        ],
        in_specs=[
            lanes((every, part)),
            whole(normed_cols.shape),
            whole(grad_queries.shape),
            whole(dkv.shape),
            whole(attended.shape),
            lanes((every, part)),
            whole(grads.shape),
            whole(gain.shape),
        ],
        out_specs=[
            whole(grads.shape),
            above((part, head_cols)),
            above((HEAD_WIDTH, key_width)),
            above((HEAD_WIDTH, key_width)),
            lanes((head_cols, part)),
            whole(gain.shape),
        ],
        compiler_params=pltpu.CompilerParams(vmem_limit_bytes=VMEM_LIMIT),
        name="weight_gradients",
    )(normed, normed_cols, grad_queries, dkv, attended, upstream, grads, gain)


def body(
    section_inputs,
    norm_gain,
    w_query,
    key_projection,
    value_projection,
    w_out,
    token_dir,
    tok_logratio,
    segment_ids,
    pair_of_slot,
    pair_counts,
):
    saved = section_inputs[0]
    width = saved.shape[2]
    every = segment_ids.size
    grads, upstream, normed, normed_cols, attended, grad_queries, dkv, gain_total = relay(
        saved,
        norm_gain[0].reshape(1, width),
        w_query[0],
        key_projection[0],
        value_projection[0],
        w_out[0],
        token_dir,
        tok_logratio,
        segment_ids,
        pair_of_slot,
        pair_counts.T,
    )
    grads, of_query, of_key, of_value, of_out, gain_total = weight_gradients(
        normed,
        normed_cols,
        grad_queries.reshape(every, -1),
        dkv.reshape(2, every, -1),
        attended,
        upstream.reshape(every, width),
        grads,
        gain_total,
    )
    return (
        grads[None],
        of_query[None],
        of_key[None],
        of_value[None],
        of_out[None],
        gain_total,
    )


def solution(mesh):
    placed = (
        P("section", None, "tp", None),
        P("section", None),
        P("section", None, "tp"),
        P("section", "tp", None),
        P("section", "tp", None),
        P("section", "tp", None),
        P(None, "tp", None),
        P(None, "tp"),
        P(),
        P(),
        P(),
    )
    return jax.shard_map(
        body,
        mesh=mesh,
        in_specs=placed,
        out_specs=(
            P("section", None, "tp", None),
            P("section", None, "tp"),
            P("section", "tp", None),
            P("section", "tp", None),
            P("section", "tp", None),
            P("section", None),
        ),
        check_vma=False,
    )
```
